32 devices in a mesh: dp: 8 (over z, x), ctx: 4 (over y, core).
Axes of the slice: x: 2, y: 2, z: 4, core: 2. Of those that a mesh axis runs over, the one named last changes fastest.
Arguments:
- tokens: bfloat16 [16, 1024, 960], P('dp', 'ctx'), may hold values from -6 to 6
- segment_ids: int32 [16, 1024], P('dp', 'ctx'), may hold values from 0 to 5, as said below
- positions: int32 [16, 1024], P('dp', 'ctx'), may hold values from 0 to 2047, as said below
- norm_attn: float32 [960], replicated, may hold values from 0.25 to 1.75
- w_query: bfloat16 [921600], P(('dp', 'ctx')), may hold values from -0.1875 to 0.1875
- w_key: bfloat16 [307200], P(('dp', 'ctx')), may hold values from -0.1875 to 0.1875
- w_value: bfloat16 [307200], P(('dp', 'ctx')), may hold values from -0.1875 to 0.1875
- w_out: bfloat16 [921600], P(('dp', 'ctx')), may hold values from -0.75 to 0.75
- norm_ffn: float32 [960], replicated, may hold values from 0.25 to 1.75
- w_gate: bfloat16 [2457600], P(('dp', 'ctx')), may hold values from -0.1875 to 0.1875
- w_up: bfloat16 [2457600], P(('dp', 'ctx')), may hold values from -0.1875 to 0.1875
- w_down: bfloat16 [2457600], P(('dp', 'ctx')), may hold values from -0.125 to 0.125
- cotangent: bfloat16 [16, 1024, 960], P('dp', 'ctx'), may hold values from -6 to 6
Outputs:
- output: bfloat16 [16, 1024, 960], P('dp', 'ctx')
- d_tokens: float32 [16, 1024, 960], P('dp', 'ctx')
- d_norm_attn: float32 [960], replicated
- d_w_query: float32 [921600], P(('dp', 'ctx'))
- d_w_key: float32 [307200], P(('dp', 'ctx'))
- d_w_value: float32 [307200], P(('dp', 'ctx'))
- d_w_out: float32 [921600], P(('dp', 'ctx'))
- d_norm_ffn: float32 [960], replicated
- d_w_gate: float32 [2457600], P(('dp', 'ctx'))
- d_w_up: float32 [2457600], P(('dp', 'ctx'))
- d_w_down: float32 [2457600], P(('dp', 'ctx'))
The draws below stay inside these ranges and needn't reach their ends.
Inputs may be any that keep to these rules, and one draw needn't show every extreme that they name: `segment_ids`: within each sequence the ids start at 0 and never fall. A run of one id is one document: a sequence's first run may be the rest of a longer document and has 102 positions or more, every later run is a document of 204 to 2047 positions, cut at the sequence's end. Within each run of one segment id the positions rise by one from token to token; every run but a sequence's first starts at 0, a sequence's first run starts at most at 1024.
All inputs are finite; a program needn't handle non-finite values.
Results may differ from the reference program's by a relative error of at most 0.02.
Values may be sent and summed in bfloat16 or wider, within the bound.
No kernel may reach another device: no remote copies, remote signals or barrier semaphores. Data moves between devices by JAX's collectives and lax.ppermute only.
A program may use at most 448 MiB of HBM per device.

```python
import math
import jax
import jax.numpy as jnp
from jax import lax

D = 960
HEADS = 15
KV_HEADS = 5
HEAD_DIM = 64
FF = 2560
LEN = 1024
SEQS = 16


def layout(key):
    base = jax.random.fold_in(key, 11)
    first_key, offset_key, rest_key = jax.random.split(base, 3)
    first = jax.random.randint(first_key, (SEQS,), LEN // 10, LEN + 1)
    first = first.at[0].set(LEN).at[SEQS - 1].set(LEN // 10)
    offset = jax.random.randint(offset_key, (SEQS,), 0, LEN + 1)
    offset = offset.at[0].set(LEN)
    others = jax.random.randint(rest_key, (SEQS, 7), LEN // 5, 2 * LEN)
    others = others.at[SEQS - 1].set(LEN // 5)
    bounds = jnp.cumsum(jnp.concatenate([first[:, None], others], axis=1), axis=1)
    index = jnp.arange(LEN, dtype=jnp.int32)
    segment = jnp.sum((index[None, :, None] >= bounds[:, None, :]).astype(jnp.int32), axis=-1)
    starts = jnp.concatenate([jnp.zeros((SEQS, 1), jnp.int32), bounds[:, :7]], axis=1)
    begin = jnp.take_along_axis(starts, segment, axis=1)
    position = index[None, :] - begin + jnp.where(segment == 0, offset[:, None], 0)
    return (segment.astype(jnp.int32), position.astype(jnp.int32))


def draw_segment_ids(key, part):
    return layout(key)[0]


def draw_positions(key, part):
    return layout(key)[1]


def block_levels(key, shape, shards, smallest, largest):
    factor_of = 1.0
    for dim, shards_of in shards:
        draws = jax.random.uniform(jax.random.fold_in(jax.random.fold_in(key, 6), dim), (shards_of,), jnp.float32, smallest / len(shards), largest / len(shards))
        factor_of = factor_of * jnp.repeat(jnp.exp(draws), shape[dim] // shards_of).reshape((-1,) + (1,) * (len(shape) - 1 - dim))
    return factor_of


def noise(stream_key, shape, scale, bound, cuts=(), held_as=jnp.bfloat16):
    level = block_levels(stream_key, shape, cuts, -0.22, 0.18) if cuts else 1.0
    entries = jax.random.normal(stream_key, shape, jnp.float32) * scale * level
    return jnp.minimum(jnp.maximum(entries, -bound), bound).astype(held_as)


def setup_inputs(seed: int = 0) -> dict:
    splits = jax.random.split(jax.random.key(seed), 14)
    tokens = noise(splits[0], (SEQS, LEN, D), 1.0, 6.0, ((0, 8), (1, 4)))
    segment_ids = draw_segment_ids(jax.random.fold_in(splits[13], 71), 0)
    positions = draw_positions(jax.random.fold_in(splits[13], 71), 0)
    norm_attn = jnp.clip(1.0 + 0.15 * jax.random.normal(splits[3], (D,), jnp.float32), 0.25, 1.75)
    w_query = noise(splits[4], (D * HEADS * HEAD_DIM,), D ** -0.5, 0.1875, ((0, 32),))
    w_key = noise(splits[5], (D * KV_HEADS * HEAD_DIM,), D ** -0.5, 0.1875, ((0, 32),))
    w_value = noise(splits[6], (D * KV_HEADS * HEAD_DIM,), D ** -0.5, 0.1875, ((0, 32),))
    w_out = noise(splits[7], (HEADS * HEAD_DIM * D,), (HEADS * HEAD_DIM // 16) ** -0.5, 0.75, ((0, 32),))
    norm_ffn = jnp.clip(1.0 + 0.15 * jax.random.normal(splits[8], (D,), jnp.float32), 0.25, 1.75)
    w_gate = noise(splits[9], (D * FF,), D ** -0.5, 0.1875, ((0, 32),))
    w_up = noise(splits[10], (D * FF,), D ** -0.5, 0.1875, ((0, 32),))
    w_down = noise(splits[11], (FF * D,), FF ** -0.5, 0.125, ((0, 32),))
    cotangent = noise(splits[12], (SEQS, LEN, D), 1.0, 6.0, ((0, 8), (1, 4)))
    return {"tokens": tokens, "segment_ids": segment_ids, "positions": positions, "norm_attn": norm_attn, "w_query": w_query, "w_key": w_key, "w_value": w_value, "w_out": w_out, "norm_ffn": norm_ffn, "w_gate": w_gate, "w_up": w_up, "w_down": w_down, "cotangent": cotangent}


norm_eps = 1e-05
rope_base = 100000.0
mask_fill = -1000000000.0
highest = lax.Precision.HIGHEST

@jax.custom_vjp
def low(v):
    return lax.optimization_barrier(v.astype(jnp.bfloat16)).astype(jnp.float32)

@jax.custom_vjp
def low_back(v):
    return v

def low_keep(v):
    return (low(v), None)

def low_pass(kept, grad):
    return (grad,)

def back_keep(v):
    return (v, None)

def back_low(kept, grad):
    return (low(grad),)
low.defvjp(low_keep, low_pass)
low_back.defvjp(back_keep, back_low)

def rope_tables(position):
    freqs = rope_base ** (-jnp.arange(0, HEAD_DIM, 2, dtype=jnp.float32) / HEAD_DIM)
    angles = position.astype(jnp.float32)[..., None] * freqs
    angles = jnp.concatenate([angles, angles], axis=-1)
    return (jnp.cos(angles)[..., None, :], jnp.sin(angles)[..., None, :])

def rotate(values, cosine, sine):
    half = values.shape[-1] // 2
    turned = jnp.concatenate([-values[..., half:], values[..., :half]], axis=-1)
    return values * cosine + turned * sine

def norm(values, gain):
    return values * lax.rsqrt(lax.optimization_barrier(jnp.mean(values * values, axis=-1, keepdims=True)) + norm_eps) * gain

def matmul(left, right):
    return jnp.dot(left, right, precision=highest)

def block_forward(params, tokens, segment, position):
    gain_attn, query_weight, key_weight, value_weight, out_weight, gain_ffn, gate_weight, up_weight, down_weight = params
    group, length, width = tokens.shape
    flat = tokens.reshape(group * length, width)
    normed = low(norm(flat, gain_attn))
    cosine, sine = rope_tables(position)
    query = low(rotate(low_back(matmul(normed, query_weight)).reshape(group, length, HEADS, HEAD_DIM), cosine, sine))
    keys = low(rotate(low_back(matmul(normed, key_weight)).reshape(group, length, KV_HEADS, HEAD_DIM), cosine, sine))
    values = low(low_back(matmul(normed, value_weight))).reshape(group, length, KV_HEADS, HEAD_DIM)
    query = query.reshape(group, length, KV_HEADS, HEADS // KV_HEADS, HEAD_DIM)
    scores = low_back(jnp.einsum('sckgd,slkd->skgcl', query, keys, precision=highest) * HEAD_DIM ** (-0.5))
    index = jnp.arange(length, dtype=jnp.int32)
    allowed = (segment[:, :, None] == segment[:, None, :]) & (index[None, None, :] <= index[None, :, None])
    masked = jnp.where(allowed[:, None, None], scores, mask_fill)
    probs = low(jax.nn.softmax(masked, axis=-1))
    attended = low(low_back(jnp.einsum('skgcl,slkd->sckgd', probs, values, precision=highest)))
    resid = flat + low_back(matmul(attended.reshape(group * length, HEADS * HEAD_DIM), out_weight))
    normed_ffn = low(norm(resid, gain_ffn))
    gate = low_back(matmul(normed_ffn, gate_weight))
    up = low_back(matmul(normed_ffn, up_weight))
    hidden = low(jax.nn.silu(gate) * up)
    return (resid + low_back(matmul(hidden, down_weight))).reshape(group, length, width)

def reference(tokens, segment_ids, positions, norm_attn, w_query, w_key, w_value, w_out, norm_ffn, w_gate, w_up, w_down, cotangent):
    seqs, length, width = tokens.shape
    group = math.gcd(seqs, max(1, 2048 // length))
    attn_width = HEADS * HEAD_DIM
    kv_width = KV_HEADS * HEAD_DIM
    params = (norm_attn.astype(jnp.float32), w_query.astype(jnp.float32).reshape(width, attn_width), w_key.astype(jnp.float32).reshape(width, kv_width), w_value.astype(jnp.float32).reshape(width, kv_width), w_out.astype(jnp.float32).reshape(attn_width, width), norm_ffn.astype(jnp.float32), w_gate.astype(jnp.float32).reshape(width, FF), w_up.astype(jnp.float32).reshape(width, FF), w_down.astype(jnp.float32).reshape(FF, width))
    segments = segment_ids.reshape(seqs // group, group, length)
    places = positions.reshape(seqs // group, group, length)
    step = jax.checkpoint(block_forward)

    def forward(inputs, weights):
        blocked = inputs.reshape(seqs // group, group, length, width)
        result = lax.map(lambda item: step(weights, item[0], item[1], item[2]), (blocked, segments, places))
        return result.reshape(seqs, length, width)
    output, pullback = jax.vjp(forward, tokens.astype(jnp.float32), params)
    grad_tokens, grads = pullback(cotangent.astype(jnp.float32))
    return (output.astype(jnp.bfloat16), grad_tokens, grads[0], grads[1].reshape(-1), grads[2].reshape(-1), grads[3].reshape(-1), grads[4].reshape(-1), grads[5], grads[6].reshape(-1), grads[7].reshape(-1), grads[8].reshape(-1))
```

```python
import jax
import jax.numpy as jnp
from jax import lax
from jax.experimental import pallas as pl
from jax.experimental.pallas import tpu as pltpu
from jax.sharding import PartitionSpec as P

D = 960
HEADS = 15
KV_HEADS = 5
HEAD_DIM = 64
FF = 2560
GROUP = HEADS // KV_HEADS
ATTN = HEADS * HEAD_DIM
KV = KV_HEADS * HEAD_DIM
AXES = ("dp", "ctx")
CORE, FIRST, SECOND = 1, 2, 4

norm_eps = 1e-05
rope_base = 100000.0
mask_fill = -1000000000.0
low = jnp.bfloat16
wide = jnp.float32


def rms_scale(values):
    return lax.rsqrt(jnp.mean(values * values, axis=-1, keepdims=True) + norm_eps)


def norm_back(values, scale, gain, grad):
    gain_grad = jnp.sum(grad * values * scale, axis=0)
    weighted = grad * gain
    inner = jnp.mean(weighted * values, axis=-1, keepdims=True)
    return (scale * weighted - values * (scale * scale * scale) * inner, gain_grad)


def rope_tables(position):
    freqs = rope_base ** (-jnp.arange(0, HEAD_DIM, 2, dtype=wide) / HEAD_DIM)
    angles = position.astype(wide)[..., None] * freqs
    angles = jnp.concatenate([angles, angles], axis=-1)
    return (jnp.cos(angles)[..., None, :], jnp.sin(angles)[..., None, :])


def rotate(values, cosine, sine):
    half = values.shape[-1] // 2
    turned = jnp.concatenate([-values[..., half:], values[..., :half]], axis=-1)
    return values * cosine + turned * sine


def rotate_back(grad, cosine, sine):
    half = grad.shape[-1] // 2
    scaled = grad * sine
    return grad * cosine + jnp.concatenate([scaled[..., half:], -scaled[..., :half]], axis=-1)


def product(left, right):
    return jnp.dot(left, right, preferred_element_type=wide)


def product_left(left, right):
    return lax.dot_general(left, right, (((0,), (0,)), ((), ())), preferred_element_type=wide)


def product_right(left, right):
    return lax.dot_general(left, right, (((1,), (1,)), ((), ())), preferred_element_type=wide)


def swap(value, mask):
    n = lax.axis_size(AXES)
    return lax.ppermute(value, AXES, [(i, i ^ mask) for i in range(n)])


def add_low(left, right):
    return (left.astype(wide) + right.astype(wide)).astype(low)


def far_masks():
    n = lax.axis_size(AXES)
    masks, m = [], 8
    while m < n:
        masks.append(m)
        m *= 2
    return masks


def block_owner(place):
    far = far_masks()
    owner = jnp.zeros_like(place)
    for bit, mask in enumerate(far + [SECOND, FIRST, CORE]):
        owner = owner | (((place >> bit) & 1) * mask)
    return owner


def gather_far(piece):
    now = piece[None]
    for mask in far_masks():
        now = jnp.concatenate([now, swap(now, mask)], axis=0)
    return now


def gather_near(now, route):
    n = now.shape[0]
    if route == 0:
        now = jnp.concatenate([now, swap(now, SECOND)], axis=0)
        half = jnp.concatenate([now, swap(now, FIRST)], axis=0)
    else:
        side = swap(now, FIRST)
        rest = swap(jnp.concatenate([now, side], axis=0), SECOND)
        half = jnp.concatenate([now, rest[:n], side, rest[n:]], axis=0)
    return half, swap(half, CORE)


def scatter_sum(mine, theirs, route):
    now = add_low(mine, swap(theirs, CORE))
    n = now.shape[0] // 4
    if route == 0:
        now = add_low(now[: 2 * n], swap(now[2 * n :], FIRST))
        now = add_low(now[:n], swap(now[n:], SECOND))
    else:
        send = jnp.concatenate([now[n : 2 * n], now[3 * n :]], axis=0)
        keep = jnp.concatenate([now[:n], now[2 * n : 3 * n]], axis=0)
        now = add_low(keep, swap(send, SECOND))
        now = add_low(now[:n], swap(now[n:], FIRST))
    for mask in far_masks()[::-1]:
        n = now.shape[0] // 2
        now = now[:n].astype(wide) + swap(now[n:], mask).astype(wide)
        if n > 1:
            now = now.astype(low)
    return now[0]


def ctx_masks():
    m, masks = lax.axis_size("ctx") // 2, []
    while m >= 1:
        masks.append(m)
        m //= 2
    return masks


def ctx_gather(value):
    now = value[None]
    for mask in ctx_masks():
        now = jnp.concatenate([now, swap(now, mask)], axis=0)
    return now


def ctx_scatter(value):
    now = value
    for mask in ctx_masks()[::-1]:
        n = now.shape[0] // 2
        now = now[:n].astype(wide) + swap(now[n:], mask).astype(wide)
        if n > 1:
            now = now.astype(low)
    return now[0]


def ctx_owner(places):
    owner = jnp.zeros_like(places)
    for bit, mask in enumerate(ctx_masks()):
        owner = owner | (((places >> bit) & 1) * mask)
    return owner


def move_blocks(parts, order, outs):
    parts = list(parts)
    if outs is None:
        each = parts[0].shape[0]
        total = each * len(parts)
        shapes = [jax.ShapeDtypeStruct((total,) + parts[0].shape[1:], parts[0].dtype)]
    else:
        total = parts[0].shape[0]
        each = total // outs
        shapes = [jax.ShapeDtypeStruct((each,) + parts[0].shape[1:], parts[0].dtype)] * outs
    n_in = len(parts)

    def kernel(order_ref, *refs):
        ins, out, sem = refs[:n_in], refs[n_in:-1], refs[-1]
        copies = []
        for p in range(total):
            if outs is None:
                src, dst = ins[p // each].at[p % each], out[0].at[order_ref[p]]
            else:
                src, dst = ins[0].at[order_ref[p]], out[p // each].at[p % each]
            copies.append(pltpu.make_async_copy(src, dst, sem.at[p]))
        for copy in copies:
            copy.start()
        for copy in copies:
            copy.wait()

    size = sum(p.size for p in parts) * 2
    return pl.pallas_call(
        kernel,
        out_shape=shapes,
        in_specs=[pl.BlockSpec(memory_space=pltpu.SMEM)]
        + [pl.BlockSpec(memory_space=pl.ANY)] * n_in,
        out_specs=[pl.BlockSpec(memory_space=pl.ANY)] * len(shapes),
        scratch_shapes=[pltpu.SemaphoreType.DMA((total,))],
        cost_estimate=pl.CostEstimate(flops=0, bytes_accessed=2 * size, transcendentals=0),
        name="move_blocks",
    )(order, *parts)


def body(
    tokens,
    segment_ids,
    positions,
    norm_attn,
    w_query,
    w_key,
    w_value,
    w_out,
    norm_ffn,
    w_gate,
    w_up,
    w_down,
    cotangent,
):
    seqs, block_len, width = tokens.shape
    n_dev = lax.axis_size(AXES)
    ctx_size = lax.axis_size("ctx")
    me = lax.axis_index(AXES)
    rows = seqs * block_len
    length = block_len * ctx_size
    score_scale = HEAD_DIM ** (-0.5)
    ctx_here = lax.axis_index("ctx")
    places = jnp.arange(n_dev, dtype=jnp.int32)
    blocked = n_dev >= 8 and (n_dev & (n_dev - 1)) == 0 and D % n_dev == 0 and FF % n_dev == 0

    if blocked:
        cut, cut_ff = D // n_dev, FF // n_dev
        pad = -(-cut // 16) * 16
        half_ff = cut_ff // 2
        order = block_owner(places) ^ me
        slot = jnp.arange(n_dev * pad, dtype=jnp.int32)
        source = jnp.where(slot % pad < cut, jnp.repeat(order, pad) * cut + slot % pad, -1)
        perm = (jnp.arange(D, dtype=jnp.int32)[:, None] == source[None, :]).astype(low)

        def spread(value):
            return product(value, perm).astype(low)

        def collect(value):
            return product_right(value, perm)

        def rows_of(shard, columns):
            return jnp.pad(shard.reshape(cut, columns), ((0, pad - cut), (0, 0)))

        own = [
            rows_of(w_query, ATTN),
            jnp.concatenate([rows_of(w_key, KV), rows_of(w_value, KV)], axis=1),
            rows_of(w_out, D),
            rows_of(w_gate, FF),
            rows_of(w_up, FF),
            w_down.reshape(cut_ff, D)[:half_ff],
            w_down.reshape(cut_ff, D)[half_ff:],
        ]
        routes = [0, 1, 1, 0, 1, 0, 1]
        full = []
        before = None
        for piece, route in zip(own, routes):
            if before is not None:
                piece, _ = lax.optimization_barrier((piece, before))
            now = gather_far(piece)
            before = now
            full.append(gather_near(now, route))
        rel = [jnp.concatenate(f, axis=0).reshape(-1, f[0].shape[-1]) for f in full[:5]]
        query_weight, kv_weight, out_weight, gate_weight, up_weight = rel
        down_halves = [
            move_blocks(full[5], order, None)[0],
            move_blocks(full[6], order, None)[0],
        ]
        down_weight = jnp.concatenate(down_halves, axis=1).reshape(FF, D)
    else:
        perm = None

        def spread(value):
            return value

        def collect(value):
            return value.astype(wide)

        def whole(shard, columns):
            return lax.all_gather(shard, AXES, axis=0, tiled=True).reshape(-1, columns)

        query_weight = whole(w_query, ATTN)
        kv_weight = jnp.concatenate([whole(w_key, KV), whole(w_value, KV)], axis=1)
        out_weight = whole(w_out, D)
        gate_weight, up_weight = whole(w_gate, FF), whole(w_up, FF)
        down_weight = whole(w_down, D)

    def collect_wide(value):
        if perm is None:
            return value
        high = lax.reduce_precision(value, 8, 7)
        return collect(high.astype(low)) + collect((value - high).astype(low))

    inputs = tokens.astype(wide).reshape(rows, D)
    grad_out = cotangent.astype(wide).reshape(rows, D)
    segment_all = ctx_gather(segment_ids)
    scale_attn = rms_scale(inputs)
    normed_attn = spread((inputs * scale_attn * norm_attn).astype(low))
    cosine, sine = rope_tables(positions)
    key_value = product(normed_attn, kv_weight).reshape(seqs, block_len, 2 * KV_HEADS, HEAD_DIM)
    key_rot = rotate(key_value[:, :, :KV_HEADS], cosine, sine).astype(low)
    both = jnp.concatenate([key_rot, key_value[:, :, KV_HEADS:].astype(low)], axis=2)
    both_all = ctx_gather(both.reshape(seqs, block_len, 2 * KV))
    query_rot = rotate(
        product(normed_attn, query_weight).reshape(seqs, block_len, HEADS, HEAD_DIM), cosine, sine
    ).astype(low)
    both_all = both_all.transpose(1, 0, 2, 3).reshape(seqs, length, 2, KV_HEADS, HEAD_DIM)
    key_heads, value_heads = both_all[:, :, 0], both_all[:, :, 1]
    segment_all = segment_all.transpose(1, 0, 2).reshape(seqs, length)
    query_index = ctx_here * block_len + jnp.arange(block_len, dtype=jnp.int32)
    key_block = ctx_owner(jnp.arange(ctx_size, dtype=jnp.int32)) ^ ctx_here
    key_index = (
        key_block[:, None] * block_len + jnp.arange(block_len, dtype=jnp.int32)[None, :]
    ).reshape(length)
    query_groups = query_rot.reshape(seqs, block_len, KV_HEADS, GROUP, HEAD_DIM)
    allowed = (
        (segment_ids[:, :, None] == segment_all[:, None, :])
        & (key_index[None, None, :] <= query_index[None, :, None])
    )[:, None, None]

    def masked_scores():
        scores = (
            jnp.einsum("sckgd,slkd->skgcl", query_groups, key_heads, preferred_element_type=wide)
            * score_scale
        )
        return jnp.where(allowed, scores, mask_fill)

    masked = masked_scores()
    row_max = jnp.max(masked, axis=-1, keepdims=True)
    exponent = jnp.exp(masked - row_max)
    total = jnp.sum(exponent, axis=-1, keepdims=True)
    probs_low = (exponent / total).astype(low)
    log_total = row_max + jnp.log(total)
    attended = spread(
        jnp.einsum("skgcl,slkd->sckgd", probs_low, value_heads, preferred_element_type=wide)
        .astype(low)
        .reshape(rows, ATTN)
    )
    resid = inputs + product(attended, out_weight)
    scale_ffn = rms_scale(resid)
    normed_ffn = spread((resid * scale_ffn * norm_ffn).astype(low))
    gate = product(normed_ffn, gate_weight)
    up = product(normed_ffn, up_weight)
    gate_sigmoid = jax.nn.sigmoid(gate)
    hidden = (gate * gate_sigmoid * up).astype(low)
    output = (resid + product(hidden, down_weight)).astype(low).reshape(seqs, block_len, D)

    down_grad = cotangent.reshape(rows, D)
    fresh_down = product_left(hidden, down_grad).astype(low)
    hidden_grad = product_right(down_grad, down_weight)
    gate_grad = (hidden_grad * up * gate_sigmoid * (1.0 + gate * (1.0 - gate_sigmoid))).astype(low)
    up_grad = (hidden_grad * gate * gate_sigmoid).astype(low)

    if blocked:
        split = n_dev * pad // 2

        def weight_grad(left, right, route):
            mine = product_left(left[:, :split], right).astype(low)
            theirs = product_left(left[:, split:], right).astype(low)
            shape = (n_dev // 2, pad, right.shape[-1])
            return scatter_sum(mine.reshape(shape), theirs.reshape(shape), route)[:cut]

        def down_scatter():
            blocks = fresh_down.reshape(n_dev, cut_ff, D)
            first = move_blocks([blocks[:, :half_ff]], order, 2)
            second = move_blocks([blocks[:, half_ff:]], order, 2)
            return jnp.concatenate([scatter_sum(*first, 0), scatter_sum(*second, 1)], axis=0)
    else:

        def weight_grad(left, right, route):
            del route
            full_grad = product_left(left, right).astype(low)
            return full_grad

        def down_scatter():
            return fresh_down

    def finish(grad):
        if blocked:
            return grad.reshape(-1)
        flat = grad.reshape(n_dev, -1)
        return lax.psum_scatter(flat, AXES, scatter_dimension=0, tiled=True).astype(wide).reshape(-1)

    d_down = finish(down_scatter())
    d_gate = finish(weight_grad(normed_ffn, gate_grad, 0))
    d_up = finish(weight_grad(normed_ffn, up_grad, 1))
    normed_grad = collect_wide(
        product_right(gate_grad, gate_weight) + product_right(up_grad, up_weight)
    )
    resid_grad, ffn_gain_grad = norm_back(resid, scale_ffn, norm_ffn, normed_grad)
    resid_grad = resid_grad + grad_out
    branch_grad = resid_grad.astype(low)
    d_out = finish(weight_grad(attended, branch_grad, 1))
    attended_grad = (
        collect(product_right(branch_grad, out_weight).astype(low))
        .astype(low)
        .reshape(seqs, block_len, KV_HEADS, GROUP, HEAD_DIM)
    )
    probs = jnp.exp(masked_scores() - log_total)
    probs_grad = jnp.einsum(
        "sckgd,slkd->skgcl", attended_grad, value_heads, preferred_element_type=wide
    )
    inner = jnp.sum(probs * probs_grad, axis=-1, keepdims=True)
    scores_grad = (probs * (probs_grad - inner)).astype(low)
    query_grad = (
        jnp.einsum("skgcl,slkd->sckgd", scores_grad, key_heads, preferred_element_type=wide)
        * score_scale
    )
    key_part = (
        jnp.einsum("skgcl,sckgd->slkd", scores_grad, query_groups, preferred_element_type=wide)
        * score_scale
    )
    value_part = jnp.einsum(
        "skgcl,sckgd->slkd", probs.astype(low), attended_grad, preferred_element_type=wide
    )
    both_part = jnp.concatenate([key_part, value_part], axis=2).astype(low)
    both_part = both_part.reshape(seqs, ctx_size, block_len, 2 * KV).transpose(1, 0, 2, 3)
    both_grad = ctx_scatter(both_part).reshape(seqs, block_len, 2 * KV_HEADS, HEAD_DIM)
    query_low = (
        rotate_back(query_grad.reshape(seqs, block_len, HEADS, HEAD_DIM), cosine, sine)
        .astype(low)
        .reshape(rows, ATTN)
    )
    key_low = rotate_back(both_grad[:, :, :KV_HEADS], cosine, sine).astype(low)
    both_low = jnp.concatenate([key_low, both_grad[:, :, KV_HEADS:].astype(low)], axis=2)
    both_low = both_low.reshape(rows, 2 * KV)
    d_query = finish(weight_grad(normed_attn, query_low, 0))
    d_both = weight_grad(normed_attn, both_low, 1)
    d_key, d_value = finish(d_both[:, :KV]), finish(d_both[:, KV:])
    attn_normed_grad = collect_wide(
        product_right(query_low, query_weight) + product_right(both_low, kv_weight)
    )
    input_grad, attn_gain_grad = norm_back(inputs, scale_attn, norm_attn, attn_normed_grad)
    d_tokens = (input_grad + resid_grad).reshape(seqs, block_len, D)
    attn_gain_sum, ffn_gain_sum = lax.psum((attn_gain_grad, ffn_gain_grad), AXES)
    return (
        output,
        d_tokens,
        attn_gain_sum,
        d_query,
        d_key,
        d_value,
        d_out,
        ffn_gain_sum,
        d_gate,
        d_up,
        d_down,
    )


def solution(mesh):
    one = P(AXES)
    tok = P("dp", "ctx", None)
    ids = P("dp", "ctx")
    in_specs = (tok, ids, ids, P(), one, one, one, one, P(), one, one, one, tok)
    out_specs = (tok, tok, P(), one, one, one, one, P(), one, one, one)
    return jax.shard_map(body, mesh=mesh, in_specs=in_specs, out_specs=out_specs, check_vma=False)
```

```python
import jax
import jax.numpy as jnp
from jax import lax
from jax.experimental import pallas as pl
from jax.experimental.pallas import tpu as pltpu
from jax.sharding import PartitionSpec as P

D = 960
HEADS = 15
KV_HEADS = 5
HEAD_DIM = 64
FF = 2560
GROUP = HEADS // KV_HEADS
ATTN = HEADS * HEAD_DIM
KV = KV_HEADS * HEAD_DIM
AXES = ("dp", "ctx")
CORE, FIRST, SECOND = 1, 2, 4

norm_eps = 1e-05
rope_base = 100000.0
mask_fill = -1000000000.0
low = jnp.bfloat16
wide = jnp.float32


def rms_scale(values):
    return lax.rsqrt(jnp.mean(values * values, axis=-1, keepdims=True) + norm_eps)


def norm_back(values, scale, gain, grad):
    gain_grad = jnp.sum(grad * values * scale, axis=0)
    weighted = grad * gain
    inner = jnp.mean(weighted * values, axis=-1, keepdims=True)
    return (scale * weighted - values * (scale * scale * scale) * inner, gain_grad)


def rope_tables(position):
    freqs = rope_base ** (-jnp.arange(0, HEAD_DIM, 2, dtype=wide) / HEAD_DIM)
    angles = freqs[:, None] * position.astype(wide)[None, :]
    angles = jnp.concatenate([angles, angles], axis=0)
    return jnp.cos(angles), jnp.sin(angles)


def by_head(values):
    return values.reshape(-1, HEAD_DIM, values.shape[-1])


def rotate(values, cosine, sine):
    values = by_head(values)
    half = HEAD_DIM // 2
    turned = jnp.concatenate([-values[:, half:], values[:, :half]], axis=1)
    return (values * cosine + turned * sine).reshape(-1, values.shape[-1])


def rotate_back(grad, cosine, sine):
    grad = by_head(grad)
    half = HEAD_DIM // 2
    scaled = grad * sine
    turned = jnp.concatenate([scaled[:, half:], -scaled[:, :half]], axis=1)
    return (grad * cosine + turned).reshape(-1, grad.shape[-1])


def product(left, right):
    return jnp.dot(left, right, preferred_element_type=wide)


def product_left(left, right):
    return lax.dot_general(left, right, (((0,), (0,)), ((), ())), preferred_element_type=wide)


def product_right(left, right):
    return lax.dot_general(left, right, (((1,), (1,)), ((), ())), preferred_element_type=wide)


def swap(value, mask):
    n = lax.axis_size(AXES)
    return lax.ppermute(value, AXES, [(i, i ^ mask) for i in range(n)])


def add_low(left, right):
    return (left.astype(wide) + right.astype(wide)).astype(low)


def far_masks():
    n = lax.axis_size(AXES)
    masks, m = [], 8
    while m < n:
        masks.append(m)
        m *= 2
    return masks


def block_owner(place):
    far = far_masks()
    owner = jnp.zeros_like(place)
    for bit, mask in enumerate(far + [SECOND, FIRST, CORE]):
        owner = owner | (((place >> bit) & 1) * mask)
    return owner


def tie(value, deps):
    if not deps:
        return value
    return lax.optimization_barrier((value, tuple(deps)))[0]


def gather_units(units):
    far_done, near_done, results = [], [], []
    for unit in units:
        now = [tie(piece[None], far_done) for piece, _ in unit]
        for mask in far_masks():
            came = [swap(value, mask) for value in now]
            now = [jnp.concatenate(pair, axis=0) for pair in zip(now, came)]
            far_done = came
        now = [tie(value, near_done) for value in now]
        n = now[0].shape[0]
        routes = [route for _, route in unit]
        side = [swap(v, FIRST if r else SECOND) for v, r in zip(now, routes)]
        two = [jnp.concatenate(pair, axis=0) for pair in zip(now, side)]
        rest = [swap(v, SECOND if r else FIRST) for v, r in zip(two, routes)]
        near_done = rest
        half = [
            jnp.concatenate([v, e[:n], d, e[n:]] if r else [t, e], axis=0)
            for v, d, t, e, r in zip(now, side, two, rest, routes)
        ]
        results.append([(h, swap(h, CORE)) for h in half])
    return results


def scatter_core(terms):
    return [(add_low(mine, swap(theirs, CORE)), route) for mine, theirs, route in terms]


def scatter_near(terms, deps):
    out, first_came, last_came = [], [], []
    mid = []
    for now, route in terms:
        n = now.shape[0] // 4
        if route == 0:
            keep, send, mask, then = now[: 2 * n], now[2 * n :], FIRST, SECOND
        else:
            send = jnp.concatenate([now[n : 2 * n], now[3 * n :]], axis=0)
            keep = jnp.concatenate([now[:n], now[2 * n : 3 * n]], axis=0)
            mask, then = SECOND, FIRST
        came = swap(tie(send, deps), mask)
        first_came.append(came)
        mid.append((add_low(keep, came), then))
    for now, then in mid:
        n = now.shape[0] // 2
        came = swap(now[n:], then)
        last_came.append(came)
        out.append(add_low(now[:n], came))
    return out, first_came, last_came


def scatter_far(terms):
    for mask in far_masks()[::-1]:
        n = terms[0].shape[0] // 2
        came = [swap(now[n:], mask) for now in terms]
        terms = [now[:n].astype(wide) + c.astype(wide) for now, c in zip(terms, came)]
        if n > 1:
            terms = [now.astype(low) for now in terms]
    return [now[0] for now in terms]


def sum_all(value):
    n, mask = lax.axis_size(AXES), 1
    while mask < n:
        value = value + swap(value, mask)
        mask *= 2
    return value


def ctx_masks():
    m, masks = lax.axis_size("ctx") // 2, []
    while m >= 1:
        masks.append(m)
        m //= 2
    return masks


def ctx_gather(value):
    now = value[None]
    for mask in ctx_masks():
        now = jnp.concatenate([now, swap(now, mask)], axis=0)
    return now


def ctx_scatter(value):
    now = value
    for mask in ctx_masks()[::-1]:
        n = now.shape[0] // 2
        now = now[:n].astype(wide) + swap(now[n:], mask).astype(wide)
        if n > 1:
            now = now.astype(low)
    return now[0]


def ctx_owner(places):
    owner = jnp.zeros_like(places)
    for bit, mask in enumerate(ctx_masks()):
        owner = owner | (((places >> bit) & 1) * mask)
    return owner


def whole_spec():
    return pl.BlockSpec(memory_space=pltpu.VMEM)


def join_blocks(parts, order):
    (a, b), (c, d) = parts
    half, top, columns = a.shape
    bottom = c.shape[1]

    def kernel(order_ref, a_ref, b_ref, c_ref, d_ref, out_ref):
        def step(p, _):
            near, far = order_ref[p], order_ref[p + half]
            out_ref[near, :top, :] = a_ref[p]
            out_ref[near, top:, :] = c_ref[p]
            out_ref[far, :top, :] = b_ref[p]
            out_ref[far, top:, :] = d_ref[p]
            return 0

        lax.fori_loop(0, half, step, 0)

    shape = (2 * half, top + bottom, columns)
    return pl.pallas_call(
        kernel,
        out_shape=jax.ShapeDtypeStruct(shape, a.dtype),
        in_specs=[pl.BlockSpec(memory_space=pltpu.SMEM)] + [whole_spec()] * 4,
        out_specs=whole_spec(),
        compiler_params=pltpu.CompilerParams(vmem_limit_bytes=24 * 2**20),
        cost_estimate=pl.CostEstimate(
            flops=0, bytes_accessed=4 * shape[0] * shape[1] * columns, transcendentals=0
        ),
        name="join_blocks",
    )(order, a, b, c, d)


def part_blocks(value, order, top):
    total, tall, columns = value.shape
    half = total // 2

    def kernel(order_ref, in_ref, a_ref, b_ref, c_ref, d_ref):
        def step(p, _):
            near, far = order_ref[p], order_ref[p + half]
            a_ref[p] = in_ref[near, :top, :]
            c_ref[p] = in_ref[near, top:, :]
            b_ref[p] = in_ref[far, :top, :]
            d_ref[p] = in_ref[far, top:, :]
            return 0

        lax.fori_loop(0, half, step, 0)

    first = jax.ShapeDtypeStruct((half, top, columns), value.dtype)
    second = jax.ShapeDtypeStruct((half, tall - top, columns), value.dtype)
    return pl.pallas_call(
        kernel,
        out_shape=[first, first, second, second],
        in_specs=[pl.BlockSpec(memory_space=pltpu.SMEM), whole_spec()],
        out_specs=[whole_spec()] * 4,
        compiler_params=pltpu.CompilerParams(vmem_limit_bytes=24 * 2**20),
        cost_estimate=pl.CostEstimate(
            flops=0, bytes_accessed=4 * value.size, transcendentals=0
        ),
        name="part_blocks",
    )(order, value)


def head_rows(ref, head):
    return ref[head * HEAD_DIM : (head + 1) * HEAD_DIM, :]


def key_blocks(kv_ref, start):
    blocks = [kv_ref[b, start : start + HEAD_DIM, :] for b in range(kv_ref.shape[0])]
    return jnp.concatenate(blocks, axis=1)


def turn(value):
    return value.astype(wide).T.astype(low)


def attend_kernel(q_ref, kv_ref, bias_ref, o_ref, lse_ref):
    for g in range(KV_HEADS):
        keys = turn(key_blocks(kv_ref, g * HEAD_DIM))
        values_t = key_blocks(kv_ref, KV + g * HEAD_DIM)
        for h in range(g * GROUP, (g + 1) * GROUP):
            scores = product(keys, head_rows(q_ref, h)) + bias_ref[0]
            top = jnp.max(scores, axis=0, keepdims=True)
            weight = jnp.exp(scores - top)
            total = jnp.sum(weight, axis=0, keepdims=True)
            mixed = product(values_t, weight.astype(low)) / total
            o_ref[h * HEAD_DIM : (h + 1) * HEAD_DIM, :] = mixed.astype(low)
            lse_ref[0, h : h + 1, :] = top + jnp.log(total)


def attend_back_kernel(q_ref, kv_ref, bias_ref, o_ref, lse_ref, do_ref, dq_ref, dkv_ref):
    width = q_ref.shape[1]
    for g in range(KV_HEADS):
        keys_t = key_blocks(kv_ref, g * HEAD_DIM)
        keys = turn(keys_t)
        values = turn(key_blocks(kv_ref, KV + g * HEAD_DIM))
        key_grad, value_grad = None, None
        for h in range(g * GROUP, (g + 1) * GROUP):
            query, grad = head_rows(q_ref, h), head_rows(do_ref, h)
            scores = product(keys, query) + bias_ref[0]
            probs = jnp.exp(scores - lse_ref[0, h : h + 1, :])
            inner = jnp.sum(
                grad.astype(wide) * head_rows(o_ref, h).astype(wide), axis=0, keepdims=True
            )
            scores_grad = (probs * (product(values, grad) - inner)).astype(low)
            dq_ref[h * HEAD_DIM : (h + 1) * HEAD_DIM, :] = product(keys_t, scores_grad)
            from_keys = product_right(scores_grad, query)
            from_values = product_right(probs.astype(low), grad)
            key_grad = from_keys if key_grad is None else key_grad + from_keys
            value_grad = from_values if value_grad is None else value_grad + from_values
        for start, value in ((g * HEAD_DIM, key_grad), (KV + g * HEAD_DIM, value_grad)):
            turned = value.T.astype(low)
            for b in range(kv_ref.shape[0]):
                dkv_ref[b, start : start + HEAD_DIM, :] = turned[:, b * width : (b + 1) * width]


def attention_specs(blocks, block_len, length):
    columns = pl.BlockSpec((ATTN, block_len), lambda s: (0, s))
    pairs = pl.BlockSpec((blocks, 2 * KV, block_len), lambda s: (0, 0, s))
    bias = pl.BlockSpec((1, length, block_len), lambda s: (s, 0, 0))
    logs = pl.BlockSpec((1, HEADS, block_len), lambda s: (s, 0, 0))
    return columns, pairs, bias, logs


def attend(query_t, pairs_t, bias):
    seqs, length, block_len = bias.shape
    columns, pairs, bias_spec, logs = attention_specs(pairs_t.shape[0], block_len, length)
    work = seqs * HEADS * length * block_len
    return pl.pallas_call(
        attend_kernel,
        grid=(seqs,),
        in_specs=[columns, pairs, bias_spec],
        out_specs=[columns, logs],
        out_shape=[
            jax.ShapeDtypeStruct(query_t.shape, low),
            jax.ShapeDtypeStruct((seqs, HEADS, block_len), wide),
        ],
        compiler_params=pltpu.CompilerParams(vmem_limit_bytes=40 * 2**20),
        cost_estimate=pl.CostEstimate(
            flops=4 * work * HEAD_DIM, bytes_accessed=8 * 2**20, transcendentals=work
        ),
        name="attend",
    )(query_t, pairs_t, bias)


def attend_back(query_t, pairs_t, bias, mixed_t, logs_all, grad_t):
    seqs, length, block_len = bias.shape
    columns, pairs, bias_spec, logs = attention_specs(pairs_t.shape[0], block_len, length)
    work = seqs * HEADS * length * block_len
    return pl.pallas_call(
        attend_back_kernel,
        grid=(seqs,),
        in_specs=[columns, pairs, bias_spec, columns, logs, columns],
        out_specs=[columns, pairs],
        out_shape=[
            jax.ShapeDtypeStruct(query_t.shape, wide),
            jax.ShapeDtypeStruct(pairs_t.shape, low),
        ],
        compiler_params=pltpu.CompilerParams(vmem_limit_bytes=48 * 2**20),
        cost_estimate=pl.CostEstimate(
            flops=10 * work * HEAD_DIM, bytes_accessed=14 * 2**20, transcendentals=work
        ),
        name="attend_back",
    )(query_t, pairs_t, bias, mixed_t, logs_all, grad_t)


def body(
    tokens,
    segment_ids,
    positions,
    norm_attn,
    w_query,
    w_key,
    w_value,
    w_out,
    norm_ffn,
    w_gate,
    w_up,
    w_down,
    cotangent,
):
    seqs, block_len, width = tokens.shape
    n_dev = lax.axis_size(AXES)
    ctx_size = lax.axis_size("ctx")
    me = lax.axis_index(AXES)
    rows = seqs * block_len
    length = block_len * ctx_size
    score_scale = HEAD_DIM ** (-0.5)
    ctx_here = lax.axis_index("ctx")
    places = jnp.arange(n_dev, dtype=jnp.int32)
    blocked = n_dev >= 8 and D % n_dev == 0 and FF % (16 * n_dev) == 0

    if blocked:
        cut, cut_ff = D // n_dev, FF // n_dev
        pad = -(-cut // 16) * 16
        top_ff = (cut_ff * 3 // 5) // 8 * 8
        order = block_owner(places) ^ me
        slot = jnp.arange(n_dev * pad, dtype=jnp.int32)
        source = jnp.where(slot % pad < cut, jnp.repeat(order, pad) * cut + slot % pad, -1)
        perm = (jnp.arange(D, dtype=jnp.int32)[:, None] == source[None, :]).astype(low)

        def spread(value):
            return product(value, perm).astype(low)

        def spread_t(value):
            return product_left(value, perm).astype(low)

        def collect(value):
            return product_right(value, perm)

        def collect_t(value):
            return product_right(perm, value)

        def rows_of(shard, columns):
            return jnp.pad(shard.reshape(cut, columns), ((0, pad - cut), (0, 0)))

        down_block = w_down.reshape(cut_ff, D)
        pairs_block = jnp.concatenate([rows_of(w_key, KV), rows_of(w_value, KV)], axis=1)
        units = gather_units(
            [
                [(rows_of(w_query, ATTN), 0), (pairs_block, 1)],
                [(down_block[:top_ff], 0), (rows_of(w_out, D), 1)],
                [(rows_of(w_gate, FF), 0), (rows_of(w_up, FF), 1)],
                [(down_block[top_ff:], 1)],
            ]
        )

        def stacked(halves):
            return jnp.concatenate(halves, axis=0).reshape(-1, halves[0].shape[-1])

        query_weight, kv_weight = stacked(units[0][0]), stacked(units[0][1])
        out_weight = stacked(units[1][1])
        gate_weight, up_weight = stacked(units[2][0]), stacked(units[2][1])
        down_weight = join_blocks((units[1][0], units[3][0]), order).reshape(FF, D)
    else:
        perm = None

        def spread(value):
            return value

        def spread_t(value):
            return value.T

        def collect(value):
            return value.astype(wide)

        def collect_t(value):
            return value.T

        def whole(shard, columns):
            return lax.all_gather(shard, AXES, axis=0, tiled=True).reshape(-1, columns)

        query_weight = whole(w_query, ATTN)
        kv_weight = jnp.concatenate([whole(w_key, KV), whole(w_value, KV)], axis=1)
        out_weight = whole(w_out, D)
        gate_weight, up_weight = whole(w_gate, FF), whole(w_up, FF)
        down_weight = whole(w_down, D)

    def collect_wide(value):
        if perm is None:
            return value
        high = lax.reduce_precision(value, 8, 7)
        return collect(high.astype(low)) + collect((value - high).astype(low))

    inputs = tokens.astype(wide).reshape(rows, D)
    grad_out = cotangent.astype(wide).reshape(rows, D)
    scale_attn = rms_scale(inputs)
    normed_attn = spread((inputs * scale_attn * norm_attn).astype(low))
    cosine, sine = rope_tables(positions.reshape(rows))
    segment_all = ctx_gather(segment_ids).transpose(1, 0, 2).reshape(seqs, length)
    query_index = ctx_here * block_len + jnp.arange(block_len, dtype=jnp.int32)
    key_block = ctx_owner(jnp.arange(ctx_size, dtype=jnp.int32)) ^ ctx_here
    key_index = (
        key_block[:, None] * block_len + jnp.arange(block_len, dtype=jnp.int32)[None, :]
    ).reshape(length)
    allowed = (segment_all[:, :, None] == segment_ids[:, None, :]) & (
        key_index[None, :, None] <= query_index[None, None, :]
    )
    bias = jnp.where(allowed, 0.0, mask_fill)

    def across(weight):
        return lax.dot_general(
            weight, normed_attn, (((0,), (1,)), ((), ())), preferred_element_type=wide
        )

    pairs_t = across(kv_weight)
    pairs_t = jnp.concatenate(
        [rotate(pairs_t[:KV], cosine, sine).astype(low), pairs_t[KV:].astype(low)], axis=0
    )
    pairs_all = ctx_gather(pairs_t)
    query_t = (rotate(across(query_weight), cosine, sine) * score_scale).astype(low)
    mixed_t, logs = attend(query_t, pairs_all, bias)
    attended = spread_t(mixed_t)
    resid = inputs + product(attended, out_weight)
    scale_ffn = rms_scale(resid)
    normed_ffn = spread((resid * scale_ffn * norm_ffn).astype(low))
    gate = product(normed_ffn, gate_weight)
    up = product(normed_ffn, up_weight)
    gate_sigmoid = jax.nn.sigmoid(gate)
    hidden = (gate * gate_sigmoid * up).astype(low)
    output = (resid + product(hidden, down_weight)).astype(low).reshape(seqs, block_len, D)

    down_grad = cotangent.reshape(rows, D)
    fresh_down = product_left(hidden, down_grad).astype(low)
    hidden_grad = product_right(down_grad, down_weight)
    gate_grad = (hidden_grad * up * gate_sigmoid * (1.0 + gate * (1.0 - gate_sigmoid))).astype(low)
    up_grad = (hidden_grad * gate * gate_sigmoid).astype(low)

    if blocked:
        split = n_dev * pad // 2

        def terms(left, right, contract, route):
            dims = (((0,), (contract,)), ((), ()))
            both = []
            for piece in (left[:, :split], left[:, split:]):
                grad = lax.dot_general(piece, right, dims, preferred_element_type=wide).astype(low)
                both.append(grad.reshape(n_dev // 2, pad, -1))
            return (*both, route)

        def flat(grad):
            return grad[:cut].reshape(-1)

        parted = part_blocks(fresh_down.reshape(n_dev, cut_ff, D), order, top_ff)
        core_down = scatter_core([(parted[0], parted[1], 0), (parted[2], parted[3], 1)])
        core_pair = scatter_core(
            [terms(normed_ffn, gate_grad, 0, 0), terms(normed_ffn, up_grad, 0, 1)]
        )
        near_down, _, last_down = scatter_near(core_down, [])
        near_pair, first_pair, last_pair = scatter_near(core_pair, last_down)
        d_down = jnp.concatenate(scatter_far(near_down), axis=0).reshape(-1)
        d_gate, d_up = [flat(g) for g in scatter_far(near_pair)]
    else:

        def finish(left, right, contract):
            grad = lax.dot_general(
                left, right, (((0,), (contract,)), ((), ())), preferred_element_type=wide
            )
            return scatter_whole(grad.astype(low))

        def scatter_whole(grad):
            grad = grad.reshape(n_dev, -1)
            return lax.psum_scatter(grad, AXES, scatter_dimension=0, tiled=True).astype(wide)

        d_down = scatter_whole(fresh_down).reshape(-1)
        d_gate = finish(normed_ffn, gate_grad, 0).reshape(-1)
        d_up = finish(normed_ffn, up_grad, 0).reshape(-1)
        last_down, first_pair, last_pair = [], [], []
    normed_grad = collect_wide(
        product_right(gate_grad, gate_weight) + product_right(up_grad, up_weight)
    )
    resid_grad, ffn_gain_grad = norm_back(resid, scale_ffn, norm_ffn, normed_grad)
    resid_grad = resid_grad + grad_out
    branch_grad = resid_grad.astype(low)
    grad_t = collect_t(product_right(branch_grad, out_weight).astype(low)).astype(low)
    grad_t = tie(grad_t, last_down)
    query_grad_t, pairs_part = attend_back(query_t, pairs_all, bias, mixed_t, logs, grad_t)
    pairs_grad = ctx_scatter(pairs_part)
    query_low = rotate_back(query_grad_t * score_scale, cosine, sine).astype(low)
    pairs_low = jnp.concatenate(
        [rotate_back(pairs_grad[:KV], cosine, sine).astype(low), pairs_grad[KV:].astype(low)],
        axis=0,
    )
    if blocked:
        core_out = scatter_core([terms(attended, branch_grad, 0, 1)])
        near_out, _, last_out = scatter_near(core_out, last_pair)
        core_last = scatter_core(
            [terms(normed_attn, query_low, 1, 0), terms(normed_attn, pairs_low, 1, 1)]
        )
        near_last, _, _ = scatter_near(core_last, last_out)
        d_out = flat(scatter_far(near_out)[0])
        d_query, d_pairs = scatter_far(near_last)
        d_query, d_key, d_value = flat(d_query), flat(d_pairs[:, :KV]), flat(d_pairs[:, KV:])
    else:
        d_out = finish(attended, branch_grad, 0).reshape(-1)
        d_query = finish(normed_attn, query_low, 1).reshape(-1)
        d_key = finish(normed_attn, pairs_low[:KV], 1).reshape(-1)
        d_value = finish(normed_attn, pairs_low[KV:], 1).reshape(-1)

    def back_through(grad_t, weight):
        return lax.dot_general(
            grad_t, weight, (((0,), (1,)), ((), ())), preferred_element_type=wide
        )

    attn_normed_grad = collect_wide(
        back_through(query_low, query_weight) + back_through(pairs_low, kv_weight)
    )
    input_grad, attn_gain_grad = norm_back(inputs, scale_attn, norm_attn, attn_normed_grad)
    d_tokens = (input_grad + resid_grad).reshape(seqs, block_len, D)
    attn_gain_sum, ffn_gain_sum = sum_all(attn_gain_grad), sum_all(ffn_gain_grad)
    return (
        output,
        d_tokens,
        attn_gain_sum,
        d_query,
        d_key,
        d_value,
        d_out,
        ffn_gain_sum,
        d_gate,
        d_up,
        d_down,
    )


def solution(mesh):
    one = P(AXES)
    tok = P("dp", "ctx", None)
    ids = P("dp", "ctx")
    in_specs = (tok, ids, ids, P(), one, one, one, one, P(), one, one, one, tok)
    out_specs = (tok, tok, P(), one, one, one, one, P(), one, one, one)
    return jax.shard_map(body, mesh=mesh, in_specs=in_specs, out_specs=out_specs, check_vma=False)
```

```python
import jax
import jax.numpy as jnp
from jax import lax
from jax.experimental import pallas as pl
from jax.experimental.pallas import tpu as pltpu
from jax.sharding import PartitionSpec as P

D = 960
HEADS = 15
KV_HEADS = 5
HEAD_DIM = 64
FF = 2560
GROUP = HEADS // KV_HEADS
ATTN = HEADS * HEAD_DIM
KV = KV_HEADS * HEAD_DIM
AXES = ("dp", "ctx")
CORE, FIRST, SECOND = 1, 2, 4

norm_eps = 1e-05
rope_base = 100000.0
mask_fill = -1000000000.0
low = jnp.bfloat16
wide = jnp.float32


def rms_scale(values):
    return lax.rsqrt(jnp.mean(values * values, axis=-1, keepdims=True) + norm_eps)


def norm_back(values, scale, gain, grad):
    gain_grad = jnp.sum(grad * values * scale, axis=0)
    weighted = grad * gain
    inner = jnp.mean(weighted * values, axis=-1, keepdims=True)
    return (scale * weighted - values * (scale * scale * scale) * inner, gain_grad)


def rope_tables(position):
    freqs = rope_base ** (-jnp.arange(0, HEAD_DIM, 2, dtype=wide) / HEAD_DIM)
    angles = freqs[:, None] * position.astype(wide)[None, :]
    angles = jnp.concatenate([angles, angles], axis=0)
    return jnp.cos(angles), jnp.sin(angles)


def by_head(values):
    return values.reshape(-1, HEAD_DIM, values.shape[-1])


def rotate(values, cosine, sine):
    values = by_head(values)
    half = HEAD_DIM // 2
    turned = jnp.concatenate([-values[:, half:], values[:, :half]], axis=1)
    return (values * cosine + turned * sine).reshape(-1, values.shape[-1])


def rotate_back(grad, cosine, sine):
    grad = by_head(grad)
    half = HEAD_DIM // 2
    scaled = grad * sine
    turned = jnp.concatenate([scaled[:, half:], -scaled[:, :half]], axis=1)
    return (grad * cosine + turned).reshape(-1, grad.shape[-1])


def product(left, right):
    return jnp.dot(left, right, preferred_element_type=wide)


def product_left(left, right):
    return lax.dot_general(left, right, (((0,), (0,)), ((), ())), preferred_element_type=wide)


def product_right(left, right):
    return lax.dot_general(left, right, (((1,), (1,)), ((), ())), preferred_element_type=wide)


def swap(value, mask):
    n = lax.axis_size(AXES)
    return lax.ppermute(value, AXES, [(i, i ^ mask) for i in range(n)])


def add_low(left, right):
    return (left.astype(wide) + right.astype(wide)).astype(low)


def far_masks():
    n = lax.axis_size(AXES)
    masks, m = [], 8
    while m < n:
        masks.append(m)
        m *= 2
    return masks


def block_owner(place):
    far = far_masks()
    owner = jnp.zeros_like(place)
    for bit, mask in enumerate(far + [SECOND, FIRST, CORE]):
        owner = owner | (((place >> bit) & 1) * mask)
    return owner


class Slots:
    def __init__(self):
        self.deps = ()

    def send(self, pairs):
        values = tuple(value for value, _ in pairs)
        if self.deps:
            values = lax.optimization_barrier((values, self.deps))[0]
        came = [swap(value, mask) for value, (_, mask) in zip(values, pairs)]
        self.deps = tuple(came)
        return came

    def hold(self, *values):
        self.deps = self.deps + values

    def after(self, value):
        return lax.optimization_barrier((value, self.deps))[0]

    def run(self, moves, extra=()):
        pairs = [piece.give(stage) for piece, stage in moves]
        came = self.send(pairs + list(extra))
        for (piece, stage), value in zip(moves, came):
            piece.take(stage, value)
        return came[len(moves) :]


class Gathered:
    def __init__(self, block, route):
        self.now, self.route = block[None], route

    def give(self, stage):
        near = (FIRST, SECOND) if self.route else (SECOND, FIRST)
        return self.now, (8, 16, *near, CORE)[stage]

    def take(self, stage, came):
        if stage == 2:
            self.own, self.side = self.now, came
        if stage == 3 and self.route:
            n = came.shape[0] // 2
            parts = [self.own, came[:n], self.side, came[n:]]
        else:
            parts = [self.now, came]
        if stage == 4:
            self.mine, self.theirs = self.now, came
        else:
            self.now = jnp.concatenate(parts, axis=0)

    def weight(self):
        whole = jnp.concatenate([self.mine, self.theirs], axis=0)
        return whole.reshape(-1, whole.shape[-1])


class Reduced:
    def __init__(self, mine, theirs, route):
        self.mine, self.theirs, self.route = mine, theirs, route

    def give(self, stage):
        near = (SECOND, FIRST) if self.route else (FIRST, SECOND)
        mask = (CORE, *near, 16, 8)[stage]
        if stage == 0:
            return self.theirs, mask
        n = self.now.shape[0] // 2
        if stage == 1 and self.route:
            q = n // 2
            self.keep = jnp.concatenate([self.now[:q], self.now[n : n + q]], axis=0)
            return jnp.concatenate([self.now[q:n], self.now[n + q :]], axis=0), mask
        self.keep = self.now[:n]
        return self.now[n:], mask

    def take(self, stage, came):
        if stage == 0:
            self.now = add_low(self.mine, came)
        elif stage == 4:
            self.result = self.keep[0].astype(wide) + came[0].astype(wide)
        else:
            self.now = add_low(self.keep, came)


def ctx_masks():
    m, masks = lax.axis_size("ctx") // 2, []
    while m >= 1:
        masks.append(m)
        m //= 2
    return masks


def ctx_gather(value):
    now = value[None]
    for mask in ctx_masks():
        now = jnp.concatenate([now, swap(now, mask)], axis=0)
    return now


def ctx_scatter(value):
    now = value
    for mask in ctx_masks()[::-1]:
        n = now.shape[0] // 2
        now = now[:n].astype(wide) + swap(now[n:], mask).astype(wide)
        if n > 1:
            now = now.astype(low)
    return now[0]


def whole_spec():
    return pl.BlockSpec(memory_space=pltpu.VMEM)


def join_blocks(parts, order):
    (a, b), (c, d) = parts
    half, top, columns = a.shape
    bottom = c.shape[1]

    def kernel(order_ref, a_ref, b_ref, c_ref, d_ref, out_ref):
        def step(p, _):
            near, far = order_ref[p], order_ref[p + half]
            out_ref[near, :top, :] = a_ref[p]
            out_ref[near, top:, :] = c_ref[p]
            out_ref[far, :top, :] = b_ref[p]
            out_ref[far, top:, :] = d_ref[p]
            return 0

        lax.fori_loop(0, half, step, 0)

    shape = (2 * half, top + bottom, columns)
    return pl.pallas_call(
        kernel,
        out_shape=jax.ShapeDtypeStruct(shape, a.dtype),
        in_specs=[pl.BlockSpec(memory_space=pltpu.SMEM)] + [whole_spec()] * 4,
        out_specs=whole_spec(),
        compiler_params=pltpu.CompilerParams(vmem_limit_bytes=24 * 2**20),
        cost_estimate=pl.CostEstimate(
            flops=0, bytes_accessed=4 * shape[0] * shape[1] * columns, transcendentals=0
        ),
        name="join_blocks",
    )(order, a, b, c, d)


def down_grad_blocks(hidden, grad, place, top):
    rows, hidden_width = hidden.shape
    columns = grad.shape[1]
    total = place.shape[0]
    tall = hidden_width // total
    group = 8

    def kernel(place_ref, h_ref, g_ref, a_ref, b_ref):
        value = product_left(h_ref[...], g_ref[...]).astype(low)
        first = pl.program_id(0) * group
        for b in range(group):
            to = place_ref[first + b]
            a_ref[to] = value[b * tall : b * tall + top]
            b_ref[to] = value[b * tall + top : (b + 1) * tall]

    return pl.pallas_call(
        kernel,
        grid=(total // group,),
        in_specs=[
            pl.BlockSpec(memory_space=pltpu.SMEM),
            pl.BlockSpec((rows, group * tall), lambda i: (0, i)),
            pl.BlockSpec((rows, columns), lambda i: (0, 0)),
        ],
        out_specs=[
            pl.BlockSpec((total, top, columns), lambda i: (0, 0, 0)),
            pl.BlockSpec((total, tall - top, columns), lambda i: (0, 0, 0)),
        ],
        out_shape=[
            jax.ShapeDtypeStruct((total, top, columns), low),
            jax.ShapeDtypeStruct((total, tall - top, columns), low),
        ],
        compiler_params=pltpu.CompilerParams(vmem_limit_bytes=32 * 2**20),
        cost_estimate=pl.CostEstimate(
            flops=2 * rows * hidden_width * columns,
            bytes_accessed=2 * (rows * (hidden_width + columns) + hidden_width * columns),
            transcendentals=0,
        ),
        name="down_grad_blocks",
    )(place, hidden, grad)


def head_rows(ref, head):
    return ref[head * HEAD_DIM : (head + 1) * HEAD_DIM, :]


def key_blocks(kv_ref, start):
    blocks = [kv_ref[b, start : start + HEAD_DIM, :] for b in range(kv_ref.shape[0])]
    return jnp.concatenate(blocks, axis=1)


def turn(value):
    return value.astype(wide).T.astype(low)


def attend_kernel(q_ref, kv_ref, bias_ref, o_ref, lse_ref):
    for g in range(KV_HEADS):
        keys = turn(key_blocks(kv_ref, g * HEAD_DIM))
        values_t = key_blocks(kv_ref, KV + g * HEAD_DIM)
        for h in range(g * GROUP, (g + 1) * GROUP):
            scores = product(keys, head_rows(q_ref, h)) + bias_ref[0]
            top = jnp.max(scores, axis=0, keepdims=True)
            weight = jnp.exp(scores - top)
            total = jnp.sum(weight, axis=0, keepdims=True)
            mixed = product(values_t, weight.astype(low)) / total
            o_ref[h * HEAD_DIM : (h + 1) * HEAD_DIM, :] = mixed.astype(low)
            lse_ref[0, h : h + 1, :] = top + jnp.log(total)


def attend_back_kernel(q_ref, kv_ref, bias_ref, o_ref, lse_ref, do_ref, dq_ref, dkv_ref):
    width = q_ref.shape[1]
    for g in range(KV_HEADS):
        keys_t = key_blocks(kv_ref, g * HEAD_DIM)
        keys = turn(keys_t)
        values = turn(key_blocks(kv_ref, KV + g * HEAD_DIM))
        key_grad, value_grad = None, None
        for h in range(g * GROUP, (g + 1) * GROUP):
            query, grad = head_rows(q_ref, h), head_rows(do_ref, h)
            scores = product(keys, query) + bias_ref[0]
            probs = jnp.exp(scores - lse_ref[0, h : h + 1, :])
            inner = jnp.sum(
                grad.astype(wide) * head_rows(o_ref, h).astype(wide), axis=0, keepdims=True
            )
            scores_grad = (probs * (product(values, grad) - inner)).astype(low)
            dq_ref[h * HEAD_DIM : (h + 1) * HEAD_DIM, :] = product(keys_t, scores_grad)
            from_keys = product_right(scores_grad, query)
            from_values = product_right(probs.astype(low), grad)
            key_grad = from_keys if key_grad is None else key_grad + from_keys
            value_grad = from_values if value_grad is None else value_grad + from_values
        for start, value in ((g * HEAD_DIM, key_grad), (KV + g * HEAD_DIM, value_grad)):
            turned = value.T.astype(low)
            for b in range(kv_ref.shape[0]):
                dkv_ref[b, start : start + HEAD_DIM, :] = turned[:, b * width : (b + 1) * width]


def attention_specs(blocks, block_len, length, seq):
    columns = pl.BlockSpec((ATTN, block_len), lambda i: (0, seq))
    pairs = pl.BlockSpec((blocks, 2 * KV, block_len), lambda i: (0, 0, seq))
    bias = pl.BlockSpec((1, length, block_len), lambda i: (seq, 0, 0))
    own = pl.BlockSpec((ATTN, block_len), lambda i: (0, 0))
    own_pairs = pl.BlockSpec((blocks, 2 * KV, block_len), lambda i: (0, 0, 0))
    logs = pl.BlockSpec((1, HEADS, block_len), lambda i: (0, 0, 0))
    return columns, pairs, bias, own, own_pairs, logs


def attend(query_t, pairs_t, bias, seq):
    _, length, block_len = bias.shape
    columns, pairs, bias_spec, own, _, logs = attention_specs(
        pairs_t.shape[0], block_len, length, seq
    )
    work = HEADS * length * block_len
    return pl.pallas_call(
        attend_kernel,
        grid=(1,),
        in_specs=[columns, pairs, bias_spec],
        out_specs=[own, logs],
        out_shape=[
            jax.ShapeDtypeStruct((ATTN, block_len), low),
            jax.ShapeDtypeStruct((1, HEADS, block_len), wide),
        ],
        compiler_params=pltpu.CompilerParams(vmem_limit_bytes=40 * 2**20),
        cost_estimate=pl.CostEstimate(
            flops=16 * work * HEAD_DIM, bytes_accessed=8 * 2**20, transcendentals=work
        ),
        name="attend",
    )(query_t, pairs_t, bias)


def attend_back(query_t, pairs_t, bias, mixed_t, logs_all, grad_t, seq):
    _, length, block_len = bias.shape
    columns, pairs, bias_spec, own, own_pairs, logs = attention_specs(
        pairs_t.shape[0], block_len, length, seq
    )
    work = HEADS * length * block_len
    return pl.pallas_call(
        attend_back_kernel,
        grid=(1,),
        in_specs=[columns, pairs, bias_spec, own, logs, columns],
        out_specs=[own, own_pairs],
        out_shape=[
            jax.ShapeDtypeStruct((ATTN, block_len), wide),
            jax.ShapeDtypeStruct((pairs_t.shape[0], 2 * KV, block_len), low),
        ],
        compiler_params=pltpu.CompilerParams(vmem_limit_bytes=48 * 2**20),
        cost_estimate=pl.CostEstimate(
            flops=40 * work * HEAD_DIM, bytes_accessed=14 * 2**20, transcendentals=work
        ),
        name="attend_back",
    )(query_t, pairs_t, bias, mixed_t, logs_all, grad_t)


def key_bias(segment_all, segment_ids, ctx_here, masks):
    blocks, seqs, block_len = segment_all.shape
    place = jnp.arange(blocks, dtype=jnp.int32)
    owner = jnp.zeros_like(place)
    for bit, mask in enumerate(masks):
        owner = owner | (((place >> bit) & 1) * mask)
    inside = jnp.arange(block_len, dtype=jnp.int32)
    key_index = ((owner ^ ctx_here)[:, None] * block_len + inside[None, :]).reshape(-1)
    query_index = ctx_here * block_len + inside
    segments = segment_all.transpose(1, 0, 2).reshape(seqs, -1)
    allowed = (segments[:, :, None] == segment_ids[:, None, :]) & (
        key_index[None, :, None] <= query_index[None, None, :]
    )
    return jnp.where(allowed, 0.0, mask_fill)


def contract(left, right, left_dim, right_dim):
    return lax.dot_general(
        left, right, (((left_dim,), (right_dim,)), ((), ())), preferred_element_type=wide
    )


def silu_parts(gate, up):
    sigmoid = jax.nn.sigmoid(gate)
    return sigmoid, (gate * sigmoid * up).astype(low)


def silu_back(hidden_grad, gate, up, sigmoid):
    gate_grad = (hidden_grad * up * sigmoid * (1.0 + gate * (1.0 - sigmoid))).astype(low)
    return gate_grad, (hidden_grad * gate * sigmoid).astype(low)


def body_blocked(
    tokens, segment_ids, positions, norm_attn, w_query, w_key, w_value, w_out,
    norm_ffn, w_gate, w_up, w_down, cotangent,
):
    seqs, block_len, _ = tokens.shape
    n_dev = lax.axis_size(AXES)
    me, ctx_here = lax.axis_index(AXES), lax.axis_index("ctx")
    rows = seqs * block_len
    score_scale = HEAD_DIM ** (-0.5)
    cut, cut_ff = D // n_dev, FF // n_dev
    pad = -(-cut // 16) * 16
    top_ff = (cut_ff * 3 // 5) // 8 * 8
    half_ff = FF // 2
    split = n_dev * pad // 2
    slots = Slots()

    def rows_of(shard, columns):
        return jnp.pad(shard.reshape(cut, columns), ((0, pad - cut), (0, 0)))

    query_piece = Gathered(rows_of(w_query, ATTN), 0)
    pairs_piece = Gathered(
        jnp.concatenate([rows_of(w_key, KV), rows_of(w_value, KV)], axis=1), 1
    )
    slots.run([(query_piece, 0), (pairs_piece, 0)])
    down_block = w_down.reshape(cut_ff, D)
    top_piece, out_piece = Gathered(down_block[:top_ff], 0), Gathered(rows_of(w_out, D), 1)
    gate_block, up_block = rows_of(w_gate, FF), rows_of(w_up, FF)
    first_pair = Gathered(gate_block[:, :half_ff], 0), Gathered(up_block[:, :half_ff], 1)
    second_pair = Gathered(gate_block[:, half_ff:], 0), Gathered(up_block[:, half_ff:], 1)
    low_piece = Gathered(down_block[top_ff:], 1)

    def at(stage, *pieces):
        return [(piece, stage) for piece in pieces]

    (seg_y,) = slots.run(at(1, query_piece, pairs_piece), [(segment_ids, FIRST)])
    segments = jnp.stack([segment_ids, seg_y])
    places = jnp.arange(n_dev, dtype=jnp.int32)
    order = block_owner(places) ^ me
    place = jnp.sum(jnp.where(order[:, None] == places[None, :], places[:, None], 0), axis=0)
    slot = jnp.arange(n_dev * pad, dtype=jnp.int32)
    source = jnp.where(slot % pad < cut, jnp.repeat(order, pad) * cut + slot % pad, -1)
    perm = (jnp.arange(D, dtype=jnp.int32)[:, None] == source[None, :]).astype(low)
    inputs = tokens.astype(wide).reshape(rows, D)
    scale_attn = rms_scale(inputs)
    normed_attn = product((inputs * scale_attn * norm_attn).astype(low), perm).astype(low)
    (seg_c,) = slots.run(
        at(2, query_piece, pairs_piece) + at(0, top_piece, out_piece), [(segments, CORE)]
    )
    segments = jnp.concatenate([segments, seg_c], axis=0)
    slots.hold(normed_attn)
    slots.run(at(3, query_piece, pairs_piece) + at(1, top_piece, out_piece))
    cosine, sine = rope_tables(positions.reshape(rows))
    bias = key_bias(segments, segment_ids, ctx_here, (2, 1))
    slots.hold(cosine, sine)
    slots.run(at(4, query_piece, pairs_piece) + at(2, top_piece, out_piece) + at(0, *first_pair))
    query_weight, kv_weight = query_piece.weight(), pairs_piece.weight()
    slots.hold(bias)
    slots.run(at(3, top_piece, out_piece) + at(1, *first_pair))
    pairs_t = contract(kv_weight, normed_attn, 0, 1)
    pairs_t = jnp.concatenate(
        [rotate(pairs_t[:KV], cosine, sine).astype(low), pairs_t[KV:].astype(low)], axis=0
    )[None]
    (came,) = slots.run(
        at(2, *first_pair) + at(0, *second_pair) + at(4, top_piece, out_piece), [(pairs_t, FIRST)]
    )
    pairs_all = jnp.concatenate([pairs_t, came], axis=0)
    query_t = contract(query_weight, normed_attn, 0, 1)
    query_t = (rotate(query_t, cosine, sine) * score_scale).astype(low)
    slots.hold(query_t)
    (came,) = slots.run(at(3, *first_pair) + at(1, *second_pair), [(pairs_all, CORE)])
    pairs_all = jnp.concatenate([pairs_all, came], axis=0)
    out_weight = out_piece.weight()
    mixed, logs = [None] * seqs, [None] * seqs
    ahead = (seqs + 1) // 2
    for seq in range(ahead):
        mixed[seq], logs[seq] = attend(query_t, pairs_all, bias, seq)
    slots.run(at(2, *second_pair) + at(0, low_piece) + at(4, *first_pair))
    slots.hold(*mixed[:ahead])
    for seq in range(ahead, seqs):
        mixed[seq], logs[seq] = attend(query_t, pairs_all, bias, seq)
    slots.run(at(3, *second_pair) + at(1, low_piece))
    slots.hold(*mixed[ahead:])
    attended = jnp.concatenate([contract(m, perm, 0, 0).astype(low) for m in mixed], axis=0)
    resid = inputs + product(attended, out_weight)
    scale_ffn = rms_scale(resid)
    normed_ffn = product((resid * scale_ffn * norm_ffn).astype(low), perm).astype(low)
    slots.run(at(2, low_piece) + at(4, *second_pair))
    slots.hold(normed_ffn)
    gate_w, up_w = [first_pair[0].weight()], [first_pair[1].weight()]
    gate, up = [product(normed_ffn, gate_w[0])], [product(normed_ffn, up_w[0])]
    slots.run(at(3, low_piece))
    slots.hold(gate[0], up[0])
    slots.run(at(4, low_piece))
    gate_w.append(second_pair[0].weight())
    up_w.append(second_pair[1].weight())
    gate.append(product(normed_ffn, gate_w[1]))
    up.append(product(normed_ffn, up_w[1]))
    down_weight = join_blocks(
        ((top_piece.mine, top_piece.theirs), (low_piece.mine, low_piece.theirs)), order
    ).reshape(FF, D)
    parts = [silu_parts(g, u) for g, u in zip(gate, up)]
    hidden = jnp.concatenate([h for _, h in parts], axis=1)
    down_grad = cotangent.reshape(rows, D)
    top_grad, low_grad = down_grad_blocks(hidden, down_grad, place, top_ff)
    slots.hold(top_grad)

    half = n_dev // 2
    top_sum = Reduced(top_grad[:half], top_grad[half:], 0)
    low_sum = Reduced(low_grad[:half], low_grad[half:], 1)

    def reduced(left, right, right_dim, route):
        both = []
        for piece in (left[:, :split], left[:, split:]):
            grad = contract(piece, right, 0, right_dim).astype(low)
            both.append(grad.reshape(half, pad, -1))
        return Reduced(*both, route)

    def flat(grad):
        return grad[:cut].reshape(-1)

    slots.run(at(0, top_sum, low_sum))
    output = (resid + product(hidden, down_weight)).astype(low).reshape(seqs, block_len, D)
    gate_grad, up_grad = [], []
    for part in range(2):
        hidden_grad = product_right(
            down_grad, down_weight[part * half_ff : (part + 1) * half_ff]
        )
        a, b = silu_back(hidden_grad, gate[part], up[part], parts[part][0])
        gate_grad.append(a)
        up_grad.append(b)
    slots.hold(gate_grad[0], up_grad[0])
    slots.run(at(1, top_sum, low_sum))
    first_sums = [reduced(normed_ffn, gate_grad[0], 0, 0), reduced(normed_ffn, up_grad[0], 0, 1)]
    slots.hold(output)
    slots.run(at(2, top_sum, low_sum) + at(0, *first_sums))
    second_sums = [reduced(normed_ffn, gate_grad[1], 0, 0), reduced(normed_ffn, up_grad[1], 0, 1)]

    def collect_wide(value):
        high = lax.reduce_precision(value, 8, 7)
        return product_right(high.astype(low), perm) + product_right(
            (value - high).astype(low), perm
        )

    slots.run(at(1, *first_sums) + at(3, top_sum, low_sum) + at(0, *second_sums))
    grad_out = cotangent.astype(wide).reshape(rows, D)
    normed_grad = sum(
        product_right(g, w) for g, w in zip(gate_grad + up_grad, gate_w + up_w)
    )
    normed_grad = collect_wide(normed_grad)
    resid_grad, ffn_gain_grad = norm_back(resid, scale_ffn, norm_ffn, normed_grad)
    resid_grad = resid_grad + grad_out
    branch_grad = resid_grad.astype(low)
    grad_t = product_right(perm, product_right(branch_grad, out_weight).astype(low)).astype(low)
    slots.hold(grad_t)
    back = [None] * seqs
    slots.run(at(2, *first_sums) + at(1, *second_sums) + at(4, top_sum, low_sum))
    for seq in range(ahead):
        back[seq] = attend_back(query_t, pairs_all, bias, mixed[seq], logs[seq], grad_t, seq)
    slots.hold(*[b[0] for b in back[:ahead]])
    out_sum = reduced(attended, branch_grad, 0, 1)
    slots.run(at(2, *second_sums) + at(3, *first_sums) + at(0, out_sum))
    for seq in range(ahead, seqs):
        back[seq] = attend_back(query_t, pairs_all, bias, mixed[seq], logs[seq], grad_t, seq)
    pairs_part = jnp.concatenate([b[1] for b in back], axis=2)
    (came,) = slots.run(
        at(1, out_sum) + at(4, *first_sums) + at(3, *second_sums), [(pairs_part[2:], CORE)]
    )
    pairs_part = add_low(pairs_part[:2], came)
    query_low = jnp.concatenate([b[0] for b in back], axis=1)
    query_low = rotate_back(query_low * score_scale, cosine, sine).astype(low)
    query_sum = reduced(normed_attn, query_low, 1, 0)
    (came,) = slots.run(
        at(2, out_sum) + at(4, *second_sums) + at(0, query_sum), [(pairs_part[1], FIRST)]
    )
    pairs_grad = pairs_part[0].astype(wide) + came.astype(wide)
    pairs_low = jnp.concatenate(
        [rotate_back(pairs_grad[:KV], cosine, sine).astype(low), pairs_grad[KV:].astype(low)],
        axis=0,
    )
    pairs_sum = reduced(normed_attn, pairs_low, 1, 1)
    slots.run(at(1, query_sum) + at(3, out_sum) + at(0, pairs_sum))
    attn_normed_grad = collect_wide(
        contract(query_low, query_weight, 0, 1) + contract(pairs_low, kv_weight, 0, 1)
    )
    input_grad, attn_gain_grad = norm_back(inputs, scale_attn, norm_attn, attn_normed_grad)
    d_tokens = (input_grad + resid_grad).reshape(seqs, block_len, D)
    gains = jnp.stack([attn_gain_grad, ffn_gain_grad])
    slots.run(at(1, pairs_sum) + at(2, query_sum) + at(4, out_sum))
    (came,) = slots.run(at(2, pairs_sum) + at(3, query_sum), [(gains, CORE)])
    gains = gains + came
    a, b, c = slots.run(
        at(3, pairs_sum) + at(4, query_sum), [(gains, m) for m in (FIRST, SECOND, FIRST | SECOND)]
    )
    gains = (gains + a) + (b + c)
    a, b, c = slots.run(at(4, pairs_sum), [(gains, m) for m in (8, 16, 24)])
    gains = (gains + a) + (b + c)
    d_gate, d_up = [
        jnp.concatenate([x.result[:cut], y.result[:cut]], axis=1).reshape(-1)
        for x, y in zip(first_sums, second_sums)
    ]
    return (
        output,
        d_tokens,
        gains[0],
        flat(query_sum.result),
        flat(pairs_sum.result[:, :KV]),
        flat(pairs_sum.result[:, KV:]),
        flat(out_sum.result),
        gains[1],
        d_gate,
        d_up,
        jnp.concatenate([top_sum.result, low_sum.result], axis=0).reshape(-1),
    )


def body_whole(
    tokens, segment_ids, positions, norm_attn, w_query, w_key, w_value, w_out,
    norm_ffn, w_gate, w_up, w_down, cotangent,
):
    seqs, block_len, _ = tokens.shape
    n_dev = lax.axis_size(AXES)
    rows = seqs * block_len
    score_scale = HEAD_DIM ** (-0.5)

    def whole(shard, columns):
        return lax.all_gather(shard, AXES, axis=0, tiled=True).reshape(-1, columns)

    query_weight = whole(w_query, ATTN)
    kv_weight = jnp.concatenate([whole(w_key, KV), whole(w_value, KV)], axis=1)
    out_weight = whole(w_out, D)
    gate_weight, up_weight = whole(w_gate, FF), whole(w_up, FF)
    down_weight = whole(w_down, D)
    inputs = tokens.astype(wide).reshape(rows, D)
    grad_out = cotangent.astype(wide).reshape(rows, D)
    scale_attn = rms_scale(inputs)
    normed_attn = (inputs * scale_attn * norm_attn).astype(low)
    cosine, sine = rope_tables(positions.reshape(rows))
    bias = key_bias(ctx_gather(segment_ids), segment_ids, lax.axis_index("ctx"), ctx_masks())
    pairs_t = contract(kv_weight, normed_attn, 0, 1)
    pairs_t = jnp.concatenate(
        [rotate(pairs_t[:KV], cosine, sine).astype(low), pairs_t[KV:].astype(low)], axis=0
    )
    pairs_all = ctx_gather(pairs_t)
    query_t = contract(query_weight, normed_attn, 0, 1)
    query_t = (rotate(query_t, cosine, sine) * score_scale).astype(low)
    mixed, logs = zip(*[attend(query_t, pairs_all, bias, seq) for seq in range(seqs)])
    attended = jnp.concatenate([m.T for m in mixed], axis=0)
    resid = inputs + product(attended, out_weight)
    scale_ffn = rms_scale(resid)
    normed_ffn = (resid * scale_ffn * norm_ffn).astype(low)
    gate, up = product(normed_ffn, gate_weight), product(normed_ffn, up_weight)
    sigmoid, hidden = silu_parts(gate, up)
    output = (resid + product(hidden, down_weight)).astype(low).reshape(seqs, block_len, D)
    down_grad = cotangent.reshape(rows, D)
    gate_grad, up_grad = silu_back(product_right(down_grad, down_weight), gate, up, sigmoid)
    normed_grad = product_right(gate_grad, gate_weight) + product_right(up_grad, up_weight)
    resid_grad, ffn_gain_grad = norm_back(resid, scale_ffn, norm_ffn, normed_grad)
    resid_grad = resid_grad + grad_out
    branch_grad = resid_grad.astype(low)
    grad_t = product_right(branch_grad, out_weight).astype(low).T
    back = [
        attend_back(query_t, pairs_all, bias, mixed[seq], logs[seq], grad_t, seq)
        for seq in range(seqs)
    ]
    pairs_grad = ctx_scatter(jnp.concatenate([b[1] for b in back], axis=2))
    query_low = jnp.concatenate([b[0] for b in back], axis=1)
    query_low = rotate_back(query_low * score_scale, cosine, sine).astype(low)
    pairs_low = jnp.concatenate(
        [rotate_back(pairs_grad[:KV], cosine, sine).astype(low), pairs_grad[KV:].astype(low)],
        axis=0,
    )
    normed_grad = contract(query_low, query_weight, 0, 1) + contract(pairs_low, kv_weight, 0, 1)
    input_grad, attn_gain_grad = norm_back(inputs, scale_attn, norm_attn, normed_grad)
    d_tokens = (input_grad + resid_grad).reshape(seqs, block_len, D)

    def finish(left, right, right_dim):
        grad = contract(left, right, 0, right_dim).astype(low).reshape(n_dev, -1)
        grad = lax.psum_scatter(grad, AXES, scatter_dimension=0, tiled=True)
        return grad.astype(wide).reshape(-1)

    attn_gain_sum, ffn_gain_sum = lax.psum((attn_gain_grad, ffn_gain_grad), AXES)
    return (
        output,
        d_tokens,
        attn_gain_sum,
        finish(normed_attn, query_low, 1),
        finish(normed_attn, pairs_low[:KV], 1),
        finish(normed_attn, pairs_low[KV:], 1),
        finish(attended, branch_grad, 0),
        ffn_gain_sum,
        finish(normed_ffn, gate_grad, 0),
        finish(normed_ffn, up_grad, 0),
        finish(hidden, down_grad, 0),
    )


def solution(mesh):
    sizes = dict(mesh.shape)
    blocked = sizes["dp"] == 8 and sizes["ctx"] == 4
    body = body_blocked if blocked else body_whole
    one = P(AXES)
    tok = P("dp", "ctx", None)
    ids = P("dp", "ctx")
    in_specs = (tok, ids, ids, P(), one, one, one, one, P(), one, one, one, tok)
    out_specs = (tok, tok, P(), one, one, one, one, P(), one, one, one)
    return jax.shard_map(body, mesh=mesh, in_specs=in_specs, out_specs=out_specs, check_vma=False)
```

```python
import jax
import jax.numpy as jnp
from jax import lax
from jax.experimental import pallas as pl
from jax.experimental.pallas import tpu as pltpu
from jax.sharding import PartitionSpec as P

D = 960
HEADS = 15
KV_HEADS = 5
HEAD_DIM = 64
FF = 2560
GROUP = HEADS // KV_HEADS
ATTN = HEADS * HEAD_DIM
KV = KV_HEADS * HEAD_DIM
AXES = ("dp", "ctx")
CORE, FIRST, SECOND = 1, 2, 4

norm_eps = 1e-05
rope_base = 100000.0
mask_fill = -1000000000.0
low = jnp.bfloat16
wide = jnp.float32


def rms_scale(values):
    return lax.rsqrt(jnp.mean(values * values, axis=-1, keepdims=True) + norm_eps)


def norm_back(values, scale, gain, grad):
    gain_grad = jnp.sum(grad * values * scale, axis=0)
    weighted = grad * gain
    inner = jnp.mean(weighted * values, axis=-1, keepdims=True)
    return (scale * weighted - values * (scale * scale * scale) * inner, gain_grad)


def rope_tables(position):
    freqs = rope_base ** (-jnp.arange(0, HEAD_DIM, 2, dtype=wide) / HEAD_DIM)
    angles = freqs[:, None] * position.astype(wide)[None, :]
    angles = jnp.concatenate([angles, angles], axis=0)
    return jnp.cos(angles), jnp.sin(angles)


def by_head(values):
    return values.reshape(-1, HEAD_DIM, values.shape[-1])


def rotate(values, cosine, sine):
    values = by_head(values)
    half = HEAD_DIM // 2
    turned = jnp.concatenate([-values[:, half:], values[:, :half]], axis=1)
    return (values * cosine + turned * sine).reshape(-1, values.shape[-1])


def rotate_back(grad, cosine, sine):
    grad = by_head(grad)
    half = HEAD_DIM // 2
    scaled = grad * sine
    turned = jnp.concatenate([scaled[:, half:], -scaled[:, :half]], axis=1)
    return (grad * cosine + turned).reshape(-1, grad.shape[-1])


def product(left, right):
    return jnp.dot(left, right, preferred_element_type=wide)


def product_left(left, right):
    return lax.dot_general(left, right, (((0,), (0,)), ((), ())), preferred_element_type=wide)


def product_right(left, right):
    return lax.dot_general(left, right, (((1,), (1,)), ((), ())), preferred_element_type=wide)


def swap(value, mask):
    n = lax.axis_size(AXES)
    return lax.ppermute(value, AXES, [(i, i ^ mask) for i in range(n)])


def add_low(left, right):
    return (left.astype(wide) + right.astype(wide)).astype(low)


def far_masks():
    n = lax.axis_size(AXES)
    masks, m = [], 8
    while m < n:
        masks.append(m)
        m *= 2
    return masks


def block_owner(place):
    far = far_masks()
    owner = jnp.zeros_like(place)
    for bit, mask in enumerate(far + [SECOND, FIRST, CORE]):
        owner = owner | (((place >> bit) & 1) * mask)
    return owner


class Slots:
    def __init__(self):
        self.deps = ()

    def after(self, value):
        return lax.optimization_barrier((value, self.deps))[0]

    def hold(self, *values):
        self.deps = self.deps + values

    def run(self, moves, late=()):
        values = tuple(move.give() for move in (*moves, *late))
        if self.deps:
            values = lax.optimization_barrier((values, self.deps))[0]
        for i, (move, value) in enumerate(zip((*moves, *late), values)):
            if i == 0:
                self.deps = ()
            came = swap(value, move.mask)
            if i < len(moves):
                self.deps += (came,)
            move.take(came)


class Move:
    def __init__(self, value, mask):
        self.value, self.mask = value, mask

    def give(self):
        return self.value

    def take(self, came):
        self.came = came


class Spread(Move):
    def take(self, came):
        self.both = jnp.concatenate([self.value, came], axis=0)


class SpreadBetween(Spread):
    def __init__(self, first, mask):
        self.own, self.side = first.value, first.came
        super().__init__(first.both, mask)

    def take(self, came):
        n = came.shape[0] // 2
        self.both = jnp.concatenate([self.own, came[:n], self.side, came[n:]], axis=0)


class SpreadFirst(Spread):
    def take(self, came):
        self.came = came
        super().take(came)


class Fold(Move):
    def __init__(self, value, mask, last=False):
        self.n, self.last = value.shape[0] // 2, last
        super().__init__(value, mask)

    def give(self):
        return self.value[self.n :]

    def take(self, came):
        if self.last:
            self.sum = self.value[0].astype(wide) + came[0].astype(wide)
        else:
            self.sum = add_low(self.value[: self.n], came)


class FoldPair(Fold):
    def __init__(self, mine, theirs, mask):
        self.value, self.theirs, self.mask, self.last = mine, theirs, mask, False
        self.n = mine.shape[0]

    def give(self):
        return self.theirs


class FoldBetween(Fold):
    def give(self):
        q = self.n // 2
        return jnp.concatenate([self.value[q : self.n], self.value[self.n + q :]], axis=0)

    def take(self, came):
        q = self.n // 2
        kept = jnp.concatenate([self.value[:q], self.value[self.n : self.n + q]], axis=0)
        self.sum = add_low(kept, came)


def ctx_masks():
    m, masks = lax.axis_size("ctx") // 2, []
    while m >= 1:
        masks.append(m)
        m //= 2
    return masks


def ctx_gather(value):
    now = value[None]
    for mask in ctx_masks():
        now = jnp.concatenate([now, swap(now, mask)], axis=0)
    return now


def ctx_scatter(value):
    now = value
    for mask in ctx_masks()[::-1]:
        n = now.shape[0] // 2
        now = now[:n].astype(wide) + swap(now[n:], mask).astype(wide)
        if n > 1:
            now = now.astype(low)
    return now[0]


def whole_spec():
    return pl.BlockSpec(memory_space=pltpu.VMEM)


def join_blocks(tops, lows, order, low_rows):
    (a, b), (c, d) = tops, lows
    half, top, columns = a.shape
    rest = c.shape[1] - low_rows

    def kernel(order_ref, a_ref, b_ref, c_ref, d_ref, down_ref, out_ref):
        def step(p, _):
            near, far = order_ref[p], order_ref[p + half]
            down_ref[near, :top, :] = a_ref[p]
            down_ref[near, top:, :] = c_ref[p, :low_rows, :]
            down_ref[far, :top, :] = b_ref[p]
            down_ref[far, top:, :] = d_ref[p, :low_rows, :]
            out_ref[p] = c_ref[p, low_rows:, :]
            out_ref[p + half] = d_ref[p, low_rows:, :]
            return 0

        lax.fori_loop(0, half, step, 0)

    shape = (2 * half, top + low_rows, columns)
    return pl.pallas_call(
        kernel,
        out_shape=[
            jax.ShapeDtypeStruct(shape, a.dtype),
            jax.ShapeDtypeStruct((2 * half, rest, columns), a.dtype),
        ],
        in_specs=[pl.BlockSpec(memory_space=pltpu.SMEM)] + [whole_spec()] * 4,
        out_specs=[whole_spec()] * 2,
        compiler_params=pltpu.CompilerParams(vmem_limit_bytes=32 * 2**20),
        cost_estimate=pl.CostEstimate(flops=0, bytes_accessed=2**20, transcendentals=0),
        name="join_blocks",
    )(order, a, b, c, d)


def down_grad_blocks(hidden, grad, place, top):
    rows, hidden_width = hidden.shape
    columns = grad.shape[1]
    total = place.shape[0]
    tall = hidden_width // total
    group = 8

    def kernel(place_ref, h_ref, g_ref, a_ref, b_ref):
        value = product_left(h_ref[...], g_ref[...]).astype(low)
        first = pl.program_id(0) * group
        for b in range(group):
            to = place_ref[first + b]
            a_ref[to] = value[b * tall : b * tall + top]
            b_ref[to] = value[b * tall + top : (b + 1) * tall]

    return pl.pallas_call(
        kernel,
        grid=(total // group,),
        in_specs=[
            pl.BlockSpec(memory_space=pltpu.SMEM),
            pl.BlockSpec((rows, group * tall), lambda i: (0, i)),
            pl.BlockSpec((rows, columns), lambda i: (0, 0)),
        ],
        out_specs=[
            pl.BlockSpec((total, top, columns), lambda i: (0, 0, 0)),
            pl.BlockSpec((total, tall - top, columns), lambda i: (0, 0, 0)),
        ],
        out_shape=[
            jax.ShapeDtypeStruct((total, top, columns), low),
            jax.ShapeDtypeStruct((total, tall - top, columns), low),
        ],
        compiler_params=pltpu.CompilerParams(vmem_limit_bytes=32 * 2**20),
        cost_estimate=pl.CostEstimate(
            flops=2 * rows * hidden_width * columns,
            bytes_accessed=2 * (rows * (hidden_width + columns) + hidden_width * columns),
            transcendentals=0,
        ),
        name="down_grad_blocks",
    )(place, hidden, grad)


def head_rows(ref, head):
    return ref[head * HEAD_DIM : (head + 1) * HEAD_DIM, :]


def key_blocks(kv_ref, start):
    blocks = [kv_ref[b, start : start + HEAD_DIM, :] for b in range(kv_ref.shape[0])]
    return jnp.concatenate(blocks, axis=1)


def turn(value):
    return value.astype(wide).T.astype(low)


def attend_kernel(q_ref, kv_ref, bias_ref, o_ref, lse_ref):
    for g in range(KV_HEADS):
        keys = turn(key_blocks(kv_ref, g * HEAD_DIM))
        values_t = key_blocks(kv_ref, KV + g * HEAD_DIM)
        for h in range(g * GROUP, (g + 1) * GROUP):
            scores = product(keys, head_rows(q_ref, h)) + bias_ref[0]
            top = jnp.max(scores, axis=0, keepdims=True)
            weight = jnp.exp(scores - top)
            total = jnp.sum(weight, axis=0, keepdims=True)
            mixed = product(values_t, weight.astype(low)) / total
            o_ref[h * HEAD_DIM : (h + 1) * HEAD_DIM, :] = mixed.astype(low)
            lse_ref[0, h : h + 1, :] = top + jnp.log(total)


def attend_back_kernel(q_ref, kv_ref, bias_ref, o_ref, lse_ref, do_ref, dq_ref, dkv_ref):
    width = q_ref.shape[1]
    for g in range(KV_HEADS):
        keys_t = key_blocks(kv_ref, g * HEAD_DIM)
        keys = turn(keys_t)
        values = turn(key_blocks(kv_ref, KV + g * HEAD_DIM))
        key_grad, value_grad = None, None
        for h in range(g * GROUP, (g + 1) * GROUP):
            query, grad = head_rows(q_ref, h), head_rows(do_ref, h)
            scores = product(keys, query) + bias_ref[0]
            probs = jnp.exp(scores - lse_ref[0, h : h + 1, :])
            inner = jnp.sum(
                grad.astype(wide) * head_rows(o_ref, h).astype(wide), axis=0, keepdims=True
            )
            scores_grad = (probs * (product(values, grad) - inner)).astype(low)
            dq_ref[h * HEAD_DIM : (h + 1) * HEAD_DIM, :] = product(keys_t, scores_grad)
            from_keys = product_right(scores_grad, query)
            from_values = product_right(probs.astype(low), grad)
            key_grad = from_keys if key_grad is None else key_grad + from_keys
            value_grad = from_values if value_grad is None else value_grad + from_values
        for start, value in ((g * HEAD_DIM, key_grad), (KV + g * HEAD_DIM, value_grad)):
            turned = value.T.astype(low)
            for b in range(kv_ref.shape[0]):
                dkv_ref[b, start : start + HEAD_DIM, :] = turned[:, b * width : (b + 1) * width]


def attention_specs(blocks, block_len, length, seq):
    columns = pl.BlockSpec((ATTN, block_len), lambda i: (0, seq))
    pairs = pl.BlockSpec((blocks, 2 * KV, block_len), lambda i: (0, 0, seq))
    bias = pl.BlockSpec((1, length, block_len), lambda i: (seq, 0, 0))
    own = pl.BlockSpec((ATTN, block_len), lambda i: (0, 0))
    own_pairs = pl.BlockSpec((blocks, 2 * KV, block_len), lambda i: (0, 0, 0))
    logs = pl.BlockSpec((1, HEADS, block_len), lambda i: (0, 0, 0))
    return columns, pairs, bias, own, own_pairs, logs


def attend(query_t, pairs_t, bias, seq):
    _, length, block_len = bias.shape
    columns, pairs, bias_spec, own, _, logs = attention_specs(
        pairs_t.shape[0], block_len, length, seq
    )
    work = HEADS * length * block_len
    return pl.pallas_call(
        attend_kernel,
        grid=(1,),
        in_specs=[columns, pairs, bias_spec],
        out_specs=[own, logs],
        out_shape=[
            jax.ShapeDtypeStruct((ATTN, block_len), low),
            jax.ShapeDtypeStruct((1, HEADS, block_len), wide),
        ],
        compiler_params=pltpu.CompilerParams(vmem_limit_bytes=40 * 2**20),
        cost_estimate=pl.CostEstimate(
            flops=work, bytes_accessed=2**20, transcendentals=0
        ),
        name="attend",
    )(query_t, pairs_t, bias)


def attend_back(query_t, pairs_t, bias, mixed_t, logs_all, grad_t, seq):
    _, length, block_len = bias.shape
    columns, pairs, bias_spec, own, own_pairs, logs = attention_specs(
        pairs_t.shape[0], block_len, length, seq
    )
    work = HEADS * length * block_len
    return pl.pallas_call(
        attend_back_kernel,
        grid=(1,),
        in_specs=[columns, pairs, bias_spec, own, logs, columns],
        out_specs=[own, own_pairs],
        out_shape=[
            jax.ShapeDtypeStruct((ATTN, block_len), wide),
            jax.ShapeDtypeStruct((pairs_t.shape[0], 2 * KV, block_len), low),
        ],
        compiler_params=pltpu.CompilerParams(vmem_limit_bytes=48 * 2**20),
        cost_estimate=pl.CostEstimate(
            flops=work, bytes_accessed=2**20, transcendentals=0
        ),
        name="attend_back",
    )(query_t, pairs_t, bias, mixed_t, logs_all, grad_t)


def key_bias(segment_all, segment_ids, ctx_here, masks):
    blocks, seqs, block_len = segment_all.shape
    place = jnp.arange(blocks, dtype=jnp.int32)
    owner = jnp.zeros_like(place)
    for bit, mask in enumerate(masks):
        owner = owner | (((place >> bit) & 1) * mask)
    inside = jnp.arange(block_len, dtype=jnp.int32)
    key_index = ((owner ^ ctx_here)[:, None] * block_len + inside[None, :]).reshape(-1)
    query_index = ctx_here * block_len + inside
    segments = segment_all.transpose(1, 0, 2).reshape(seqs, -1)
    allowed = (segments[:, :, None] == segment_ids[:, None, :]) & (
        key_index[None, :, None] <= query_index[None, None, :]
    )
    return jnp.where(allowed, 0.0, mask_fill)


def contract(left, right, left_dim, right_dim):
    return lax.dot_general(
        left, right, (((left_dim,), (right_dim,)), ((), ())), preferred_element_type=wide
    )


def silu_parts(gate, up):
    sigmoid = jax.nn.sigmoid(gate)
    return sigmoid, (gate * sigmoid * up).astype(low)


def silu_back(hidden_grad, gate, up, sigmoid):
    gate_grad = (hidden_grad * up * sigmoid * (1.0 + gate * (1.0 - sigmoid))).astype(low)
    return gate_grad, (hidden_grad * gate * sigmoid).astype(low)


def body_blocked(
    tokens, segment_ids, positions, norm_attn, w_query, w_key, w_value, w_out,
    norm_ffn, w_gate, w_up, w_down, cotangent,
):
    seqs, block_len, _ = tokens.shape
    n_dev = lax.axis_size(AXES)
    me, ctx_here = lax.axis_index(AXES), lax.axis_index("ctx")
    rows = seqs * block_len
    score_scale = HEAD_DIM ** (-0.5)
    cut, cut_ff = D // n_dev, FF // n_dev
    pad = -(-cut // 16) * 16
    top_ff = (cut_ff * 3 // 5) // 8 * 8
    low_ff = cut_ff - top_ff
    half = n_dev // 2
    split = half * pad
    slots = Slots()
    ahead = (seqs + 1) // 2

    def rows_of(shard, columns):
        return jnp.pad(shard.reshape(cut, columns), ((0, pad - cut), (0, 0)))

    def weight(move):
        return move.both.reshape(-1, move.both.shape[-1])

    attn_block = jnp.concatenate(
        [rows_of(w_key, KV), rows_of(w_value, KV), rows_of(w_query, ATTN)], axis=1
    )[None]
    attn = Spread(attn_block, 8)
    slots.run([attn])
    mix_block = jnp.concatenate([w_down.reshape(cut_ff, D), rows_of(w_out, D)], axis=0)[None]
    mix = Spread(mix_block, 8)
    attn = Spread(attn.both, 16)
    seg_y = Move(slots.after(segment_ids), FIRST)
    inputs = slots.after(tokens).astype(wide).reshape(rows, D)
    slots.run([attn, mix], [seg_y])
    places = jnp.arange(n_dev, dtype=jnp.int32)
    order = block_owner(places) ^ me
    place = jnp.sum(jnp.where(order[:, None] == places[None, :], places[:, None], 0), axis=0)
    slot = jnp.arange(n_dev * pad, dtype=jnp.int32)
    source = jnp.where(slot % pad < cut, jnp.repeat(order, pad) * cut + slot % pad, -1)
    perm = (jnp.arange(D, dtype=jnp.int32)[:, None] == source[None, :]).astype(low)
    scale_attn = rms_scale(inputs)
    normed_attn = product((inputs * scale_attn * norm_attn).astype(low), perm).astype(low)
    segments = jnp.stack([segment_ids, seg_y.came])
    seg_c = Move(segments, CORE)
    pairs_w = SpreadFirst(attn.both[..., : 2 * KV], FIRST)
    query_w = Spread(attn.both[..., 2 * KV :], SECOND)
    mix = Spread(mix.both, 16)
    angles = slots.after(positions).reshape(rows)
    slots.run([pairs_w, query_w], [mix, seg_c])
    cosine, sine = rope_tables(angles)
    segments = jnp.concatenate([segments, seg_c.came], axis=0)
    bias = key_bias(slots.after(segments), segment_ids, ctx_here, (2, 1))
    slots.hold(normed_attn)
    pairs_w = SpreadBetween(pairs_w, SECOND)
    query_w = Spread(query_w.both, FIRST)
    pair_block = jnp.concatenate([rows_of(w_gate, FF), rows_of(w_up, FF)], axis=1)[None]
    pair = Spread(pair_block, 8)
    slots.run([pairs_w, query_w], [pair])
    slots.hold(cosine, sine)
    pairs_w, query_w = Spread(pairs_w.both, CORE), Spread(query_w.both, CORE)
    top_w, low_w = Spread(mix.both[:, :top_ff], SECOND), SpreadFirst(mix.both[:, top_ff:], FIRST)
    pair = Spread(pair.both, 16)
    slots.run([pairs_w, query_w, top_w, low_w], [pair])
    query_weight, kv_weight = weight(query_w), weight(pairs_w)
    top_w, low_w = Spread(top_w.both, FIRST), SpreadBetween(low_w, SECOND)
    slots.run([], [top_w, low_w])
    pairs_t = contract(kv_weight, normed_attn, 0, 1)
    pairs_t = jnp.concatenate(
        [rotate(pairs_t[:KV], cosine, sine).astype(low), pairs_t[KV:].astype(low)], axis=0
    )[None]
    pairs_all = Spread(pairs_t, FIRST)
    gate_w = Spread(pair.both[..., :FF], SECOND)
    slots.hold(bias)
    slots.run([pairs_all], [gate_w])
    query_t = contract(query_weight, normed_attn, 0, 1)
    query_t = (rotate(query_t, cosine, sine) * score_scale).astype(low)
    slots.hold(query_t)
    pairs_all = Spread(pairs_all.both, CORE)
    up_w = SpreadFirst(pair.both[..., FF:], FIRST)
    top_core = Move(top_w.both, CORE)
    low_core = Move(low_w.both, CORE)
    slots.run([pairs_all], [up_w, top_core, low_core])
    pairs_all = pairs_all.both
    mixed, logs = [None] * seqs, [None] * seqs
    for seq in range(ahead):
        mixed[seq], logs[seq] = attend(query_t, pairs_all, bias, seq)
    gate_w, up_w = Spread(gate_w.both, FIRST), SpreadBetween(up_w, SECOND)
    slots.run([], [gate_w, up_w])
    slots.hold(up_w.own)
    for seq in range(ahead, seqs):
        mixed[seq], logs[seq] = attend(slots.after(query_t), pairs_all, bias, seq)
    down_weight, out_weight = join_blocks(
        (top_w.both, top_core.came), (low_w.both, low_core.came), order, low_ff
    )
    down_weight, out_weight = down_weight.reshape(FF, D), out_weight.reshape(-1, D)
    gate_w, up_w = Spread(gate_w.both, CORE), Spread(up_w.both, CORE)
    slots.run([], [gate_w, up_w])
    attended = jnp.concatenate([contract(m, perm, 0, 0).astype(low) for m in mixed], axis=0)
    resid = inputs + product(attended, out_weight)
    scale_ffn = rms_scale(resid)
    normed_ffn = product((resid * scale_ffn * norm_ffn).astype(low), perm).astype(low)
    gate_weight, up_weight = weight(gate_w), weight(up_w)
    gate, up = product(normed_ffn, gate_weight), product(normed_ffn, up_weight)
    sigmoid, hidden = silu_parts(gate, up)
    down_grad = cotangent.reshape(rows, D)
    top_grad, low_grad = down_grad_blocks(hidden, down_grad, place, top_ff)

    def halves(left, right, right_dim):
        both = []
        for piece in (left[:, :split], left[:, split:]):
            grad = contract(piece, right, 0, right_dim).astype(low)
            both.append(grad.reshape(half, pad, -1))
        return FoldPair(*both, CORE)

    def flat(grad):
        return grad[:cut].reshape(-1)

    def collect_wide(value):
        high = lax.reduce_precision(value, 8, 7)
        return product_right(high.astype(low), perm) + product_right(
            (value - high).astype(low), perm
        )

    top_s = FoldPair(top_grad[:half], top_grad[half:], CORE)
    low_s = FoldPair(low_grad[:half], low_grad[half:], CORE)
    slots.run([top_s, low_s])
    hidden_grad = product_right(down_grad, down_weight)
    gate_grad, up_grad = silu_back(hidden_grad, gate, up, sigmoid)
    slots.hold(gate_grad, up_grad)
    top_s, low_s = Fold(top_s.sum, FIRST), FoldBetween(low_s.sum, SECOND)
    slots.run([top_s, low_s])
    gate_s, up_s = halves(normed_ffn, gate_grad, 0), halves(normed_ffn, up_grad, 0)
    top_s, low_s = Fold(top_s.sum, SECOND), Fold(low_s.sum, FIRST)
    slots.run([gate_s, up_s, top_s, low_s])
    normed_grad = product_right(gate_grad, gate_weight) + product_right(up_grad, up_weight)
    normed_grad = collect_wide(normed_grad)
    grad_out = cotangent.astype(wide).reshape(rows, D)
    resid_grad, ffn_gain_grad = norm_back(resid, scale_ffn, norm_ffn, normed_grad)
    resid_grad = resid_grad + grad_out
    branch_grad = resid_grad.astype(low)
    grad_t = product_right(perm, product_right(branch_grad, out_weight).astype(low)).astype(low)
    gate_s, up_s = Fold(gate_s.sum, FIRST), FoldBetween(up_s.sum, SECOND)
    down_s = Fold(jnp.concatenate([top_s.sum, low_s.sum], axis=1), 16)
    grad_t = slots.after(grad_t)
    slots.run([gate_s, up_s], [down_s])
    back = [
        attend_back(query_t, pairs_all, bias, mixed[seq], logs[seq], grad_t, seq)
        for seq in range(seqs)
    ]
    pairs_part = jnp.concatenate([b[1] for b in back], axis=2)
    pairs_s = FoldPair(pairs_part[:2], pairs_part[2:], CORE)
    gate_s, up_s = Fold(gate_s.sum, SECOND), Fold(up_s.sum, FIRST)
    down_s = Fold(down_s.sum, 8, last=True)
    slots.run([pairs_s], [gate_s, up_s, down_s])
    out_s = halves(slots.after(attended), branch_grad, 0)
    pairs_s = Fold(pairs_s.sum, FIRST, last=True)
    slots.run([pairs_s], [out_s])
    query_low = jnp.concatenate([b[0] for b in back], axis=1)
    query_low = rotate_back(slots.after(query_low) * score_scale, cosine, sine).astype(low)
    query_s = halves(normed_attn, query_low, 1)
    pairs_grad = pairs_s.sum
    pairs_low = jnp.concatenate(
        [rotate_back(pairs_grad[:KV], cosine, sine).astype(low), pairs_grad[KV:].astype(low)],
        axis=0,
    )
    pairs_s = halves(normed_attn, pairs_low, 1)
    out_s = FoldBetween(out_s.sum, SECOND)
    pair_s = Fold(jnp.concatenate([gate_s.sum, up_s.sum], axis=2), 16)
    slots.run([pairs_s, query_s, out_s], [pair_s])
    attn_normed_grad = collect_wide(
        contract(query_low, query_weight, 0, 1) + contract(pairs_low, kv_weight, 0, 1)
    )
    input_grad, attn_gain_grad = norm_back(inputs, scale_attn, norm_attn, attn_normed_grad)
    d_tokens = (input_grad + resid_grad).reshape(seqs, block_len, D)
    output = (resid + product(slots.after(hidden), down_weight)).astype(low)
    output = output.reshape(seqs, block_len, D)
    query_s, pairs_s = Fold(query_s.sum, FIRST), FoldBetween(pairs_s.sum, SECOND)
    out_s = Fold(out_s.sum, FIRST)
    slots.run([query_s, pairs_s, out_s])
    query_s, pairs_s = Fold(query_s.sum, SECOND), Fold(pairs_s.sum, FIRST)
    out_s = Fold(out_s.sum, 16)
    pair_s = Fold(pair_s.sum, 8, last=True)
    gains = Move(jnp.stack([attn_gain_grad, ffn_gain_grad]), CORE)
    slots.run([query_s, pairs_s, out_s, pair_s, gains])
    attn_s = Fold(jnp.concatenate([pairs_s.sum, query_s.sum], axis=2), 16)
    out_s = Fold(out_s.sum, 8, last=True)
    gains = gains.value + gains.came
    asked = [Move(gains, m) for m in (FIRST, SECOND, FIRST | SECOND)]
    slots.run([attn_s, out_s, *asked])
    gains = (gains + asked[0].came) + (asked[1].came + asked[2].came)
    attn_s = Fold(attn_s.sum, 8, last=True)
    asked = [Move(gains, m) for m in (8, 16, 24)]
    slots.run([attn_s, *asked])
    gains = (gains + asked[0].came) + (asked[1].came + asked[2].came)
    return (
        output,
        d_tokens,
        gains[0],
        flat(attn_s.sum[:, 2 * KV :]),
        flat(attn_s.sum[:, :KV]),
        flat(attn_s.sum[:, KV : 2 * KV]),
        flat(out_s.sum),
        gains[1],
        flat(pair_s.sum[:, :FF]),
        flat(pair_s.sum[:, FF:]),
        down_s.sum.reshape(-1),
    )


def body_whole(
    tokens, segment_ids, positions, norm_attn, w_query, w_key, w_value, w_out,
    norm_ffn, w_gate, w_up, w_down, cotangent,
):
    seqs, block_len, _ = tokens.shape
    n_dev = lax.axis_size(AXES)
    rows = seqs * block_len
    score_scale = HEAD_DIM ** (-0.5)

    def whole(shard, columns):
        return lax.all_gather(shard, AXES, axis=0, tiled=True).reshape(-1, columns)

    query_weight = whole(w_query, ATTN)
    kv_weight = jnp.concatenate([whole(w_key, KV), whole(w_value, KV)], axis=1)
    out_weight = whole(w_out, D)
    gate_weight, up_weight = whole(w_gate, FF), whole(w_up, FF)
    down_weight = whole(w_down, D)
    inputs = tokens.astype(wide).reshape(rows, D)
    grad_out = cotangent.astype(wide).reshape(rows, D)
    scale_attn = rms_scale(inputs)
    normed_attn = (inputs * scale_attn * norm_attn).astype(low)
    cosine, sine = rope_tables(positions.reshape(rows))
    bias = key_bias(ctx_gather(segment_ids), segment_ids, lax.axis_index("ctx"), ctx_masks())
    pairs_t = contract(kv_weight, normed_attn, 0, 1)
    pairs_t = jnp.concatenate(
        [rotate(pairs_t[:KV], cosine, sine).astype(low), pairs_t[KV:].astype(low)], axis=0
    )
    pairs_all = ctx_gather(pairs_t)
    query_t = contract(query_weight, normed_attn, 0, 1)
    query_t = (rotate(query_t, cosine, sine) * score_scale).astype(low)
    mixed, logs = zip(*[attend(query_t, pairs_all, bias, seq) for seq in range(seqs)])
    attended = jnp.concatenate([m.T for m in mixed], axis=0)
    resid = inputs + product(attended, out_weight)
    scale_ffn = rms_scale(resid)
    normed_ffn = (resid * scale_ffn * norm_ffn).astype(low)
    gate, up = product(normed_ffn, gate_weight), product(normed_ffn, up_weight)
    sigmoid, hidden = silu_parts(gate, up)
    output = (resid + product(hidden, down_weight)).astype(low).reshape(seqs, block_len, D)
    down_grad = cotangent.reshape(rows, D)
    gate_grad, up_grad = silu_back(product_right(down_grad, down_weight), gate, up, sigmoid)
    normed_grad = product_right(gate_grad, gate_weight) + product_right(up_grad, up_weight)
    resid_grad, ffn_gain_grad = norm_back(resid, scale_ffn, norm_ffn, normed_grad)
    resid_grad = resid_grad + grad_out
    branch_grad = resid_grad.astype(low)
    grad_t = product_right(branch_grad, out_weight).astype(low).T
    back = [
        attend_back(query_t, pairs_all, bias, mixed[seq], logs[seq], grad_t, seq)
        for seq in range(seqs)
    ]
    pairs_grad = ctx_scatter(jnp.concatenate([b[1] for b in back], axis=2))
    query_low = jnp.concatenate([b[0] for b in back], axis=1)
    query_low = rotate_back(query_low * score_scale, cosine, sine).astype(low)
    pairs_low = jnp.concatenate(
        [rotate_back(pairs_grad[:KV], cosine, sine).astype(low), pairs_grad[KV:].astype(low)],
        axis=0,
    )
    normed_grad = contract(query_low, query_weight, 0, 1) + contract(pairs_low, kv_weight, 0, 1)
    input_grad, attn_gain_grad = norm_back(inputs, scale_attn, norm_attn, normed_grad)
    d_tokens = (input_grad + resid_grad).reshape(seqs, block_len, D)

    def finish(left, right, right_dim):
        grad = contract(left, right, 0, right_dim).astype(low).reshape(n_dev, -1)
        grad = lax.psum_scatter(grad, AXES, scatter_dimension=0, tiled=True)
        return grad.astype(wide).reshape(-1)

    attn_gain_sum, ffn_gain_sum = lax.psum((attn_gain_grad, ffn_gain_grad), AXES)
    return (
        output,
        d_tokens,
        attn_gain_sum,
        finish(normed_attn, query_low, 1),
        finish(normed_attn, pairs_low[:KV], 1),
        finish(normed_attn, pairs_low[KV:], 1),
        finish(attended, branch_grad, 0),
        ffn_gain_sum,
        finish(normed_ffn, gate_grad, 0),
        finish(normed_ffn, up_grad, 0),
        finish(hidden, down_grad, 0),
    )


def solution(mesh):
    sizes = dict(mesh.shape)
    blocked = sizes["dp"] == 8 and sizes["ctx"] == 4
    body = body_blocked if blocked else body_whole
    one = P(AXES)
    tok = P("dp", "ctx", None)
    ids = P("dp", "ctx")
    in_specs = (tok, ids, ids, P(), one, one, one, one, P(), one, one, one, tok)
    out_specs = (tok, tok, P(), one, one, one, one, P(), one, one, one)
    return jax.shard_map(body, mesh=mesh, in_specs=in_specs, out_specs=out_specs, check_vma=False)
```

```python
import functools

import jax
import jax.numpy as jnp
from jax import lax
from jax.experimental import pallas as pl
from jax.experimental.pallas import tpu as pltpu
from jax.sharding import PartitionSpec as P

D = 960
HEADS = 15
KV_HEADS = 5
HEAD_DIM = 64
FF = 2560
GROUP = HEADS // KV_HEADS
ATTN = HEADS * HEAD_DIM
KV = KV_HEADS * HEAD_DIM
AXES = ("dp", "ctx")
CORE, FIRST, SECOND = 1, 2, 4

norm_eps = 1e-05
rope_base = 100000.0
mask_fill = -1000000000.0
low = jnp.bfloat16
wide = jnp.float32


def rms_scale(values):
    return lax.rsqrt(jnp.mean(values * values, axis=-1, keepdims=True) + norm_eps)


def norm_back(values, scale, gain, grad):
    gain_grad = jnp.sum(grad * values * scale, axis=0)
    weighted = grad * gain
    inner = jnp.mean(weighted * values, axis=-1, keepdims=True)
    return (scale * weighted - values * (scale * scale * scale) * inner, gain_grad)


def rope_tables(position):
    freqs = rope_base ** (-jnp.arange(0, HEAD_DIM, 2, dtype=wide) / HEAD_DIM)
    angles = freqs[:, None] * position.astype(wide)[None, :]
    angles = jnp.concatenate([angles, angles], axis=0)
    return jnp.cos(angles), jnp.sin(angles)


def by_head(values):
    return values.reshape(-1, HEAD_DIM, values.shape[-1])


def rotate(values, cosine, sine):
    values = by_head(values)
    half = HEAD_DIM // 2
    turned = jnp.concatenate([-values[:, half:], values[:, :half]], axis=1)
    return (values * cosine + turned * sine).reshape(-1, values.shape[-1])


def rotate_back(grad, cosine, sine):
    grad = by_head(grad)
    half = HEAD_DIM // 2
    scaled = grad * sine
    turned = jnp.concatenate([scaled[:, half:], -scaled[:, :half]], axis=1)
    return (grad * cosine + turned).reshape(-1, grad.shape[-1])


def product(left, right):
    return jnp.dot(left, right, preferred_element_type=wide)


def product_left(left, right):
    return lax.dot_general(left, right, (((0,), (0,)), ((), ())), preferred_element_type=wide)


def product_right(left, right):
    return lax.dot_general(left, right, (((1,), (1,)), ((), ())), preferred_element_type=wide)


def swap(value, mask):
    n = lax.axis_size(AXES)
    return lax.ppermute(value, AXES, [(i, i ^ mask) for i in range(n)])


def add_low(left, right):
    return (left.astype(wide) + right.astype(wide)).astype(low)


def far_masks():
    n = lax.axis_size(AXES)
    masks, m = [], 8
    while m < n:
        masks.append(m)
        m *= 2
    return masks


def block_owner(place):
    far = far_masks()
    owner = jnp.zeros_like(place)
    for bit, mask in enumerate(far + [SECOND, FIRST, CORE]):
        owner = owner | (((place >> bit) & 1) * mask)
    return owner


class Slots:
    def __init__(self):
        self.deps = ()

    def after(self, value):
        return lax.optimization_barrier((value, self.deps))[0]

    def hold(self, *values):
        self.deps = self.deps + values

    def run(self, moves, late=()):
        before, self.deps = self.deps, ()
        for i, move in enumerate((*moves, *late)):
            value = move.give()
            if before:
                value = lax.optimization_barrier((value, before))[0]
            came = swap(value, move.mask)
            if i < len(moves):
                self.deps += (came,)
            move.take(came)


class Move:
    def __init__(self, value, mask):
        self.value, self.mask = value, mask

    def give(self):
        return self.value

    def take(self, came):
        self.came = came


class Spread(Move):
    def take(self, came):
        self.came = came
        self.both = jnp.concatenate([self.value, came], axis=0)


class SpreadBetween(Spread):
    def __init__(self, first, mask):
        self.own, self.side = first.value, first.came
        super().__init__(first.both, mask)

    def take(self, came):
        n = came.shape[0] // 2
        self.both = jnp.concatenate([self.own, came[:n], self.side, came[n:]], axis=0)


class SpreadFirst(Spread):
    def take(self, came):
        self.came = came
        super().take(came)


class Fold(Move):
    def __init__(self, value, mask, last=False):
        self.n, self.last = value.shape[0] // 2, last
        super().__init__(value, mask)

    def give(self):
        return self.value[self.n :]

    def take(self, came):
        if self.last:
            self.sum = self.value[0].astype(wide) + came[0].astype(wide)
        else:
            self.sum = add_low(self.value[: self.n], came)


class FoldPair(Fold):
    def __init__(self, mine, theirs, mask):
        self.value, self.theirs, self.mask, self.last = mine, theirs, mask, False
        self.n = mine.shape[0]

    def give(self):
        return self.theirs


class FoldBetween(Fold):
    def give(self):
        q = self.n // 2
        return jnp.concatenate([self.value[q : self.n], self.value[self.n + q :]], axis=0)

    def take(self, came):
        q = self.n // 2
        kept = jnp.concatenate([self.value[:q], self.value[self.n : self.n + q]], axis=0)
        self.sum = add_low(kept, came)


def ctx_masks():
    m, masks = lax.axis_size("ctx") // 2, []
    while m >= 1:
        masks.append(m)
        m //= 2
    return masks


def ctx_gather(value):
    now = value[None]
    for mask in ctx_masks():
        now = jnp.concatenate([now, swap(now, mask)], axis=0)
    return now


def ctx_scatter(value):
    now = value
    for mask in ctx_masks()[::-1]:
        n = now.shape[0] // 2
        now = now[:n].astype(wide) + swap(now[n:], mask).astype(wide)
        if n > 1:
            now = now.astype(low)
    return now[0]


def whole_spec():
    return pl.BlockSpec(memory_space=pltpu.VMEM)


def join_blocks(tops, lows, order, low_rows):
    (a, b), (c, d) = tops, lows
    half, top, columns = a.shape
    rest = c.shape[1] - low_rows

    def kernel(order_ref, a_ref, b_ref, c_ref, d_ref, down_ref, out_ref):
        def step(p, _):
            near, far = order_ref[p], order_ref[p + half]
            down_ref[near, :top, :] = a_ref[p]
            down_ref[near, top:, :] = c_ref[p, :low_rows, :]
            down_ref[far, :top, :] = b_ref[p]
            down_ref[far, top:, :] = d_ref[p, :low_rows, :]
            out_ref[p] = c_ref[p, low_rows:, :]
            out_ref[p + half] = d_ref[p, low_rows:, :]
            return 0

        lax.fori_loop(0, half, step, 0)

    shape = (2 * half, top + low_rows, columns)
    return pl.pallas_call(
        kernel,
        out_shape=[
            jax.ShapeDtypeStruct(shape, a.dtype),
            jax.ShapeDtypeStruct((2 * half, rest, columns), a.dtype),
        ],
        in_specs=[pl.BlockSpec(memory_space=pltpu.SMEM)] + [whole_spec()] * 4,
        out_specs=[whole_spec()] * 2,
        compiler_params=pltpu.CompilerParams(vmem_limit_bytes=32 * 2**20),
        cost_estimate=pl.CostEstimate(flops=0, bytes_accessed=2**20, transcendentals=0),
        name="join_blocks",
    )(order, a, b, c, d)


def down_grad_blocks(hidden, grad, place, top):
    rows, hidden_width = hidden.shape
    columns = grad.shape[1]
    total = place.shape[0]
    tall = hidden_width // total
    group = 8

    def kernel(place_ref, h_ref, g_ref, a_ref, b_ref):
        value = product_left(h_ref[...], g_ref[...]).astype(low)
        first = pl.program_id(0) * group
        for b in range(group):
            to = place_ref[first + b]
            a_ref[to] = value[b * tall : b * tall + top]
            b_ref[to] = value[b * tall + top : (b + 1) * tall]

    return pl.pallas_call(
        kernel,
        grid=(total // group,),
        in_specs=[
            pl.BlockSpec(memory_space=pltpu.SMEM),
            pl.BlockSpec((rows, group * tall), lambda i: (0, i)),
            pl.BlockSpec((rows, columns), lambda i: (0, 0)),
        ],
        out_specs=[
            pl.BlockSpec((total, top, columns), lambda i: (0, 0, 0)),
            pl.BlockSpec((total, tall - top, columns), lambda i: (0, 0, 0)),
        ],
        out_shape=[
            jax.ShapeDtypeStruct((total, top, columns), low),
            jax.ShapeDtypeStruct((total, tall - top, columns), low),
        ],
        compiler_params=pltpu.CompilerParams(vmem_limit_bytes=32 * 2**20),
        cost_estimate=pl.CostEstimate(
            flops=2 * rows * hidden_width * columns,
            bytes_accessed=2 * (rows * (hidden_width + columns) + hidden_width * columns),
            transcendentals=0,
        ),
        name="down_grad_blocks",
    )(place, hidden, grad)


def head_rows(ref, head):
    return ref[head * HEAD_DIM : (head + 1) * HEAD_DIM, :]


def key_blocks(kv_ref, start):
    blocks = [kv_ref[b, start : start + HEAD_DIM, :] for b in range(kv_ref.shape[0])]
    return jnp.concatenate(blocks, axis=1)


def turn(value):
    return value.astype(wide).T.astype(low)


def attend_kernel(q_ref, kv_ref, bias_ref, o_ref, lse_ref):
    for g in range(KV_HEADS):
        keys = turn(key_blocks(kv_ref, g * HEAD_DIM))
        values_t = key_blocks(kv_ref, KV + g * HEAD_DIM)
        for h in range(g * GROUP, (g + 1) * GROUP):
            scores = product(keys, head_rows(q_ref, h)) + bias_ref[0]
            top = jnp.max(scores, axis=0, keepdims=True)
            weight = jnp.exp(scores - top)
            total = jnp.sum(weight, axis=0, keepdims=True)
            mixed = product(values_t, weight.astype(low)) / total
            o_ref[h * HEAD_DIM : (h + 1) * HEAD_DIM, :] = mixed.astype(low)
            lse_ref[0, h : h + 1, :] = top + jnp.log(total)


def attend_back_kernel(q_ref, kv_ref, bias_ref, o_ref, lse_ref, do_ref, dq_ref, dkv_ref):
    width = q_ref.shape[1]
    for g in range(KV_HEADS):
        keys_t = key_blocks(kv_ref, g * HEAD_DIM)
        keys = turn(keys_t)
        values = turn(key_blocks(kv_ref, KV + g * HEAD_DIM))
        key_grad, value_grad = None, None
        for h in range(g * GROUP, (g + 1) * GROUP):
            query, grad = head_rows(q_ref, h), head_rows(do_ref, h)
            scores = product(keys, query) + bias_ref[0]
            probs = jnp.exp(scores - lse_ref[0, h : h + 1, :])
            inner = jnp.sum(
                grad.astype(wide) * head_rows(o_ref, h).astype(wide), axis=0, keepdims=True
            )
            scores_grad = (probs * (product(values, grad) - inner)).astype(low)
            dq_ref[h * HEAD_DIM : (h + 1) * HEAD_DIM, :] = product(keys_t, scores_grad)
            from_keys = product_right(scores_grad, query)
            from_values = product_right(probs.astype(low), grad)
            key_grad = from_keys if key_grad is None else key_grad + from_keys
            value_grad = from_values if value_grad is None else value_grad + from_values
        for start, value in ((g * HEAD_DIM, key_grad), (KV + g * HEAD_DIM, value_grad)):
            turned = value.T.astype(low)
            for b in range(kv_ref.shape[0]):
                dkv_ref[b, start : start + HEAD_DIM, :] = turned[:, b * width : (b + 1) * width]


def attention_specs(blocks, block_len, length, seq):
    columns = pl.BlockSpec((ATTN, block_len), lambda i: (0, seq))
    pairs = pl.BlockSpec((blocks, 2 * KV, block_len), lambda i: (0, 0, seq))
    bias = pl.BlockSpec((1, length, block_len), lambda i: (seq, 0, 0))
    own = pl.BlockSpec((ATTN, block_len), lambda i: (0, 0))
    own_pairs = pl.BlockSpec((blocks, 2 * KV, block_len), lambda i: (0, 0, 0))
    logs = pl.BlockSpec((1, HEADS, block_len), lambda i: (0, 0, 0))
    return columns, pairs, bias, own, own_pairs, logs


def attend(query_t, pairs_t, bias, seq):
    _, length, block_len = bias.shape
    columns, pairs, bias_spec, own, _, logs = attention_specs(
        pairs_t.shape[0], block_len, length, seq
    )
    work = HEADS * length * block_len
    return pl.pallas_call(
        attend_kernel,
        grid=(1,),
        in_specs=[columns, pairs, bias_spec],
        out_specs=[own, logs],
        out_shape=[
            jax.ShapeDtypeStruct((ATTN, block_len), low),
            jax.ShapeDtypeStruct((1, HEADS, block_len), wide),
        ],
        compiler_params=pltpu.CompilerParams(vmem_limit_bytes=40 * 2**20),
        cost_estimate=pl.CostEstimate(
            flops=work, bytes_accessed=2**20, transcendentals=0
        ),
        name="attend",
    )(query_t, pairs_t, bias)


def attend_back(query_t, pairs_t, bias, mixed_t, logs_all, grad_t, seq):
    _, length, block_len = bias.shape
    columns, pairs, bias_spec, own, own_pairs, logs = attention_specs(
        pairs_t.shape[0], block_len, length, seq
    )
    work = HEADS * length * block_len
    return pl.pallas_call(
        attend_back_kernel,
        grid=(1,),
        in_specs=[columns, pairs, bias_spec, own, logs, columns],
        out_specs=[own, own_pairs],
        out_shape=[
            jax.ShapeDtypeStruct((ATTN, block_len), wide),
            jax.ShapeDtypeStruct((pairs_t.shape[0], 2 * KV, block_len), low),
        ],
        compiler_params=pltpu.CompilerParams(vmem_limit_bytes=48 * 2**20),
        cost_estimate=pl.CostEstimate(
            flops=work, bytes_accessed=2**20, transcendentals=0
        ),
        name="attend_back",
    )(query_t, pairs_t, bias, mixed_t, logs_all, grad_t)


def project_kernel(a_ref, q0_ref, q1_ref, p0_ref, p1_ref, cos_ref, sin_ref, q_ref, p_ref, *, scale):
    split = q0_ref.shape[0]
    half = HEAD_DIM // 2
    first, second = a_ref[:, :split], a_ref[:, split:]
    cosine, sine = cos_ref[...], sin_ref[...]

    def turned(value):
        upper, lower = value[half:], value[:half]
        return value * cosine + jnp.concatenate([-upper, lower], axis=0) * sine

    pairs = (product(first, p0_ref[...]) + product(second, p1_ref[...])).T
    for h in range(KV_HEADS):
        at = slice(h * HEAD_DIM, (h + 1) * HEAD_DIM)
        p_ref[at, :] = turned(pairs[at]).astype(low)
    p_ref[KV:, :] = pairs[KV:].astype(low)
    query = (product(first, q0_ref[...]) + product(second, q1_ref[...])).T
    for h in range(HEADS):
        at = slice(h * HEAD_DIM, (h + 1) * HEAD_DIM)
        q_ref[at, :] = (turned(query[at]) * scale).astype(low)


def project(normed, query_halves, pairs_halves, cosine, sine, scale):
    rows = normed.shape[0]
    halves = [h.reshape(-1, h.shape[-1]) for h in (*query_halves, *pairs_halves)]
    return pl.pallas_call(
        functools.partial(project_kernel, scale=scale),
        in_specs=[whole_spec()] * 7,
        out_specs=[whole_spec()] * 2,
        out_shape=[
            jax.ShapeDtypeStruct((ATTN, rows), low),
            jax.ShapeDtypeStruct((2 * KV, rows), low),
        ],
        compiler_params=pltpu.CompilerParams(vmem_limit_bytes=40 * 2**20),
        cost_estimate=pl.CostEstimate(flops=rows, bytes_accessed=2**20, transcendentals=0),
        name="project",
    )(normed, *halves, cosine, sine)


def key_bias(segment_all, segment_ids, ctx_here, masks):
    blocks, seqs, block_len = segment_all.shape
    place = jnp.arange(blocks, dtype=jnp.int32)
    owner = jnp.zeros_like(place)
    for bit, mask in enumerate(masks):
        owner = owner | (((place >> bit) & 1) * mask)
    inside = jnp.arange(block_len, dtype=jnp.int32)
    key_index = ((owner ^ ctx_here)[:, None] * block_len + inside[None, :]).reshape(-1)
    query_index = ctx_here * block_len + inside
    segments = segment_all.transpose(1, 0, 2).reshape(seqs, -1)
    allowed = (segments[:, :, None] == segment_ids[:, None, :]) & (
        key_index[None, :, None] <= query_index[None, None, :]
    )
    return jnp.where(allowed, 0.0, mask_fill)


def contract(left, right, left_dim, right_dim):
    return lax.dot_general(
        left, right, (((left_dim,), (right_dim,)), ((), ())), preferred_element_type=wide
    )


def silu_parts(gate, up):
    sigmoid = jax.nn.sigmoid(gate)
    return sigmoid, (gate * sigmoid * up).astype(low)


def silu_back(hidden_grad, gate, up, sigmoid):
    gate_grad = (hidden_grad * up * sigmoid * (1.0 + gate * (1.0 - sigmoid))).astype(low)
    return gate_grad, (hidden_grad * gate * sigmoid).astype(low)


def body_blocked(
    tokens, segment_ids, positions, norm_attn, w_query, w_key, w_value, w_out,
    norm_ffn, w_gate, w_up, w_down, cotangent,
):
    seqs, block_len, _ = tokens.shape
    n_dev = lax.axis_size(AXES)
    me, ctx_here = lax.axis_index(AXES), lax.axis_index("ctx")
    rows = seqs * block_len
    score_scale = HEAD_DIM ** (-0.5)
    cut, cut_ff = D // n_dev, FF // n_dev
    pad = -(-cut // 16) * 16
    top_ff = (cut_ff * 3 // 5) // 8 * 8
    low_ff = cut_ff - top_ff
    half = n_dev // 2
    split = half * pad
    slots = Slots()
    ahead = (seqs + 1) // 2

    def rows_of(shard, columns):
        return jnp.pad(shard.reshape(cut, columns), ((0, pad - cut), (0, 0)))

    def weight(move):
        return move.both.reshape(-1, move.both.shape[-1])

    attn_block = jnp.concatenate(
        [rows_of(w_key, KV), rows_of(w_value, KV), rows_of(w_query, ATTN)], axis=1
    )[None]
    attn = Spread(attn_block, 8)
    slots.run([attn])
    mix_block = jnp.concatenate([w_down.reshape(cut_ff, D), rows_of(w_out, D)], axis=0)[None]
    mix = Spread(mix_block, 8)
    attn = Spread(attn.both, 16)
    seg_y = Move(slots.after(segment_ids), FIRST)
    inputs = slots.after(tokens).astype(wide).reshape(rows, D)
    slots.run([attn, mix], [seg_y])
    places = jnp.arange(n_dev, dtype=jnp.int32)
    order = block_owner(places) ^ me
    place = jnp.sum(jnp.where(order[:, None] == places[None, :], places[:, None], 0), axis=0)
    slot = jnp.arange(n_dev * pad, dtype=jnp.int32)
    source = jnp.where(slot % pad < cut, jnp.repeat(order, pad) * cut + slot % pad, -1)
    perm = (jnp.arange(D, dtype=jnp.int32)[:, None] == source[None, :]).astype(low)
    scale_attn = rms_scale(inputs)
    normed_attn = product((inputs * scale_attn * norm_attn).astype(low), perm).astype(low)
    segments = jnp.stack([segment_ids, seg_y.came])
    seg_c = Move(segments, CORE)
    pairs_w = SpreadFirst(attn.both[..., : 2 * KV], FIRST)
    query_w = Spread(attn.both[..., 2 * KV :], SECOND)
    mix = Spread(mix.both, 16)
    angles = slots.after(positions).reshape(rows)
    slots.run([pairs_w, query_w], [mix, seg_c])
    cosine, sine = rope_tables(angles)
    segments = jnp.concatenate([segments, seg_c.came], axis=0)
    bias = key_bias(slots.after(segments), segment_ids, ctx_here, (2, 1))
    slots.hold(normed_attn)
    pairs_w = SpreadBetween(pairs_w, SECOND)
    query_w = Spread(query_w.both, FIRST)
    pair_block = jnp.concatenate([rows_of(w_gate, FF), rows_of(w_up, FF)], axis=1)[None]
    pair = Spread(pair_block, 8)
    slots.run([pairs_w, query_w], [pair])
    slots.hold(cosine, sine)
    pairs_w, query_w = Spread(pairs_w.both, CORE), Spread(query_w.both, CORE)
    top_w, low_w = Spread(mix.both[:, :top_ff], SECOND), SpreadFirst(mix.both[:, top_ff:], FIRST)
    gate_w = Spread(pair.both[..., :FF], 16)
    slots.run([pairs_w, query_w, top_w, low_w], [gate_w])
    query_weight, kv_weight = weight(query_w), weight(pairs_w)
    query_t, pairs_t = project(
        normed_attn,
        (query_w.value, query_w.came),
        (pairs_w.value, pairs_w.came),
        cosine,
        sine,
        score_scale,
    )
    top_w, low_w = Spread(top_w.both, FIRST), SpreadBetween(low_w, SECOND)
    slots.run([], [top_w, low_w])
    pairs_all = Spread(pairs_t[None], FIRST)
    up_w = Spread(pair.both[..., FF:], 16)
    gate_w = Spread(gate_w.both, SECOND)
    slots.hold(bias, query_t)
    slots.run([pairs_all], [up_w, gate_w])
    pairs_all = Spread(pairs_all.both, CORE)
    up_w = SpreadFirst(up_w.both, FIRST)
    top_core = Move(top_w.both, CORE)
    low_core = Move(low_w.both, CORE)
    slots.run([pairs_all], [up_w, top_core, low_core])
    pairs_all = pairs_all.both
    mixed, logs = [None] * seqs, [None] * seqs
    for seq in range(ahead):
        mixed[seq], logs[seq] = attend(query_t, pairs_all, bias, seq)
    gate_w, up_w = Spread(gate_w.both, FIRST), SpreadBetween(up_w, SECOND)
    slots.hold(*mixed[:ahead], up_w.side)
    query_t = slots.after(query_t)
    slots.run([], [gate_w, up_w])
    for seq in range(ahead, seqs):
        mixed[seq], logs[seq] = attend(query_t, pairs_all, bias, seq)
    down_weight, out_weight = join_blocks(
        (top_w.both, top_core.came), (low_w.both, low_core.came), order, low_ff
    )
    down_weight, out_weight = down_weight.reshape(FF, D), out_weight.reshape(-1, D)
    down_grad = cotangent.reshape(rows, D)
    hidden_grad = product_right(down_grad, down_weight)
    gate_w, up_w = Spread(gate_w.both, CORE), Spread(up_w.both, CORE)
    slots.run([gate_w, up_w])
    attended = jnp.concatenate([contract(m, perm, 0, 0).astype(low) for m in mixed], axis=0)
    resid = inputs + product(attended, out_weight)
    scale_ffn = rms_scale(resid)
    normed_ffn = product((resid * scale_ffn * norm_ffn).astype(low), perm).astype(low)
    gate_weight, up_weight = weight(gate_w), weight(up_w)
    gate, up = product(normed_ffn, gate_weight), product(normed_ffn, up_weight)
    sigmoid, hidden = silu_parts(gate, up)
    top_grad, low_grad = down_grad_blocks(hidden, down_grad, place, top_ff)

    def halves(left, right, right_dim):
        both = []
        for piece in (left[:, :split], left[:, split:]):
            grad = contract(piece, right, 0, right_dim).astype(low)
            both.append(grad.reshape(half, pad, -1))
        return FoldPair(*both, CORE)

    def flat(grad):
        return grad[:cut].reshape(-1)

    def collect_wide(value):
        high = lax.reduce_precision(value, 8, 7)
        return product_right(high.astype(low), perm) + product_right(
            (value - high).astype(low), perm
        )

    top_s = FoldPair(top_grad[:half], top_grad[half:], CORE)
    low_s = FoldPair(low_grad[:half], low_grad[half:], CORE)
    slots.run([top_s, low_s])
    gate_grad, up_grad = silu_back(hidden_grad, gate, up, sigmoid)
    slots.hold(gate_grad, up_grad)
    top_s, low_s = Fold(top_s.sum, FIRST), FoldBetween(low_s.sum, SECOND)
    slots.run([top_s, low_s])
    gate_s, up_s = halves(normed_ffn, gate_grad, 0), halves(normed_ffn, up_grad, 0)
    top_s, low_s = Fold(top_s.sum, SECOND), Fold(low_s.sum, FIRST)
    slots.run([gate_s, up_s, top_s, low_s])
    normed_grad = product_right(gate_grad, gate_weight) + product_right(up_grad, up_weight)
    normed_grad = collect_wide(normed_grad)
    grad_out = cotangent.astype(wide).reshape(rows, D)
    resid_grad, ffn_gain_grad = norm_back(resid, scale_ffn, norm_ffn, normed_grad)
    resid_grad = resid_grad + grad_out
    branch_grad = resid_grad.astype(low)
    grad_t = product_right(perm, product_right(branch_grad, out_weight).astype(low)).astype(low)
    gate_s, up_s = Fold(gate_s.sum, FIRST), FoldBetween(up_s.sum, SECOND)
    down_s = Fold(jnp.concatenate([top_s.sum, low_s.sum], axis=1), 16)
    grad_t = slots.after(grad_t)
    slots.run([gate_s, up_s], [down_s])
    back = [
        attend_back(query_t, pairs_all, bias, mixed[seq], logs[seq], grad_t, seq)
        for seq in range(seqs)
    ]
    out_s = halves(attended, branch_grad, 0)
    pairs_part = jnp.concatenate([b[1] for b in back], axis=2)
    pairs_s = FoldPair(pairs_part[:2], pairs_part[2:], CORE)
    gate_s, up_s = Fold(gate_s.sum, SECOND), Fold(up_s.sum, FIRST)
    down_s = Fold(down_s.sum, 8, last=True)
    slots.run([pairs_s], [gate_s, up_s, down_s, out_s])
    pairs_s = Fold(pairs_s.sum, FIRST, last=True)
    gate_s, up_s = Fold(gate_s.sum, 16), Fold(up_s.sum, 16)
    query_low = jnp.concatenate([b[0] for b in back], axis=1)
    query_low = rotate_back(query_low * score_scale, cosine, sine).astype(low)
    query_s = halves(normed_attn, query_low, 1)
    out_s = FoldBetween(out_s.sum, SECOND)
    slots.hold(query_s.value)
    slots.run([pairs_s, query_s], [gate_s, out_s])
    query_s, out_s = Fold(query_s.sum, FIRST), Fold(out_s.sum, FIRST)
    slots.run([], [query_s, out_s, up_s])
    pairs_grad = pairs_s.sum
    pairs_low = jnp.concatenate(
        [rotate_back(pairs_grad[:KV], cosine, sine).astype(low), pairs_grad[KV:].astype(low)],
        axis=0,
    )
    pairs_s = halves(normed_attn, pairs_low, 1)
    slots.run([pairs_s])
    attn_normed_grad = collect_wide(
        contract(query_low, query_weight, 0, 1) + contract(pairs_low, kv_weight, 0, 1)
    )
    input_grad, attn_gain_grad = norm_back(inputs, scale_attn, norm_attn, attn_normed_grad)
    d_tokens = (input_grad + resid_grad).reshape(seqs, block_len, D)
    output = (resid + product(slots.after(hidden), down_weight)).astype(low)
    output = output.reshape(seqs, block_len, D)
    query_s = Fold(query_s.sum, SECOND)
    pairs_s = FoldBetween(pairs_s.sum, SECOND)
    gate_s = Fold(gate_s.sum, 8, last=True)
    slots.run([pairs_s], [query_s, gate_s])
    attn_s = Fold(jnp.concatenate([query_s.sum, out_s.sum], axis=2), 16)
    pairs_s = Fold(pairs_s.sum, FIRST)
    up_s = Fold(up_s.sum, 8, last=True)
    gains = Move(jnp.stack([attn_gain_grad, ffn_gain_grad]), CORE)
    slots.run([pairs_s, attn_s, gains], [up_s])
    attn_s = Fold(attn_s.sum, 8, last=True)
    pairs_s = Fold(pairs_s.sum, 16)
    gains = gains.value + gains.came
    asked = [Move(gains, m) for m in (FIRST, SECOND, FIRST | SECOND)]
    slots.run([pairs_s, attn_s, *asked])
    gains = (gains + asked[0].came) + (asked[1].came + asked[2].came)
    pairs_s = Fold(pairs_s.sum, 8, last=True)
    asked = [Move(gains, m) for m in (8, 16, 24)]
    slots.run([pairs_s, *asked])
    gains = (gains + asked[0].came) + (asked[1].came + asked[2].came)
    return (
        output,
        d_tokens,
        gains[0],
        flat(attn_s.sum[:, :ATTN]),
        flat(pairs_s.sum[:, :KV]),
        flat(pairs_s.sum[:, KV:]),
        flat(attn_s.sum[:, ATTN:]),
        gains[1],
        flat(gate_s.sum),
        flat(up_s.sum),
        down_s.sum.reshape(-1),
    )


def body_whole(
    tokens, segment_ids, positions, norm_attn, w_query, w_key, w_value, w_out,
    norm_ffn, w_gate, w_up, w_down, cotangent,
):
    seqs, block_len, _ = tokens.shape
    n_dev = lax.axis_size(AXES)
    rows = seqs * block_len
    score_scale = HEAD_DIM ** (-0.5)

    def whole(shard, columns):
        return lax.all_gather(shard, AXES, axis=0, tiled=True).reshape(-1, columns)

    query_weight = whole(w_query, ATTN)
    kv_weight = jnp.concatenate([whole(w_key, KV), whole(w_value, KV)], axis=1)
    out_weight = whole(w_out, D)
    gate_weight, up_weight = whole(w_gate, FF), whole(w_up, FF)
    down_weight = whole(w_down, D)
    inputs = tokens.astype(wide).reshape(rows, D)
    grad_out = cotangent.astype(wide).reshape(rows, D)
    scale_attn = rms_scale(inputs)
    normed_attn = (inputs * scale_attn * norm_attn).astype(low)
    cosine, sine = rope_tables(positions.reshape(rows))
    bias = key_bias(ctx_gather(segment_ids), segment_ids, lax.axis_index("ctx"), ctx_masks())
    pairs_t = contract(kv_weight, normed_attn, 0, 1)
    pairs_t = jnp.concatenate(
        [rotate(pairs_t[:KV], cosine, sine).astype(low), pairs_t[KV:].astype(low)], axis=0
    )
    pairs_all = ctx_gather(pairs_t)
    query_t = contract(query_weight, normed_attn, 0, 1)
    query_t = (rotate(query_t, cosine, sine) * score_scale).astype(low)
    mixed, logs = zip(*[attend(query_t, pairs_all, bias, seq) for seq in range(seqs)])
    attended = jnp.concatenate([m.T for m in mixed], axis=0)
    resid = inputs + product(attended, out_weight)
    scale_ffn = rms_scale(resid)
    normed_ffn = (resid * scale_ffn * norm_ffn).astype(low)
    gate, up = product(normed_ffn, gate_weight), product(normed_ffn, up_weight)
    sigmoid, hidden = silu_parts(gate, up)
    output = (resid + product(hidden, down_weight)).astype(low).reshape(seqs, block_len, D)
    down_grad = cotangent.reshape(rows, D)
    gate_grad, up_grad = silu_back(product_right(down_grad, down_weight), gate, up, sigmoid)
    normed_grad = product_right(gate_grad, gate_weight) + product_right(up_grad, up_weight)
    resid_grad, ffn_gain_grad = norm_back(resid, scale_ffn, norm_ffn, normed_grad)
    resid_grad = resid_grad + grad_out
    branch_grad = resid_grad.astype(low)
    grad_t = product_right(branch_grad, out_weight).astype(low).T
    back = [
        attend_back(query_t, pairs_all, bias, mixed[seq], logs[seq], grad_t, seq)
        for seq in range(seqs)
    ]
    pairs_grad = ctx_scatter(jnp.concatenate([b[1] for b in back], axis=2))
    query_low = jnp.concatenate([b[0] for b in back], axis=1)
    query_low = rotate_back(query_low * score_scale, cosine, sine).astype(low)
    pairs_low = jnp.concatenate(
        [rotate_back(pairs_grad[:KV], cosine, sine).astype(low), pairs_grad[KV:].astype(low)],
        axis=0,
    )
    normed_grad = contract(query_low, query_weight, 0, 1) + contract(pairs_low, kv_weight, 0, 1)
    input_grad, attn_gain_grad = norm_back(inputs, scale_attn, norm_attn, normed_grad)
    d_tokens = (input_grad + resid_grad).reshape(seqs, block_len, D)

    def finish(left, right, right_dim):
        grad = contract(left, right, 0, right_dim).astype(low).reshape(n_dev, -1)
        grad = lax.psum_scatter(grad, AXES, scatter_dimension=0, tiled=True)
        return grad.astype(wide).reshape(-1)

    attn_gain_sum, ffn_gain_sum = lax.psum((attn_gain_grad, ffn_gain_grad), AXES)
    return (
        output,
        d_tokens,
        attn_gain_sum,
        finish(normed_attn, query_low, 1),
        finish(normed_attn, pairs_low[:KV], 1),
        finish(normed_attn, pairs_low[KV:], 1),
        finish(attended, branch_grad, 0),
        ffn_gain_sum,
        finish(normed_ffn, gate_grad, 0),
        finish(normed_ffn, up_grad, 0),
        finish(hidden, down_grad, 0),
    )


def solution(mesh):
    sizes = dict(mesh.shape)
    blocked = sizes["dp"] == 8 and sizes["ctx"] == 4
    body = body_blocked if blocked else body_whole
    one = P(AXES)
    tok = P("dp", "ctx", None)
    ids = P("dp", "ctx")
    in_specs = (tok, ids, ids, P(), one, one, one, one, P(), one, one, one, tok)
    out_specs = (tok, tok, P(), one, one, one, one, P(), one, one, one)
    return jax.shard_map(body, mesh=mesh, in_specs=in_specs, out_specs=out_specs, check_vma=False)
```

```python
import functools

import jax
import jax.numpy as jnp
from jax import lax
from jax.experimental import pallas as pl
from jax.experimental.pallas import tpu as pltpu
from jax.sharding import PartitionSpec as P

D = 960
HEADS = 15
KV_HEADS = 5
HEAD_DIM = 64
FF = 2560
GROUP = HEADS // KV_HEADS
ATTN = HEADS * HEAD_DIM
KV = KV_HEADS * HEAD_DIM
AXES = ("dp", "ctx")
CORE, FIRST, SECOND = 1, 2, 4

norm_eps = 1e-05
rope_base = 100000.0
mask_fill = -1000000000.0
low = jnp.bfloat16
wide = jnp.float32


def rms_scale(values):
    return lax.rsqrt(jnp.mean(values * values, axis=-1, keepdims=True) + norm_eps)


def norm_back(values, scale, gain, grad):
    gain_grad = jnp.sum(grad * values * scale, axis=0)
    weighted = grad * gain
    inner = jnp.mean(weighted * values, axis=-1, keepdims=True)
    return (scale * weighted - values * (scale * scale * scale) * inner, gain_grad)


def rope_tables(position):
    freqs = rope_base ** (-jnp.arange(0, HEAD_DIM, 2, dtype=wide) / HEAD_DIM)
    angles = freqs[:, None] * position.astype(wide)[None, :]
    angles = jnp.concatenate([angles, angles], axis=0)
    return jnp.cos(angles), jnp.sin(angles)


def by_head(values):
    return values.reshape(-1, HEAD_DIM, values.shape[-1])


def rotate(values, cosine, sine):
    values = by_head(values)
    half = HEAD_DIM // 2
    turned = jnp.concatenate([-values[:, half:], values[:, :half]], axis=1)
    return (values * cosine + turned * sine).reshape(-1, values.shape[-1])


def rotate_back(grad, cosine, sine):
    grad = by_head(grad)
    half = HEAD_DIM // 2
    scaled = grad * sine
    turned = jnp.concatenate([scaled[:, half:], -scaled[:, :half]], axis=1)
    return (grad * cosine + turned).reshape(-1, grad.shape[-1])


def product(left, right):
    return jnp.dot(left, right, preferred_element_type=wide)


def product_left(left, right):
    return lax.dot_general(left, right, (((0,), (0,)), ((), ())), preferred_element_type=wide)


def product_right(left, right):
    return lax.dot_general(left, right, (((1,), (1,)), ((), ())), preferred_element_type=wide)


def swap(value, mask):
    n = lax.axis_size(AXES)
    return lax.ppermute(value, AXES, [(i, i ^ mask) for i in range(n)])


def add_low(left, right):
    return (left.astype(wide) + right.astype(wide)).astype(low)


def far_masks():
    n = lax.axis_size(AXES)
    masks, m = [], 8
    while m < n:
        masks.append(m)
        m *= 2
    return masks


def block_owner(place):
    far = far_masks()
    owner = jnp.zeros_like(place)
    for bit, mask in enumerate(far + [SECOND, FIRST, CORE]):
        owner = owner | (((place >> bit) & 1) * mask)
    return owner


class Slots:
    def __init__(self):
        self.deps = ()

    def after(self, value):
        return lax.optimization_barrier((value, self.deps))[0]

    def hold(self, *values):
        self.deps = self.deps + values

    def run(self, moves, late=()):
        before, self.deps = self.deps, ()
        for i, move in enumerate((*moves, *late)):
            value = move.give()
            if before:
                value = lax.optimization_barrier((value, before))[0]
            came = swap(value, move.mask)
            if i < len(moves):
                self.deps += (came,)
            move.take(came)


class Move:
    def __init__(self, value, mask):
        self.value, self.mask = value, mask

    def give(self):
        return self.value

    def take(self, came):
        self.came = came


class Spread(Move):
    def take(self, came):
        self.came = came
        self.both = jnp.concatenate([self.value, came], axis=0)


class SpreadBetween(Spread):
    def __init__(self, first, mask):
        self.own, self.side = first.value, first.came
        super().__init__(first.both, mask)

    def take(self, came):
        n = came.shape[0] // 2
        self.both = jnp.concatenate([self.own, came[:n], self.side, came[n:]], axis=0)


class SpreadFirst(Spread):
    def take(self, came):
        self.came = came
        super().take(came)


class Fold(Move):
    def __init__(self, value, mask, last=False):
        self.n, self.last = value.shape[0] // 2, last
        super().__init__(value, mask)

    def give(self):
        return self.value[self.n :]

    def take(self, came):
        if self.last:
            self.sum = self.value[0].astype(wide) + came[0].astype(wide)
        else:
            self.sum = add_low(self.value[: self.n], came)


class FoldPair(Fold):
    def __init__(self, mine, theirs, mask):
        self.value, self.theirs, self.mask, self.last = mine, theirs, mask, False
        self.n = mine.shape[0]

    def give(self):
        return self.theirs


class FoldBetween(Fold):
    def give(self):
        q = self.n // 2
        return jnp.concatenate([self.value[q : self.n], self.value[self.n + q :]], axis=0)

    def take(self, came):
        q = self.n // 2
        kept = jnp.concatenate([self.value[:q], self.value[self.n : self.n + q]], axis=0)
        self.sum = add_low(kept, came)


def ctx_masks():
    m, masks = lax.axis_size("ctx") // 2, []
    while m >= 1:
        masks.append(m)
        m //= 2
    return masks


def ctx_gather(value):
    now = value[None]
    for mask in ctx_masks():
        now = jnp.concatenate([now, swap(now, mask)], axis=0)
    return now


def ctx_scatter(value):
    now = value
    for mask in ctx_masks()[::-1]:
        n = now.shape[0] // 2
        now = now[:n].astype(wide) + swap(now[n:], mask).astype(wide)
        if n > 1:
            now = now.astype(low)
    return now[0]


def whole_spec():
    return pl.BlockSpec(memory_space=pltpu.VMEM)


def join_blocks(tops, lows, order, low_rows):
    (a, b), (c, d) = tops, lows
    half, top, columns = a.shape
    rest = c.shape[1] - low_rows

    def kernel(order_ref, a_ref, b_ref, c_ref, d_ref, down_ref, out_ref):
        def step(p, _):
            near, far = order_ref[p], order_ref[p + half]
            down_ref[near, :top, :] = a_ref[p]
            down_ref[near, top:, :] = c_ref[p, :low_rows, :]
            down_ref[far, :top, :] = b_ref[p]
            down_ref[far, top:, :] = d_ref[p, :low_rows, :]
            out_ref[p] = c_ref[p, low_rows:, :]
            out_ref[p + half] = d_ref[p, low_rows:, :]
            return 0

        lax.fori_loop(0, half, step, 0)

    shape = (2 * half, top + low_rows, columns)
    return pl.pallas_call(
        kernel,
        out_shape=[
            jax.ShapeDtypeStruct(shape, a.dtype),
            jax.ShapeDtypeStruct((2 * half, rest, columns), a.dtype),
        ],
        in_specs=[pl.BlockSpec(memory_space=pltpu.SMEM)] + [whole_spec()] * 4,
        out_specs=[whole_spec()] * 2,
        compiler_params=pltpu.CompilerParams(vmem_limit_bytes=32 * 2**20),
        cost_estimate=pl.CostEstimate(flops=0, bytes_accessed=2**20, transcendentals=0),
        name="join_blocks",
    )(order, a, b, c, d)


def down_grad_blocks(hidden, grad, place, top):
    rows, hidden_width = hidden.shape
    columns = grad.shape[1]
    total = place.shape[0]
    tall = hidden_width // total
    group = 8

    def kernel(place_ref, h_ref, g_ref, a_ref, b_ref):
        value = product_left(h_ref[...], g_ref[...]).astype(low)
        first = pl.program_id(0) * group
        for b in range(group):
            to = place_ref[first + b]
            a_ref[to] = value[b * tall : b * tall + top]
            b_ref[to] = value[b * tall + top : (b + 1) * tall]

    return pl.pallas_call(
        kernel,
        grid=(total // group,),
        in_specs=[
            pl.BlockSpec(memory_space=pltpu.SMEM),
            pl.BlockSpec((rows, group * tall), lambda i: (0, i)),
            pl.BlockSpec((rows, columns), lambda i: (0, 0)),
        ],
        out_specs=[
            pl.BlockSpec((total, top, columns), lambda i: (0, 0, 0)),
            pl.BlockSpec((total, tall - top, columns), lambda i: (0, 0, 0)),
        ],
        out_shape=[
            jax.ShapeDtypeStruct((total, top, columns), low),
            jax.ShapeDtypeStruct((total, tall - top, columns), low),
        ],
        compiler_params=pltpu.CompilerParams(vmem_limit_bytes=32 * 2**20),
        cost_estimate=pl.CostEstimate(
            flops=2 * rows * hidden_width * columns,
            bytes_accessed=2 * (rows * (hidden_width + columns) + hidden_width * columns),
            transcendentals=0,
        ),
        name="down_grad_blocks",
    )(place, hidden, grad)


def head_rows(ref, head):
    return ref[head * HEAD_DIM : (head + 1) * HEAD_DIM, :]


def key_blocks(kv_ref, start):
    blocks = [kv_ref[b, start : start + HEAD_DIM, :] for b in range(kv_ref.shape[0])]
    return jnp.concatenate(blocks, axis=1)


def turn(value):
    return value.astype(wide).T.astype(low)


def attend_kernel(q_ref, kv_ref, bias_ref, o_ref, lse_ref):
    for g in range(KV_HEADS):
        keys = turn(key_blocks(kv_ref, g * HEAD_DIM))
        values_t = key_blocks(kv_ref, KV + g * HEAD_DIM)
        for h in range(g * GROUP, (g + 1) * GROUP):
            scores = product(keys, head_rows(q_ref, h)) + bias_ref[0]
            top = jnp.max(scores, axis=0, keepdims=True)
            weight = jnp.exp(scores - top)
            total = jnp.sum(weight, axis=0, keepdims=True)
            mixed = product(values_t, weight.astype(low)) / total
            o_ref[h * HEAD_DIM : (h + 1) * HEAD_DIM, :] = mixed.astype(low)
            lse_ref[0, h : h + 1, :] = top + jnp.log(total)


def attend_back_kernel(q_ref, kv_ref, bias_ref, o_ref, lse_ref, do_ref, dq_ref, dkv_ref):
    width = q_ref.shape[1]
    for g in range(KV_HEADS):
        keys_t = key_blocks(kv_ref, g * HEAD_DIM)
        keys = turn(keys_t)
        values = turn(key_blocks(kv_ref, KV + g * HEAD_DIM))
        key_grad, value_grad = None, None
        for h in range(g * GROUP, (g + 1) * GROUP):
            query, grad = head_rows(q_ref, h), head_rows(do_ref, h)
            scores = product(keys, query) + bias_ref[0]
            probs = jnp.exp(scores - lse_ref[0, h : h + 1, :])
            inner = jnp.sum(
                grad.astype(wide) * head_rows(o_ref, h).astype(wide), axis=0, keepdims=True
            )
            scores_grad = (probs * (product(values, grad) - inner)).astype(low)
            dq_ref[h * HEAD_DIM : (h + 1) * HEAD_DIM, :] = product(keys_t, scores_grad)
            from_keys = product_right(scores_grad, query)
            from_values = product_right(probs.astype(low), grad)
            key_grad = from_keys if key_grad is None else key_grad + from_keys
            value_grad = from_values if value_grad is None else value_grad + from_values
        for start, value in ((g * HEAD_DIM, key_grad), (KV + g * HEAD_DIM, value_grad)):
            turned = value.T.astype(low)
            for b in range(kv_ref.shape[0]):
                dkv_ref[b, start : start + HEAD_DIM, :] = turned[:, b * width : (b + 1) * width]


def attention_specs(blocks, block_len, length, seq):
    columns = pl.BlockSpec((ATTN, block_len), lambda i: (0, seq))
    pairs = pl.BlockSpec((blocks, 2 * KV, block_len), lambda i: (0, 0, seq))
    bias = pl.BlockSpec((1, length, block_len), lambda i: (seq, 0, 0))
    own = pl.BlockSpec((ATTN, block_len), lambda i: (0, 0))
    own_pairs = pl.BlockSpec((blocks, 2 * KV, block_len), lambda i: (0, 0, 0))
    logs = pl.BlockSpec((1, HEADS, block_len), lambda i: (0, 0, 0))
    return columns, pairs, bias, own, own_pairs, logs


def attend(query_t, pairs_t, bias, seq):
    _, length, block_len = bias.shape
    columns, pairs, bias_spec, own, _, logs = attention_specs(
        pairs_t.shape[0], block_len, length, seq
    )
    work = HEADS * length * block_len
    return pl.pallas_call(
        attend_kernel,
        grid=(1,),
        in_specs=[columns, pairs, bias_spec],
        out_specs=[own, logs],
        out_shape=[
            jax.ShapeDtypeStruct((ATTN, block_len), low),
            jax.ShapeDtypeStruct((1, HEADS, block_len), wide),
        ],
        compiler_params=pltpu.CompilerParams(vmem_limit_bytes=40 * 2**20),
        cost_estimate=pl.CostEstimate(
            flops=work, bytes_accessed=2**20, transcendentals=0
        ),
        name="attend",
    )(query_t, pairs_t, bias)


def attend_back(query_t, pairs_t, bias, mixed_t, logs_all, grad_t, seq):
    _, length, block_len = bias.shape
    columns, pairs, bias_spec, own, own_pairs, logs = attention_specs(
        pairs_t.shape[0], block_len, length, seq
    )
    work = HEADS * length * block_len
    return pl.pallas_call(
        attend_back_kernel,
        grid=(1,),
        in_specs=[columns, pairs, bias_spec, own, logs, columns],
        out_specs=[own, own_pairs],
        out_shape=[
            jax.ShapeDtypeStruct((ATTN, block_len), wide),
            jax.ShapeDtypeStruct((pairs_t.shape[0], 2 * KV, block_len), low),
        ],
        compiler_params=pltpu.CompilerParams(vmem_limit_bytes=48 * 2**20),
        cost_estimate=pl.CostEstimate(
            flops=work, bytes_accessed=2**20, transcendentals=0
        ),
        name="attend_back",
    )(query_t, pairs_t, bias, mixed_t, logs_all, grad_t)


def project_kernel(a_ref, q0_ref, q1_ref, p0_ref, p1_ref, cos_ref, sin_ref, q_ref, p_ref, *, scale):
    split = q0_ref.shape[0]
    half = HEAD_DIM // 2
    first, second = a_ref[:, :split], a_ref[:, split:]
    cosine, sine = cos_ref[...], sin_ref[...]

    def turned(value):
        upper, lower = value[half:], value[:half]
        return value * cosine + jnp.concatenate([-upper, lower], axis=0) * sine

    pairs = (product(first, p0_ref[...]) + product(second, p1_ref[...])).T
    for h in range(KV_HEADS):
        at = slice(h * HEAD_DIM, (h + 1) * HEAD_DIM)
        p_ref[at, :] = turned(pairs[at]).astype(low)
    p_ref[KV:, :] = pairs[KV:].astype(low)
    query = (product(first, q0_ref[...]) + product(second, q1_ref[...])).T
    for h in range(HEADS):
        at = slice(h * HEAD_DIM, (h + 1) * HEAD_DIM)
        q_ref[at, :] = (turned(query[at]) * scale).astype(low)


def project(normed, query_halves, pairs_halves, cosine, sine, scale):
    rows = normed.shape[0]
    halves = [h.reshape(-1, h.shape[-1]) for h in (*query_halves, *pairs_halves)]
    return pl.pallas_call(
        functools.partial(project_kernel, scale=scale),
        in_specs=[whole_spec()] * 7,
        out_specs=[whole_spec()] * 2,
        out_shape=[
            jax.ShapeDtypeStruct((ATTN, rows), low),
            jax.ShapeDtypeStruct((2 * KV, rows), low),
        ],
        compiler_params=pltpu.CompilerParams(vmem_limit_bytes=40 * 2**20),
        cost_estimate=pl.CostEstimate(flops=rows, bytes_accessed=2**20, transcendentals=0),
        name="project",
    )(normed, *halves, cosine, sine)


def key_bias(segment_all, segment_ids, ctx_here, masks):
    blocks, seqs, block_len = segment_all.shape
    place = jnp.arange(blocks, dtype=jnp.int32)
    owner = jnp.zeros_like(place)
    for bit, mask in enumerate(masks):
        owner = owner | (((place >> bit) & 1) * mask)
    inside = jnp.arange(block_len, dtype=jnp.int32)
    key_index = ((owner ^ ctx_here)[:, None] * block_len + inside[None, :]).reshape(-1)
    query_index = ctx_here * block_len + inside
    segments = segment_all.transpose(1, 0, 2).reshape(seqs, -1)
    allowed = (segments[:, :, None] == segment_ids[:, None, :]) & (
        key_index[None, :, None] <= query_index[None, None, :]
    )
    return jnp.where(allowed, 0.0, mask_fill)


def contract(left, right, left_dim, right_dim):
    return lax.dot_general(
        left, right, (((left_dim,), (right_dim,)), ((), ())), preferred_element_type=wide
    )


def silu_parts(gate, up):
    sigmoid = jax.nn.sigmoid(gate)
    return sigmoid, (gate * sigmoid * up).astype(low)


def silu_back(hidden_grad, gate, up, sigmoid):
    gate_grad = (hidden_grad * up * sigmoid * (1.0 + gate * (1.0 - sigmoid))).astype(low)
    return gate_grad, (hidden_grad * gate * sigmoid).astype(low)


def body_blocked(
    tokens, segment_ids, positions, norm_attn, w_query, w_key, w_value, w_out,
    norm_ffn, w_gate, w_up, w_down, cotangent,
):
    seqs, block_len, _ = tokens.shape
    n_dev = lax.axis_size(AXES)
    me, ctx_here = lax.axis_index(AXES), lax.axis_index("ctx")
    rows = seqs * block_len
    score_scale = HEAD_DIM ** (-0.5)
    cut, cut_ff = D // n_dev, FF // n_dev
    pad = -(-cut // 16) * 16
    top_ff = (cut_ff * 3 // 5) // 8 * 8
    low_ff = cut_ff - top_ff
    half = n_dev // 2
    split = half * pad
    slots = Slots()
    ahead = (seqs + 1) // 2

    def rows_of(shard, columns):
        return jnp.pad(shard.reshape(cut, columns), ((0, pad - cut), (0, 0)))

    def weight(move):
        return move.both.reshape(-1, move.both.shape[-1])

    attn_block = jnp.concatenate(
        [rows_of(w_key, KV), rows_of(w_value, KV), rows_of(w_query, ATTN)], axis=1
    )[None]
    attn = Spread(attn_block, 8)
    slots.run([attn])
    mix_block = jnp.concatenate([w_down.reshape(cut_ff, D), rows_of(w_out, D)], axis=0)[None]
    mix = Spread(mix_block, 8)
    attn = Spread(attn.both, 16)
    seg_y = Move(slots.after(segment_ids), FIRST)
    inputs = slots.after(tokens).astype(wide).reshape(rows, D)
    slots.run([attn, mix], [seg_y])
    places = jnp.arange(n_dev, dtype=jnp.int32)
    order = block_owner(places) ^ me
    place = jnp.sum(jnp.where(order[:, None] == places[None, :], places[:, None], 0), axis=0)
    slot = jnp.arange(n_dev * pad, dtype=jnp.int32)
    source = jnp.where(slot % pad < cut, jnp.repeat(order, pad) * cut + slot % pad, -1)
    perm = (jnp.arange(D, dtype=jnp.int32)[:, None] == source[None, :]).astype(low)
    scale_attn = rms_scale(inputs)
    normed_attn = product((inputs * scale_attn * norm_attn).astype(low), perm).astype(low)
    segments = jnp.stack([segment_ids, seg_y.came])
    seg_c = Move(segments, CORE)
    pairs_w = SpreadFirst(attn.both[..., : 2 * KV], FIRST)
    query_w = Spread(attn.both[..., 2 * KV :], SECOND)
    mix = Spread(mix.both, 16)
    angles = slots.after(positions).reshape(rows)
    slots.run([pairs_w, query_w], [mix, seg_c])
    cosine, sine = rope_tables(angles)
    segments = jnp.concatenate([segments, seg_c.came], axis=0)
    bias = key_bias(slots.after(segments), segment_ids, ctx_here, (2, 1))
    slots.hold(normed_attn)
    pairs_w = SpreadBetween(pairs_w, SECOND)
    query_w = Spread(query_w.both, FIRST)
    pair_block = jnp.concatenate([rows_of(w_gate, FF), rows_of(w_up, FF)], axis=1)[None]
    pair = Spread(pair_block, 8)
    slots.run([pairs_w, query_w], [pair])
    slots.hold(cosine, sine)
    pairs_w, query_w = Spread(pairs_w.both, CORE), Spread(query_w.both, CORE)
    top_w, low_w = Spread(mix.both[:, :top_ff], SECOND), SpreadFirst(mix.both[:, top_ff:], FIRST)
    gate_w = Spread(pair.both[..., :FF], 16)
    slots.run([pairs_w, query_w, top_w, low_w], [gate_w])
    query_weight, kv_weight = weight(query_w), weight(pairs_w)
    query_t, pairs_t = project(
        normed_attn,
        (query_w.value, query_w.came),
        (pairs_w.value, pairs_w.came),
        cosine,
        sine,
        score_scale,
    )
    top_w, low_w = Spread(top_w.both, FIRST), SpreadBetween(low_w, SECOND)
    slots.run([], [top_w, low_w])
    pairs_all = Spread(pairs_t[None], FIRST)
    up_w = Spread(pair.both[..., FF:], 16)
    gate_w = Spread(gate_w.both, SECOND)
    slots.hold(bias, query_t)
    slots.run([pairs_all], [up_w, gate_w])
    pairs_all = Spread(pairs_all.both, CORE)
    up_w = SpreadFirst(up_w.both, FIRST)
    top_core = Move(top_w.both, CORE)
    low_core = Move(low_w.both, CORE)
    slots.run([pairs_all], [up_w, top_core, low_core])
    pairs_all = pairs_all.both
    mixed, logs = [None] * seqs, [None] * seqs
    for seq in range(ahead):
        mixed[seq], logs[seq] = attend(query_t, pairs_all, bias, seq)
    gate_w, up_w = Spread(gate_w.both, FIRST), SpreadBetween(up_w, SECOND)
    slots.run([], [gate_w, up_w])
    for seq in range(ahead, seqs):
        mixed[seq], logs[seq] = attend(query_t, pairs_all, bias, seq)
    down_weight, out_weight = join_blocks(
        (top_w.both, top_core.came), (low_w.both, low_core.came), order, low_ff
    )
    down_weight, out_weight = down_weight.reshape(FF, D), out_weight.reshape(-1, D)
    down_grad = cotangent.reshape(rows, D)
    hidden_grad = product_right(down_grad, down_weight)
    gate_w, up_w = Spread(gate_w.both, CORE), Spread(up_w.both, CORE)
    slots.run([gate_w, up_w])
    attended = jnp.concatenate([contract(m, perm, 0, 0).astype(low) for m in mixed], axis=0)
    resid = inputs + product(attended, out_weight)
    scale_ffn = rms_scale(resid)
    normed_ffn = product((resid * scale_ffn * norm_ffn).astype(low), perm).astype(low)
    gate_weight, up_weight = weight(gate_w), weight(up_w)
    gate, up = product(normed_ffn, gate_weight), product(normed_ffn, up_weight)
    sigmoid, hidden = silu_parts(gate, up)
    gate_grad, up_grad = silu_back(hidden_grad, gate, up, sigmoid)

    def halves(left, right, right_dim):
        both = []
        for piece in (left[:, :split], left[:, split:]):
            grad = contract(piece, right, 0, right_dim).astype(low)
            both.append(grad.reshape(half, pad, -1))
        return FoldPair(*both, CORE)

    def flat(grad):
        return grad[:cut].reshape(-1)

    def collect_wide(value):
        high = lax.reduce_precision(value, 8, 7)
        return product_right(high.astype(low), perm) + product_right(
            (value - high).astype(low), perm
        )

    gate_s, up_s = halves(normed_ffn, gate_grad, 0), halves(normed_ffn, up_grad, 0)
    slots.run([gate_s, up_s])
    top_grad, low_grad = down_grad_blocks(hidden, down_grad, place, top_ff)
    top_s = FoldPair(top_grad[:half], top_grad[half:], CORE)
    low_s = FoldPair(low_grad[:half], low_grad[half:], CORE)
    gate_s, up_s = Fold(gate_s.sum, FIRST), FoldBetween(up_s.sum, SECOND)
    slots.run([gate_s, up_s], [top_s, low_s])
    normed_grad = product_right(gate_grad, gate_weight) + product_right(up_grad, up_weight)
    normed_grad = collect_wide(normed_grad)
    grad_out = cotangent.astype(wide).reshape(rows, D)
    resid_grad, ffn_gain_grad = norm_back(resid, scale_ffn, norm_ffn, normed_grad)
    resid_grad = resid_grad + grad_out
    branch_grad = resid_grad.astype(low)
    grad_t = product_right(perm, product_right(branch_grad, out_weight).astype(low)).astype(low)
    grad_t = slots.after(grad_t)
    back = [None] * seqs
    for seq in range(ahead):
        back[seq] = attend_back(query_t, pairs_all, bias, mixed[seq], logs[seq], grad_t, seq)
    gate_s, up_s = Fold(gate_s.sum, SECOND), Fold(up_s.sum, FIRST)
    top_s, low_s = Fold(top_s.sum, FIRST), FoldBetween(low_s.sum, SECOND)
    slots.run([gate_s, up_s], [top_s, low_s])
    grad_t = slots.after(grad_t)
    for seq in range(ahead, seqs):
        back[seq] = attend_back(query_t, pairs_all, bias, mixed[seq], logs[seq], grad_t, seq)
    gate_s, up_s = Fold(gate_s.sum, 16), Fold(up_s.sum, 16)
    out_s = halves(slots.after(attended), branch_grad, 0)
    slots.run([], [gate_s, up_s])
    pairs_part = jnp.concatenate([b[1] for b in back], axis=2)
    pairs_s = FoldPair(pairs_part[:2], pairs_part[2:], CORE)
    top_s, low_s = Fold(top_s.sum, SECOND), Fold(low_s.sum, FIRST)
    slots.run([pairs_s], [top_s, low_s, out_s])
    query_low = jnp.concatenate([b[0] for b in back], axis=1)
    query_low = rotate_back(query_low * score_scale, cosine, sine).astype(low)
    query_s = halves(normed_attn, query_low, 1)
    pairs_s = Fold(pairs_s.sum, FIRST, last=True)
    out_s = FoldBetween(out_s.sum, SECOND)
    slots.run([pairs_s, query_s], [out_s])
    gate_s, up_s = Fold(gate_s.sum, 8, last=True), Fold(up_s.sum, 8, last=True)
    down_s = Fold(jnp.concatenate([top_s.sum, low_s.sum], axis=1), 16)
    pairs_grad = slots.after(pairs_s.sum)
    query_s, out_s = Fold(query_s.sum, FIRST), Fold(out_s.sum, FIRST)
    slots.run([], [query_s, out_s, gate_s, up_s, down_s])
    pairs_low = jnp.concatenate(
        [rotate_back(pairs_grad[:KV], cosine, sine).astype(low), pairs_grad[KV:].astype(low)],
        axis=0,
    )
    pairs_s = halves(normed_attn, pairs_low, 1)
    slots.run([pairs_s])
    attn_normed_grad = collect_wide(
        contract(query_low, query_weight, 0, 1) + contract(pairs_low, kv_weight, 0, 1)
    )
    input_grad, attn_gain_grad = norm_back(inputs, scale_attn, norm_attn, attn_normed_grad)
    d_tokens = (input_grad + resid_grad).reshape(seqs, block_len, D)
    output = (resid + product(slots.after(hidden), down_weight)).astype(low)
    output = output.reshape(seqs, block_len, D)
    query_s = Fold(query_s.sum, SECOND)
    pairs_s = FoldBetween(pairs_s.sum, SECOND)
    down_s = Fold(down_s.sum, 8, last=True)
    slots.run([pairs_s], [query_s, down_s])
    attn_s = Fold(jnp.concatenate([query_s.sum, out_s.sum], axis=2), 16)
    pairs_s = Fold(pairs_s.sum, FIRST)
    gains = Move(jnp.stack([attn_gain_grad, ffn_gain_grad]), CORE)
    slots.run([pairs_s, attn_s, gains])
    attn_s = Fold(attn_s.sum, 8, last=True)
    pairs_s = Fold(pairs_s.sum, 16)
    gains = gains.value + gains.came
    asked = [Move(gains, m) for m in (FIRST, SECOND, FIRST | SECOND)]
    slots.run([pairs_s, attn_s, *asked])
    gains = (gains + asked[0].came) + (asked[1].came + asked[2].came)
    pairs_s = Fold(pairs_s.sum, 8, last=True)
    asked = [Move(gains, m) for m in (8, 16, 24)]
    slots.run([pairs_s, *asked])
    gains = (gains + asked[0].came) + (asked[1].came + asked[2].came)
    return (
        output,
        d_tokens,
        gains[0],
        flat(attn_s.sum[:, :ATTN]),
        flat(pairs_s.sum[:, :KV]),
        flat(pairs_s.sum[:, KV:]),
        flat(attn_s.sum[:, ATTN:]),
        gains[1],
        flat(gate_s.sum),
        flat(up_s.sum),
        down_s.sum.reshape(-1),
    )


def body_whole(
    tokens, segment_ids, positions, norm_attn, w_query, w_key, w_value, w_out,
    norm_ffn, w_gate, w_up, w_down, cotangent,
):
    seqs, block_len, _ = tokens.shape
    n_dev = lax.axis_size(AXES)
    rows = seqs * block_len
    score_scale = HEAD_DIM ** (-0.5)

    def whole(shard, columns):
        return lax.all_gather(shard, AXES, axis=0, tiled=True).reshape(-1, columns)

    query_weight = whole(w_query, ATTN)
    kv_weight = jnp.concatenate([whole(w_key, KV), whole(w_value, KV)], axis=1)
    out_weight = whole(w_out, D)
    gate_weight, up_weight = whole(w_gate, FF), whole(w_up, FF)
    down_weight = whole(w_down, D)
    inputs = tokens.astype(wide).reshape(rows, D)
    grad_out = cotangent.astype(wide).reshape(rows, D)
    scale_attn = rms_scale(inputs)
    normed_attn = (inputs * scale_attn * norm_attn).astype(low)
    cosine, sine = rope_tables(positions.reshape(rows))
    bias = key_bias(ctx_gather(segment_ids), segment_ids, lax.axis_index("ctx"), ctx_masks())
    pairs_t = contract(kv_weight, normed_attn, 0, 1)
    pairs_t = jnp.concatenate(
        [rotate(pairs_t[:KV], cosine, sine).astype(low), pairs_t[KV:].astype(low)], axis=0
    )
    pairs_all = ctx_gather(pairs_t)
    query_t = contract(query_weight, normed_attn, 0, 1)
    query_t = (rotate(query_t, cosine, sine) * score_scale).astype(low)
    mixed, logs = zip(*[attend(query_t, pairs_all, bias, seq) for seq in range(seqs)])
    attended = jnp.concatenate([m.T for m in mixed], axis=0)
    resid = inputs + product(attended, out_weight)
    scale_ffn = rms_scale(resid)
    normed_ffn = (resid * scale_ffn * norm_ffn).astype(low)
    gate, up = product(normed_ffn, gate_weight), product(normed_ffn, up_weight)
    sigmoid, hidden = silu_parts(gate, up)
    output = (resid + product(hidden, down_weight)).astype(low).reshape(seqs, block_len, D)
    down_grad = cotangent.reshape(rows, D)
    gate_grad, up_grad = silu_back(product_right(down_grad, down_weight), gate, up, sigmoid)
    normed_grad = product_right(gate_grad, gate_weight) + product_right(up_grad, up_weight)
    resid_grad, ffn_gain_grad = norm_back(resid, scale_ffn, norm_ffn, normed_grad)
    resid_grad = resid_grad + grad_out
    branch_grad = resid_grad.astype(low)
    grad_t = product_right(branch_grad, out_weight).astype(low).T
    back = [
        attend_back(query_t, pairs_all, bias, mixed[seq], logs[seq], grad_t, seq)
        for seq in range(seqs)
    ]
    pairs_grad = ctx_scatter(jnp.concatenate([b[1] for b in back], axis=2))
    query_low = jnp.concatenate([b[0] for b in back], axis=1)
    query_low = rotate_back(query_low * score_scale, cosine, sine).astype(low)
    pairs_low = jnp.concatenate(
        [rotate_back(pairs_grad[:KV], cosine, sine).astype(low), pairs_grad[KV:].astype(low)],
        axis=0,
    )
    normed_grad = contract(query_low, query_weight, 0, 1) + contract(pairs_low, kv_weight, 0, 1)
    input_grad, attn_gain_grad = norm_back(inputs, scale_attn, norm_attn, normed_grad)
    d_tokens = (input_grad + resid_grad).reshape(seqs, block_len, D)

    def finish(left, right, right_dim):
        grad = contract(left, right, 0, right_dim).astype(low).reshape(n_dev, -1)
        grad = lax.psum_scatter(grad, AXES, scatter_dimension=0, tiled=True)
        return grad.astype(wide).reshape(-1)

    attn_gain_sum, ffn_gain_sum = lax.psum((attn_gain_grad, ffn_gain_grad), AXES)
    return (
        output,
        d_tokens,
        attn_gain_sum,
        finish(normed_attn, query_low, 1),
        finish(normed_attn, pairs_low[:KV], 1),
        finish(normed_attn, pairs_low[KV:], 1),
        finish(attended, branch_grad, 0),
        ffn_gain_sum,
        finish(normed_ffn, gate_grad, 0),
        finish(normed_ffn, up_grad, 0),
        finish(hidden, down_grad, 0),
    )


def solution(mesh):
    sizes = dict(mesh.shape)
    blocked = sizes["dp"] == 8 and sizes["ctx"] == 4
    body = body_blocked if blocked else body_whole
    one = P(AXES)
    tok = P("dp", "ctx", None)
    ids = P("dp", "ctx")
    in_specs = (tok, ids, ids, P(), one, one, one, one, P(), one, one, one, tok)
    out_specs = (tok, tok, P(), one, one, one, one, P(), one, one, one)
    return jax.shard_map(body, mesh=mesh, in_specs=in_specs, out_specs=out_specs, check_vma=False)
```

```python
import functools

import jax
import jax.numpy as jnp
from jax import lax
from jax.experimental import pallas as pl
from jax.experimental.pallas import tpu as pltpu
from jax.sharding import PartitionSpec as P

D = 960
HEADS = 15
KV_HEADS = 5
HEAD_DIM = 64
FF = 2560
GROUP = HEADS // KV_HEADS
ATTN = HEADS * HEAD_DIM
KV = KV_HEADS * HEAD_DIM
AXES = ("dp", "ctx")
CORE, FIRST, SECOND = 1, 2, 4

norm_eps = 1e-05
rope_base = 100000.0
mask_fill = -1000000000.0
low = jnp.bfloat16
wide = jnp.float32


def rms_scale(values):
    return lax.rsqrt(jnp.mean(values * values, axis=-1, keepdims=True) + norm_eps)


def norm_back(values, scale, gain, grad):
    gain_grad = jnp.sum(grad * values * scale, axis=0)
    weighted = grad * gain
    inner = jnp.mean(weighted * values, axis=-1, keepdims=True)
    return (scale * weighted - values * (scale * scale * scale) * inner, gain_grad)


def rope_tables(position):
    freqs = rope_base ** (-jnp.arange(0, HEAD_DIM, 2, dtype=wide) / HEAD_DIM)
    angles = freqs[:, None] * position.astype(wide)[None, :]
    angles = jnp.concatenate([angles, angles], axis=0)
    return jnp.cos(angles), jnp.sin(angles)


def by_head(values):
    return values.reshape(-1, HEAD_DIM, values.shape[-1])


def rotate(values, cosine, sine):
    values = by_head(values)
    half = HEAD_DIM // 2
    turned = jnp.concatenate([-values[:, half:], values[:, :half]], axis=1)
    return (values * cosine + turned * sine).reshape(-1, values.shape[-1])


def rotate_back(grad, cosine, sine):
    grad = by_head(grad)
    half = HEAD_DIM // 2
    scaled = grad * sine
    turned = jnp.concatenate([scaled[:, half:], -scaled[:, :half]], axis=1)
    return (grad * cosine + turned).reshape(-1, grad.shape[-1])


def product(left, right):
    return jnp.dot(left, right, preferred_element_type=wide)


def product_left(left, right):
    return lax.dot_general(left, right, (((0,), (0,)), ((), ())), preferred_element_type=wide)


def product_right(left, right):
    return lax.dot_general(left, right, (((1,), (1,)), ((), ())), preferred_element_type=wide)


def swap(value, mask):
    n = lax.axis_size(AXES)
    return lax.ppermute(value, AXES, [(i, i ^ mask) for i in range(n)])


def add_low(left, right):
    return (left.astype(wide) + right.astype(wide)).astype(low)


def far_masks():
    n = lax.axis_size(AXES)
    masks, m = [], 8
    while m < n:
        masks.append(m)
        m *= 2
    return masks


def block_owner(place):
    far = far_masks()
    owner = jnp.zeros_like(place)
    for bit, mask in enumerate(far + [SECOND, FIRST, CORE]):
        owner = owner | (((place >> bit) & 1) * mask)
    return owner


class Slots:
    def __init__(self):
        self.deps = ()

    def after(self, value):
        return lax.optimization_barrier((value, self.deps))[0]

    def hold(self, *values):
        self.deps = self.deps + values

    def run(self, moves, late=()):
        before, self.deps = self.deps, ()
        for i, move in enumerate((*moves, *late)):
            value = move.give()
            if before:
                value = lax.optimization_barrier((value, before))[0]
            came = swap(value, move.mask)
            if i < len(moves):
                self.deps += (came,)
            move.take(came)


class Move:
    def __init__(self, value, mask):
        self.value, self.mask = value, mask

    def give(self):
        return self.value

    def take(self, came):
        self.came = came


class Spread(Move):
    def take(self, came):
        self.came = came
        self.both = jnp.concatenate([self.value, came], axis=0)


class SpreadBetween(Spread):
    def __init__(self, first, mask):
        self.own, self.side = first.value, first.came
        super().__init__(first.both, mask)

    def take(self, came):
        n = came.shape[0] // 2
        self.both = jnp.concatenate([self.own, came[:n], self.side, came[n:]], axis=0)


class SpreadFirst(Spread):
    def take(self, came):
        self.came = came
        super().take(came)


class Fold(Move):
    def __init__(self, value, mask, last=False):
        self.n, self.last = value.shape[0] // 2, last
        super().__init__(value, mask)

    def give(self):
        return self.value[self.n :]

    def take(self, came):
        if self.last:
            self.sum = self.value[0].astype(wide) + came[0].astype(wide)
        else:
            self.sum = add_low(self.value[: self.n], came)


class FoldPair(Fold):
    def __init__(self, mine, theirs, mask):
        self.value, self.theirs, self.mask, self.last = mine, theirs, mask, False
        self.n = mine.shape[0]

    def give(self):
        return self.theirs


class FoldBetween(Fold):
    def give(self):
        q = self.n // 2
        return jnp.concatenate([self.value[q : self.n], self.value[self.n + q :]], axis=0)

    def take(self, came):
        q = self.n // 2
        kept = jnp.concatenate([self.value[:q], self.value[self.n : self.n + q]], axis=0)
        self.sum = add_low(kept, came)


def ctx_masks():
    m, masks = lax.axis_size("ctx") // 2, []
    while m >= 1:
        masks.append(m)
        m //= 2
    return masks


def ctx_gather(value):
    now = value[None]
    for mask in ctx_masks():
        now = jnp.concatenate([now, swap(now, mask)], axis=0)
    return now


def ctx_scatter(value):
    now = value
    for mask in ctx_masks()[::-1]:
        n = now.shape[0] // 2
        now = now[:n].astype(wide) + swap(now[n:], mask).astype(wide)
        if n > 1:
            now = now.astype(low)
    return now[0]


def whole_spec():
    return pl.BlockSpec(memory_space=pltpu.VMEM)


def join_blocks(tops, lows, order, low_rows):
    (a, b), (c, d) = tops, lows
    half, top, columns = a.shape
    rest = c.shape[1] - low_rows

    def kernel(order_ref, a_ref, b_ref, c_ref, d_ref, down_ref, out_ref):
        def step(p, _):
            near, far = order_ref[p], order_ref[p + half]
            down_ref[near, :top, :] = a_ref[p]
            down_ref[near, top:, :] = c_ref[p, :low_rows, :]
            down_ref[far, :top, :] = b_ref[p]
            down_ref[far, top:, :] = d_ref[p, :low_rows, :]
            out_ref[p] = c_ref[p, low_rows:, :]
            out_ref[p + half] = d_ref[p, low_rows:, :]
            return 0

        lax.fori_loop(0, half, step, 0)

    shape = (2 * half, top + low_rows, columns)
    return pl.pallas_call(
        kernel,
        out_shape=[
            jax.ShapeDtypeStruct(shape, a.dtype),
            jax.ShapeDtypeStruct((2 * half, rest, columns), a.dtype),
        ],
        in_specs=[pl.BlockSpec(memory_space=pltpu.SMEM)] + [whole_spec()] * 4,
        out_specs=[whole_spec()] * 2,
        compiler_params=pltpu.CompilerParams(vmem_limit_bytes=32 * 2**20),
        cost_estimate=pl.CostEstimate(flops=0, bytes_accessed=2**20, transcendentals=0),
        name="join_blocks",
    )(order, a, b, c, d)


def down_grad_blocks(hidden, grad, place, top):
    rows, hidden_width = hidden.shape
    columns = grad.shape[1]
    total = place.shape[0]
    tall = hidden_width // total
    group = 8

    def kernel(place_ref, h_ref, g_ref, a_ref, b_ref):
        value = product_left(h_ref[...], g_ref[...]).astype(low)
        first = pl.program_id(0) * group
        for b in range(group):
            to = place_ref[first + b]
            a_ref[to] = value[b * tall : b * tall + top]
            b_ref[to] = value[b * tall + top : (b + 1) * tall]

    return pl.pallas_call(
        kernel,
        grid=(total // group,),
        in_specs=[
            pl.BlockSpec(memory_space=pltpu.SMEM),
            pl.BlockSpec((rows, group * tall), lambda i: (0, i)),
            pl.BlockSpec((rows, columns), lambda i: (0, 0)),
        ],
        out_specs=[
            pl.BlockSpec((total, top, columns), lambda i: (0, 0, 0)),
            pl.BlockSpec((total, tall - top, columns), lambda i: (0, 0, 0)),
        ],
        out_shape=[
            jax.ShapeDtypeStruct((total, top, columns), low),
            jax.ShapeDtypeStruct((total, tall - top, columns), low),
        ],
        compiler_params=pltpu.CompilerParams(vmem_limit_bytes=32 * 2**20),
        cost_estimate=pl.CostEstimate(
            flops=2 * rows * hidden_width * columns,
            bytes_accessed=2 * (rows * (hidden_width + columns) + hidden_width * columns),
            transcendentals=0,
        ),
        name="down_grad_blocks",
    )(place, hidden, grad)


def head_rows(ref, head):
    return ref[head * HEAD_DIM : (head + 1) * HEAD_DIM, :]


def key_blocks(kv_ref, start):
    blocks = [kv_ref[b, start : start + HEAD_DIM, :] for b in range(kv_ref.shape[0])]
    return jnp.concatenate(blocks, axis=1)


def turn(value):
    return value.astype(wide).T.astype(low)


def attend_kernel(q_ref, kv_ref, bias_ref, o_ref, lse_ref):
    for g in range(KV_HEADS):
        keys = turn(key_blocks(kv_ref, g * HEAD_DIM))
        values_t = key_blocks(kv_ref, KV + g * HEAD_DIM)
        for h in range(g * GROUP, (g + 1) * GROUP):
            scores = product(keys, head_rows(q_ref, h)) + bias_ref[0]
            top = jnp.max(scores, axis=0, keepdims=True)
            weight = jnp.exp(scores - top)
            total = jnp.sum(weight, axis=0, keepdims=True)
            mixed = product(values_t, weight.astype(low)) / total
            o_ref[h * HEAD_DIM : (h + 1) * HEAD_DIM, :] = mixed.astype(low)
            lse_ref[0, h : h + 1, :] = top + jnp.log(total)


def attend_back_kernel(q_ref, kv_ref, bias_ref, o_ref, lse_ref, do_ref, dq_ref, dkv_ref):
    width = q_ref.shape[1]
    for g in range(KV_HEADS):
        keys_t = key_blocks(kv_ref, g * HEAD_DIM)
        keys = turn(keys_t)
        values = turn(key_blocks(kv_ref, KV + g * HEAD_DIM))
        key_grad, value_grad = None, None
        for h in range(g * GROUP, (g + 1) * GROUP):
            query, grad = head_rows(q_ref, h), head_rows(do_ref, h)
            scores = product(keys, query) + bias_ref[0]
            probs = jnp.exp(scores - lse_ref[0, h : h + 1, :])
            inner = jnp.sum(
                grad.astype(wide) * head_rows(o_ref, h).astype(wide), axis=0, keepdims=True
            )
            scores_grad = (probs * (product(values, grad) - inner)).astype(low)
            dq_ref[h * HEAD_DIM : (h + 1) * HEAD_DIM, :] = product(keys_t, scores_grad)
            from_keys = product_right(scores_grad, query)
            from_values = product_right(probs.astype(low), grad)
            key_grad = from_keys if key_grad is None else key_grad + from_keys
            value_grad = from_values if value_grad is None else value_grad + from_values
        for start, value in ((g * HEAD_DIM, key_grad), (KV + g * HEAD_DIM, value_grad)):
            turned = value.T.astype(low)
            for b in range(kv_ref.shape[0]):
                dkv_ref[b, start : start + HEAD_DIM, :] = turned[:, b * width : (b + 1) * width]


def attention_specs(blocks, block_len, length, seq):
    columns = pl.BlockSpec((ATTN, block_len), lambda i: (0, seq))
    pairs = pl.BlockSpec((blocks, 2 * KV, block_len), lambda i: (0, 0, seq))
    bias = pl.BlockSpec((1, length, block_len), lambda i: (seq, 0, 0))
    own = pl.BlockSpec((ATTN, block_len), lambda i: (0, 0))
    own_pairs = pl.BlockSpec((blocks, 2 * KV, block_len), lambda i: (0, 0, 0))
    logs = pl.BlockSpec((1, HEADS, block_len), lambda i: (0, 0, 0))
    return columns, pairs, bias, own, own_pairs, logs


def attend(query_t, pairs_t, bias, seq):
    _, length, block_len = bias.shape
    columns, pairs, bias_spec, own, _, logs = attention_specs(
        pairs_t.shape[0], block_len, length, seq
    )
    work = HEADS * length * block_len
    return pl.pallas_call(
        attend_kernel,
        grid=(1,),
        in_specs=[columns, pairs, bias_spec],
        out_specs=[own, logs],
        out_shape=[
            jax.ShapeDtypeStruct((ATTN, block_len), low),
            jax.ShapeDtypeStruct((1, HEADS, block_len), wide),
        ],
        compiler_params=pltpu.CompilerParams(vmem_limit_bytes=40 * 2**20),
        cost_estimate=pl.CostEstimate(
            flops=work, bytes_accessed=2**20, transcendentals=0
        ),
        name="attend",
    )(query_t, pairs_t, bias)


def attend_back(query_t, pairs_t, bias, mixed_t, logs_all, grad_t, seq):
    _, length, block_len = bias.shape
    columns, pairs, bias_spec, own, own_pairs, logs = attention_specs(
        pairs_t.shape[0], block_len, length, seq
    )
    work = HEADS * length * block_len
    return pl.pallas_call(
        attend_back_kernel,
        grid=(1,),
        in_specs=[columns, pairs, bias_spec, own, logs, columns],
        out_specs=[own, own_pairs],
        out_shape=[
            jax.ShapeDtypeStruct((ATTN, block_len), wide),
            jax.ShapeDtypeStruct((pairs_t.shape[0], 2 * KV, block_len), low),
        ],
        compiler_params=pltpu.CompilerParams(vmem_limit_bytes=48 * 2**20),
        cost_estimate=pl.CostEstimate(
            flops=work, bytes_accessed=2**20, transcendentals=0
        ),
        name="attend_back",
    )(query_t, pairs_t, bias, mixed_t, logs_all, grad_t)


def project_kernel(a_ref, q0_ref, q1_ref, p0_ref, p1_ref, cos_ref, sin_ref, q_ref, p_ref, *, scale):
    split = q0_ref.shape[0]
    half = HEAD_DIM // 2
    first, second = a_ref[:, :split], a_ref[:, split:]
    cosine, sine = cos_ref[...], sin_ref[...]

    def turned(value):
        upper, lower = value[half:], value[:half]
        return value * cosine + jnp.concatenate([-upper, lower], axis=0) * sine

    pairs = (product(first, p0_ref[...]) + product(second, p1_ref[...])).T
    for h in range(KV_HEADS):
        at = slice(h * HEAD_DIM, (h + 1) * HEAD_DIM)
        p_ref[at, :] = turned(pairs[at]).astype(low)
    p_ref[KV:, :] = pairs[KV:].astype(low)
    query = (product(first, q0_ref[...]) + product(second, q1_ref[...])).T
    for h in range(HEADS):
        at = slice(h * HEAD_DIM, (h + 1) * HEAD_DIM)
        q_ref[at, :] = (turned(query[at]) * scale).astype(low)


def project(normed, query_halves, pairs_halves, cosine, sine, scale):
    rows = normed.shape[0]
    halves = [h.reshape(-1, h.shape[-1]) for h in (*query_halves, *pairs_halves)]
    return pl.pallas_call(
        functools.partial(project_kernel, scale=scale),
        in_specs=[whole_spec()] * 7,
        out_specs=[whole_spec()] * 2,
        out_shape=[
            jax.ShapeDtypeStruct((ATTN, rows), low),
            jax.ShapeDtypeStruct((2 * KV, rows), low),
        ],
        compiler_params=pltpu.CompilerParams(vmem_limit_bytes=40 * 2**20),
        cost_estimate=pl.CostEstimate(flops=rows, bytes_accessed=2**20, transcendentals=0),
        name="project",
    )(normed, *halves, cosine, sine)


def key_bias(segment_all, segment_ids, ctx_here, masks):
    blocks, seqs, block_len = segment_all.shape
    place = jnp.arange(blocks, dtype=jnp.int32)
    owner = jnp.zeros_like(place)
    for bit, mask in enumerate(masks):
        owner = owner | (((place >> bit) & 1) * mask)
    inside = jnp.arange(block_len, dtype=jnp.int32)
    key_index = ((owner ^ ctx_here)[:, None] * block_len + inside[None, :]).reshape(-1)
    query_index = ctx_here * block_len + inside
    segments = segment_all.transpose(1, 0, 2).reshape(seqs, -1)
    allowed = (segments[:, :, None] == segment_ids[:, None, :]) & (
        key_index[None, :, None] <= query_index[None, None, :]
    )
    return jnp.where(allowed, 0.0, mask_fill)


def contract(left, right, left_dim, right_dim):
    return lax.dot_general(
        left, right, (((left_dim,), (right_dim,)), ((), ())), preferred_element_type=wide
    )


def silu_parts(gate, up):
    sigmoid = jax.nn.sigmoid(gate)
    return sigmoid, (gate * sigmoid * up).astype(low)


def silu_back(hidden_grad, gate, up, sigmoid):
    gate_grad = (hidden_grad * up * sigmoid * (1.0 + gate * (1.0 - sigmoid))).astype(low)
    return gate_grad, (hidden_grad * gate * sigmoid).astype(low)


def body_blocked(
    tokens, segment_ids, positions, norm_attn, w_query, w_key, w_value, w_out,
    norm_ffn, w_gate, w_up, w_down, cotangent,
):
    seqs, block_len, _ = tokens.shape
    n_dev = lax.axis_size(AXES)
    me, ctx_here = lax.axis_index(AXES), lax.axis_index("ctx")
    rows = seqs * block_len
    score_scale = HEAD_DIM ** (-0.5)
    cut, cut_ff = D // n_dev, FF // n_dev
    pad = -(-cut // 16) * 16
    top_ff = (cut_ff * 3 // 5) // 8 * 8
    low_ff = cut_ff - top_ff
    half = n_dev // 2
    split = half * pad
    slots = Slots()
    ahead = (seqs + 1) // 2

    def rows_of(shard, columns):
        return jnp.pad(shard.reshape(cut, columns), ((0, pad - cut), (0, 0)))

    def weight(move):
        return move.both.reshape(-1, move.both.shape[-1])

    attn_block = jnp.concatenate(
        [rows_of(w_key, KV), rows_of(w_value, KV), rows_of(w_query, ATTN)], axis=1
    )[None]
    attn = Spread(attn_block, 8)
    slots.run([attn])
    mix_block = jnp.concatenate([w_down.reshape(cut_ff, D), rows_of(w_out, D)], axis=0)[None]
    mix = Spread(mix_block, 8)
    attn = Spread(attn.both, 16)
    seg_y = Move(slots.after(segment_ids), FIRST)
    inputs = slots.after(tokens).astype(wide).reshape(rows, D)
    slots.run([attn, mix], [seg_y])
    places = jnp.arange(n_dev, dtype=jnp.int32)
    order = block_owner(places) ^ me
    place = jnp.sum(jnp.where(order[:, None] == places[None, :], places[:, None], 0), axis=0)
    slot = jnp.arange(n_dev * pad, dtype=jnp.int32)
    source = jnp.where(slot % pad < cut, jnp.repeat(order, pad) * cut + slot % pad, -1)
    perm = (jnp.arange(D, dtype=jnp.int32)[:, None] == source[None, :]).astype(low)
    scale_attn = rms_scale(inputs)
    normed_attn = product((inputs * scale_attn * norm_attn).astype(low), perm).astype(low)
    segments = jnp.stack([segment_ids, seg_y.came])
    seg_c = Move(segments, CORE)
    pairs_w = SpreadFirst(attn.both[..., : 2 * KV], FIRST)
    query_w = Spread(attn.both[..., 2 * KV :], SECOND)
    angles = slots.after(positions).reshape(rows)
    mix = Spread(mix.both, 16)
    slots.run([pairs_w, query_w], [mix, seg_c])
    cosine, sine = rope_tables(angles)
    segments = jnp.concatenate([segments, seg_c.came], axis=0)
    bias = key_bias(slots.after(segments), segment_ids, ctx_here, (2, 1))
    slots.hold(normed_attn)
    pairs_w = SpreadBetween(pairs_w, SECOND)
    query_w = Spread(query_w.both, FIRST)
    pair_block = jnp.concatenate([rows_of(w_gate, FF), rows_of(w_up, FF)], axis=1)[None]
    pair = Spread(pair_block, 8)
    slots.run([pairs_w, query_w])
    slots.hold(cosine, sine)
    pairs_w, query_w = Spread(pairs_w.both, CORE), Spread(query_w.both, CORE)
    top_w, low_w = Spread(mix.both[:, :top_ff], SECOND), SpreadFirst(mix.both[:, top_ff:], FIRST)
    slots.run([pairs_w, query_w], [top_w, low_w, pair])
    query_weight, kv_weight = weight(query_w), weight(pairs_w)
    query_t, pairs_t = project(
        normed_attn,
        (query_w.value, query_w.came),
        (pairs_w.value, pairs_w.came),
        cosine,
        sine,
        score_scale,
    )
    gate_w = Spread(pair.both[..., :FF], 16)
    pairs_all = Spread(pairs_t[None], FIRST)
    slots.hold(query_t)
    top_w, low_w = Spread(top_w.both, FIRST), SpreadBetween(low_w, SECOND)
    slots.run([pairs_all], [gate_w, low_w, top_w])
    pairs_all = Spread(pairs_all.both, CORE)
    up_w = Spread(pair.both[..., FF:], 16)
    gate_w = Spread(gate_w.both, SECOND)
    slots.run([pairs_all], [gate_w, up_w])
    pairs_all = pairs_all.both
    mixed, logs = [None] * seqs, [None] * seqs
    for seq in range(ahead):
        mixed[seq], logs[seq] = attend(query_t, pairs_all, bias, seq)
    up_w = SpreadFirst(up_w.both, FIRST)
    top_core = Move(top_w.both, CORE)
    low_core = Move(low_w.both, CORE)
    slots.run([], [up_w, top_core, low_core])
    gate_w, up_w = Spread(gate_w.both, FIRST), SpreadBetween(up_w, SECOND)
    slots.run([], [gate_w, up_w])
    for seq in range(ahead, seqs):
        mixed[seq], logs[seq] = attend(query_t, pairs_all, bias, seq)
    down_weight, out_weight = join_blocks(
        (top_w.both, top_core.came), (low_w.both, low_core.came), order, low_ff
    )
    down_weight, out_weight = down_weight.reshape(FF, D), out_weight.reshape(-1, D)
    down_grad = cotangent.reshape(rows, D)
    hidden_grad = product_right(down_grad, down_weight)
    gate_w, up_w = Spread(gate_w.both, CORE), Spread(up_w.both, CORE)
    slots.run([gate_w, up_w])
    attended = jnp.concatenate([contract(m, perm, 0, 0).astype(low) for m in mixed], axis=0)
    resid = inputs + product(attended, out_weight)
    scale_ffn = rms_scale(resid)
    normed_ffn = product((resid * scale_ffn * norm_ffn).astype(low), perm).astype(low)
    gate_weight, up_weight = weight(gate_w), weight(up_w)
    gate, up = product(normed_ffn, gate_weight), product(normed_ffn, up_weight)
    sigmoid, hidden = silu_parts(gate, up)
    gate_grad, up_grad = silu_back(hidden_grad, gate, up, sigmoid)

    def halves(left, right, right_dim):
        both = []
        for piece in (left[:, :split], left[:, split:]):
            grad = contract(piece, right, 0, right_dim).astype(low)
            both.append(grad.reshape(half, pad, -1))
        return FoldPair(*both, CORE)

    def flat(grad):
        return grad[:cut].reshape(-1)

    def collect_wide(value):
        high = lax.reduce_precision(value, 8, 7)
        return product_right(high.astype(low), perm) + product_right(
            (value - high).astype(low), perm
        )

    gate_s, up_s = halves(normed_ffn, gate_grad, 0), halves(normed_ffn, up_grad, 0)
    slots.run([gate_s, up_s])
    top_grad, low_grad = down_grad_blocks(slots.after(hidden), down_grad, place, top_ff)
    gate_low, up_low = slots.after((gate_grad, up_grad))
    top_s = FoldPair(top_grad[:half], top_grad[half:], CORE)
    low_s = FoldPair(low_grad[:half], low_grad[half:], CORE)
    gate_s, up_s = Fold(gate_s.sum, FIRST), FoldBetween(up_s.sum, SECOND)
    slots.run([gate_s, up_s], [top_s, low_s])
    normed_grad = product_right(gate_low, gate_weight) + product_right(up_low, up_weight)
    normed_grad = collect_wide(normed_grad)
    grad_out = cotangent.astype(wide).reshape(rows, D)
    resid_grad, ffn_gain_grad = norm_back(resid, scale_ffn, norm_ffn, normed_grad)
    resid_grad = resid_grad + grad_out
    branch_grad = resid_grad.astype(low)
    grad_t = product_right(perm, product_right(branch_grad, out_weight).astype(low)).astype(low)
    grad_t = slots.after(grad_t)
    back = [None] * seqs
    for seq in range(ahead):
        back[seq] = attend_back(query_t, pairs_all, bias, mixed[seq], logs[seq], grad_t, seq)
    gate_s, up_s = Fold(gate_s.sum, SECOND), Fold(up_s.sum, FIRST)
    top_s, low_s = Fold(top_s.sum, FIRST), FoldBetween(low_s.sum, SECOND)
    slots.run([gate_s, up_s], [top_s, low_s])
    grad_t = slots.after(grad_t)
    for seq in range(ahead, seqs):
        back[seq] = attend_back(query_t, pairs_all, bias, mixed[seq], logs[seq], grad_t, seq)
    gate_s, up_s = Fold(gate_s.sum, 16), Fold(up_s.sum, 16)
    out_s = halves(slots.after(attended), branch_grad, 0)
    slots.run([], [gate_s, up_s])
    pairs_part = jnp.concatenate([b[1] for b in back], axis=2)
    pairs_s = FoldPair(pairs_part[:2], pairs_part[2:], CORE)
    top_s, low_s = Fold(top_s.sum, SECOND), Fold(low_s.sum, FIRST)
    slots.run([pairs_s], [top_s, low_s, out_s])
    query_low = jnp.concatenate([b[0] for b in back], axis=1)
    query_low = rotate_back(query_low * score_scale, cosine, sine).astype(low)
    query_s = halves(normed_attn, query_low, 1)
    pairs_s = Fold(pairs_s.sum, FIRST, last=True)
    out_s = FoldBetween(out_s.sum, SECOND)
    down_s = Fold(jnp.concatenate([top_s.sum, low_s.sum], axis=1), 16)
    slots.run([pairs_s, query_s], [out_s, down_s])
    gate_s, up_s = Fold(gate_s.sum, 8, last=True), Fold(up_s.sum, 8, last=True)
    pairs_grad = slots.after(pairs_s.sum)
    query_s, out_s = Fold(query_s.sum, FIRST), Fold(out_s.sum, FIRST)
    slots.run([], [query_s, out_s, gate_s, up_s])
    pairs_low = jnp.concatenate(
        [rotate_back(pairs_grad[:KV], cosine, sine).astype(low), pairs_grad[KV:].astype(low)],
        axis=0,
    )
    pairs_s = halves(normed_attn, pairs_low, 1)
    slots.run([pairs_s])
    query_s = Fold(query_s.sum, SECOND)
    pairs_s = FoldBetween(pairs_s.sum, SECOND)
    down_s = Fold(down_s.sum, 8, last=True)
    output = (resid + product(slots.after(hidden), down_weight)).astype(low)
    output = output.reshape(seqs, block_len, D)
    slots.run([pairs_s], [query_s, down_s])
    query_low, pairs_low = slots.after((query_low, pairs_low))
    attn_normed_grad = collect_wide(
        contract(query_low, query_weight, 0, 1) + contract(pairs_low, kv_weight, 0, 1)
    )
    input_grad, attn_gain_grad = norm_back(inputs, scale_attn, norm_attn, attn_normed_grad)
    d_tokens = (input_grad + resid_grad).reshape(seqs, block_len, D)
    attn_s = Fold(jnp.concatenate([query_s.sum, out_s.sum], axis=2), 16)
    pairs_s = Fold(pairs_s.sum, FIRST)
    gains = Move(jnp.stack([attn_gain_grad, ffn_gain_grad]), CORE)
    slots.run([pairs_s], [attn_s])
    attn_s = Fold(attn_s.sum, 8, last=True)
    pairs_s = Fold(pairs_s.sum, 16)
    slots.run([pairs_s], [gains])
    gains = gains.value + gains.came
    asked = [Move(gains, m) for m in (FIRST, SECOND, FIRST | SECOND)]
    slots.run([], [attn_s, *asked])
    gains = (gains + asked[0].came) + (asked[1].came + asked[2].came)
    pairs_s = Fold(pairs_s.sum, 8, last=True)
    asked = [Move(gains, m) for m in (8, 16, 24)]
    slots.run([], [pairs_s, *asked])
    gains = (gains + asked[0].came) + (asked[1].came + asked[2].came)
    return (
        output,
        d_tokens,
        gains[0],
        flat(attn_s.sum[:, :ATTN]),
        flat(pairs_s.sum[:, :KV]),
        flat(pairs_s.sum[:, KV:]),
        flat(attn_s.sum[:, ATTN:]),
        gains[1],
        flat(gate_s.sum),
        flat(up_s.sum),
        down_s.sum.reshape(-1),
    )


def body_whole(
    tokens, segment_ids, positions, norm_attn, w_query, w_key, w_value, w_out,
    norm_ffn, w_gate, w_up, w_down, cotangent,
):
    seqs, block_len, _ = tokens.shape
    n_dev = lax.axis_size(AXES)
    rows = seqs * block_len
    score_scale = HEAD_DIM ** (-0.5)

    def whole(shard, columns):
        return lax.all_gather(shard, AXES, axis=0, tiled=True).reshape(-1, columns)

    query_weight = whole(w_query, ATTN)
    kv_weight = jnp.concatenate([whole(w_key, KV), whole(w_value, KV)], axis=1)
    out_weight = whole(w_out, D)
    gate_weight, up_weight = whole(w_gate, FF), whole(w_up, FF)
    down_weight = whole(w_down, D)
    inputs = tokens.astype(wide).reshape(rows, D)
    grad_out = cotangent.astype(wide).reshape(rows, D)
    scale_attn = rms_scale(inputs)
    normed_attn = (inputs * scale_attn * norm_attn).astype(low)
    cosine, sine = rope_tables(positions.reshape(rows))
    bias = key_bias(ctx_gather(segment_ids), segment_ids, lax.axis_index("ctx"), ctx_masks())
    pairs_t = contract(kv_weight, normed_attn, 0, 1)
    pairs_t = jnp.concatenate(
        [rotate(pairs_t[:KV], cosine, sine).astype(low), pairs_t[KV:].astype(low)], axis=0
    )
    pairs_all = ctx_gather(pairs_t)
    query_t = contract(query_weight, normed_attn, 0, 1)
    query_t = (rotate(query_t, cosine, sine) * score_scale).astype(low)
    mixed, logs = zip(*[attend(query_t, pairs_all, bias, seq) for seq in range(seqs)])
    attended = jnp.concatenate([m.T for m in mixed], axis=0)
    resid = inputs + product(attended, out_weight)
    scale_ffn = rms_scale(resid)
    normed_ffn = (resid * scale_ffn * norm_ffn).astype(low)
    gate, up = product(normed_ffn, gate_weight), product(normed_ffn, up_weight)
    sigmoid, hidden = silu_parts(gate, up)
    output = (resid + product(hidden, down_weight)).astype(low).reshape(seqs, block_len, D)
    down_grad = cotangent.reshape(rows, D)
    gate_grad, up_grad = silu_back(product_right(down_grad, down_weight), gate, up, sigmoid)
    normed_grad = product_right(gate_grad, gate_weight) + product_right(up_grad, up_weight)
    resid_grad, ffn_gain_grad = norm_back(resid, scale_ffn, norm_ffn, normed_grad)
    resid_grad = resid_grad + grad_out
    branch_grad = resid_grad.astype(low)
    grad_t = product_right(branch_grad, out_weight).astype(low).T
    back = [
        attend_back(query_t, pairs_all, bias, mixed[seq], logs[seq], grad_t, seq)
        for seq in range(seqs)
    ]
    pairs_grad = ctx_scatter(jnp.concatenate([b[1] for b in back], axis=2))
    query_low = jnp.concatenate([b[0] for b in back], axis=1)
    query_low = rotate_back(query_low * score_scale, cosine, sine).astype(low)
    pairs_low = jnp.concatenate(
        [rotate_back(pairs_grad[:KV], cosine, sine).astype(low), pairs_grad[KV:].astype(low)],
        axis=0,
    )
    normed_grad = contract(query_low, query_weight, 0, 1) + contract(pairs_low, kv_weight, 0, 1)
    input_grad, attn_gain_grad = norm_back(inputs, scale_attn, norm_attn, normed_grad)
    d_tokens = (input_grad + resid_grad).reshape(seqs, block_len, D)

    def finish(left, right, right_dim):
        grad = contract(left, right, 0, right_dim).astype(low).reshape(n_dev, -1)
        grad = lax.psum_scatter(grad, AXES, scatter_dimension=0, tiled=True)
        return grad.astype(wide).reshape(-1)

    attn_gain_sum, ffn_gain_sum = lax.psum((attn_gain_grad, ffn_gain_grad), AXES)
    return (
        output,
        d_tokens,
        attn_gain_sum,
        finish(normed_attn, query_low, 1),
        finish(normed_attn, pairs_low[:KV], 1),
        finish(normed_attn, pairs_low[KV:], 1),
        finish(attended, branch_grad, 0),
        ffn_gain_sum,
        finish(normed_ffn, gate_grad, 0),
        finish(normed_ffn, up_grad, 0),
        finish(hidden, down_grad, 0),
    )


def solution(mesh):
    sizes = dict(mesh.shape)
    blocked = sizes["dp"] == 8 and sizes["ctx"] == 4
    body = body_blocked if blocked else body_whole
    one = P(AXES)
    tok = P("dp", "ctx", None)
    ids = P("dp", "ctx")
    in_specs = (tok, ids, ids, P(), one, one, one, one, P(), one, one, one, tok)
    out_specs = (tok, tok, P(), one, one, one, one, P(), one, one, one)
    return jax.shard_map(body, mesh=mesh, in_specs=in_specs, out_specs=out_specs, check_vma=False)
```

```python
import functools

import jax
import jax.numpy as jnp
from jax import lax
from jax.experimental import pallas as pl
from jax.experimental.pallas import tpu as pltpu
from jax.sharding import PartitionSpec as P

D = 960
HEADS = 15
KV_HEADS = 5
HEAD_DIM = 64
FF = 2560
GROUP = HEADS // KV_HEADS
ATTN = HEADS * HEAD_DIM
KV = KV_HEADS * HEAD_DIM
AXES = ("dp", "ctx")
CORE, FIRST, SECOND = 1, 2, 4

norm_eps = 1e-05
rope_base = 100000.0
mask_fill = -1000000000.0
low = jnp.bfloat16
wide = jnp.float32


def rms_scale(values):
    return lax.rsqrt(jnp.mean(values * values, axis=-1, keepdims=True) + norm_eps)


def norm_back(values, scale, gain, grad):
    gain_grad = jnp.sum(grad * values * scale, axis=0)
    weighted = grad * gain
    inner = jnp.mean(weighted * values, axis=-1, keepdims=True)
    return (scale * weighted - values * (scale * scale * scale) * inner, gain_grad)


def rope_tables(position):
    freqs = rope_base ** (-jnp.arange(0, HEAD_DIM, 2, dtype=wide) / HEAD_DIM)
    angles = freqs[:, None] * position.astype(wide)[None, :]
    angles = jnp.concatenate([angles, angles], axis=0)
    return jnp.cos(angles), jnp.sin(angles)


def by_head(values):
    return values.reshape(-1, HEAD_DIM, values.shape[-1])


def rotate(values, cosine, sine):
    values = by_head(values)
    half = HEAD_DIM // 2
    turned = jnp.concatenate([-values[:, half:], values[:, :half]], axis=1)
    return (values * cosine + turned * sine).reshape(-1, values.shape[-1])


def rotate_back(grad, cosine, sine):
    grad = by_head(grad)
    half = HEAD_DIM // 2
    scaled = grad * sine
    turned = jnp.concatenate([scaled[:, half:], -scaled[:, :half]], axis=1)
    return (grad * cosine + turned).reshape(-1, grad.shape[-1])


def product(left, right):
    return jnp.dot(left, right, preferred_element_type=wide)


def product_left(left, right):
    return lax.dot_general(left, right, (((0,), (0,)), ((), ())), preferred_element_type=wide)


def product_right(left, right):
    return lax.dot_general(left, right, (((1,), (1,)), ((), ())), preferred_element_type=wide)


def swap(value, mask):
    n = lax.axis_size(AXES)
    return lax.ppermute(value, AXES, [(i, i ^ mask) for i in range(n)])


def add_low(left, right):
    return (left.astype(wide) + right.astype(wide)).astype(low)


def far_masks():
    n = lax.axis_size(AXES)
    masks, m = [], 8
    while m < n:
        masks.append(m)
        m *= 2
    return masks


def block_owner(place):
    far = far_masks()
    owner = jnp.zeros_like(place)
    for bit, mask in enumerate(far + [SECOND, FIRST, CORE]):
        owner = owner | (((place >> bit) & 1) * mask)
    return owner


class Slots:
    def __init__(self):
        self.deps = ()

    def after(self, value):
        return lax.optimization_barrier((value, self.deps))[0]

    def hold(self, *values):
        self.deps = self.deps + values

    def run(self, moves, late=()):
        before, self.deps = self.deps, ()
        for i, move in enumerate((*moves, *late)):
            value = move.give()
            if before:
                value = lax.optimization_barrier((value, before))[0]
            came = swap(value, move.mask)
            if i < len(moves):
                self.deps += (came,)
            move.take(came)


class Move:
    def __init__(self, value, mask):
        self.value, self.mask = value, mask

    def give(self):
        return self.value

    def take(self, came):
        self.came = came


class Spread(Move):
    def take(self, came):
        self.came = came
        self.both = jnp.concatenate([self.value, came], axis=0)


class SpreadBetween(Spread):
    def __init__(self, first, mask):
        self.own, self.side = first.value, first.came
        super().__init__(first.both, mask)

    def take(self, came):
        n = came.shape[0] // 2
        self.both = jnp.concatenate([self.own, came[:n], self.side, came[n:]], axis=0)


class SpreadFirst(Spread):
    def take(self, came):
        self.came = came
        super().take(came)


class Fold(Move):
    def __init__(self, value, mask, last=False):
        self.n, self.last = value.shape[0] // 2, last
        super().__init__(value, mask)

    def give(self):
        return self.value[self.n :]

    def take(self, came):
        if self.last:
            self.sum = self.value[0].astype(wide) + came[0].astype(wide)
        else:
            self.sum = add_low(self.value[: self.n], came)


class FoldPair(Fold):
    def __init__(self, mine, theirs, mask):
        self.value, self.theirs, self.mask, self.last = mine, theirs, mask, False
        self.n = mine.shape[0]

    def give(self):
        return self.theirs


class FoldBetween(Fold):
    def give(self):
        q = self.n // 2
        return jnp.concatenate([self.value[q : self.n], self.value[self.n + q :]], axis=0)

    def take(self, came):
        q = self.n // 2
        kept = jnp.concatenate([self.value[:q], self.value[self.n : self.n + q]], axis=0)
        self.sum = add_low(kept, came)


def ctx_masks():
    m, masks = lax.axis_size("ctx") // 2, []
    while m >= 1:
        masks.append(m)
        m //= 2
    return masks


def ctx_gather(value):
    now = value[None]
    for mask in ctx_masks():
        now = jnp.concatenate([now, swap(now, mask)], axis=0)
    return now


def ctx_scatter(value):
    now = value
    for mask in ctx_masks()[::-1]:
        n = now.shape[0] // 2
        now = now[:n].astype(wide) + swap(now[n:], mask).astype(wide)
        if n > 1:
            now = now.astype(low)
    return now[0]


def whole_spec():
    return pl.BlockSpec(memory_space=pltpu.VMEM)


def join_blocks(tops, lows, order, low_rows):
    (a, b), (c, d) = tops, lows
    half, top, columns = a.shape
    rest = c.shape[1] - low_rows

    def kernel(order_ref, a_ref, b_ref, c_ref, d_ref, down_ref, out_ref):
        def step(p, _):
            near, far = order_ref[p], order_ref[p + half]
            down_ref[near, :top, :] = a_ref[p]
            down_ref[near, top:, :] = c_ref[p, :low_rows, :]
            down_ref[far, :top, :] = b_ref[p]
            down_ref[far, top:, :] = d_ref[p, :low_rows, :]
            out_ref[p] = c_ref[p, low_rows:, :]
            out_ref[p + half] = d_ref[p, low_rows:, :]
            return 0

        lax.fori_loop(0, half, step, 0)

    shape = (2 * half, top + low_rows, columns)
    return pl.pallas_call(
        kernel,
        out_shape=[
            jax.ShapeDtypeStruct(shape, a.dtype),
            jax.ShapeDtypeStruct((2 * half, rest, columns), a.dtype),
        ],
        in_specs=[pl.BlockSpec(memory_space=pltpu.SMEM)] + [whole_spec()] * 4,
        out_specs=[whole_spec()] * 2,
        compiler_params=pltpu.CompilerParams(vmem_limit_bytes=32 * 2**20),
        cost_estimate=pl.CostEstimate(flops=0, bytes_accessed=2**20, transcendentals=0),
        name="join_blocks",
    )(order, a, b, c, d)


def down_grad_blocks(hidden, grad, place, top):
    rows, hidden_width = hidden.shape
    columns = grad.shape[1]
    total = place.shape[0]
    tall = hidden_width // total
    group = 8

    def kernel(place_ref, h_ref, g_ref, a_ref, b_ref):
        value = product_left(h_ref[...], g_ref[...]).astype(low)
        first = pl.program_id(0) * group
        for b in range(group):
            to = place_ref[first + b]
            a_ref[to] = value[b * tall : b * tall + top]
            b_ref[to] = value[b * tall + top : (b + 1) * tall]

    return pl.pallas_call(
        kernel,
        grid=(total // group,),
        in_specs=[
            pl.BlockSpec(memory_space=pltpu.SMEM),
            pl.BlockSpec((rows, group * tall), lambda i: (0, i)),
            pl.BlockSpec((rows, columns), lambda i: (0, 0)),
        ],
        out_specs=[
            pl.BlockSpec((total, top, columns), lambda i: (0, 0, 0)),
            pl.BlockSpec((total, tall - top, columns), lambda i: (0, 0, 0)),
        ],
        out_shape=[
            jax.ShapeDtypeStruct((total, top, columns), low),
            jax.ShapeDtypeStruct((total, tall - top, columns), low),
        ],
        compiler_params=pltpu.CompilerParams(vmem_limit_bytes=32 * 2**20),
        cost_estimate=pl.CostEstimate(
            flops=2 * rows * hidden_width * columns,
            bytes_accessed=2 * (rows * (hidden_width + columns) + hidden_width * columns),
            transcendentals=0,
        ),
        name="down_grad_blocks",
    )(place, hidden, grad)


def head_rows(ref, head):
    return ref[head * HEAD_DIM : (head + 1) * HEAD_DIM, :]


def key_blocks(kv_ref, start):
    blocks = [kv_ref[b, start : start + HEAD_DIM, :] for b in range(kv_ref.shape[0])]
    return jnp.concatenate(blocks, axis=1)


def turn(value):
    return value.astype(wide).T.astype(low)


def attend_kernel(q_ref, kv_ref, bias_ref, o_ref, lse_ref):
    for g in range(KV_HEADS):
        keys = turn(key_blocks(kv_ref, g * HEAD_DIM))
        values_t = key_blocks(kv_ref, KV + g * HEAD_DIM)
        for h in range(g * GROUP, (g + 1) * GROUP):
            scores = product(keys, head_rows(q_ref, h)) + bias_ref[0]
            top = jnp.max(scores, axis=0, keepdims=True)
            weight = jnp.exp(scores - top)
            total = jnp.sum(weight, axis=0, keepdims=True)
            mixed = product(values_t, weight.astype(low)) / total
            o_ref[h * HEAD_DIM : (h + 1) * HEAD_DIM, :] = mixed.astype(low)
            lse_ref[0, h : h + 1, :] = top + jnp.log(total)


def attend_back_kernel(q_ref, kv_ref, bias_ref, o_ref, lse_ref, do_ref, dq_ref, dkv_ref):
    width = q_ref.shape[1]
    for g in range(KV_HEADS):
        keys_t = key_blocks(kv_ref, g * HEAD_DIM)
        keys = turn(keys_t)
        values = turn(key_blocks(kv_ref, KV + g * HEAD_DIM))
        key_grad, value_grad = None, None
        for h in range(g * GROUP, (g + 1) * GROUP):
            query, grad = head_rows(q_ref, h), head_rows(do_ref, h)
            scores = product(keys, query) + bias_ref[0]
            probs = jnp.exp(scores - lse_ref[0, h : h + 1, :])
            inner = jnp.sum(
                grad.astype(wide) * head_rows(o_ref, h).astype(wide), axis=0, keepdims=True
            )
            scores_grad = (probs * (product(values, grad) - inner)).astype(low)
            dq_ref[h * HEAD_DIM : (h + 1) * HEAD_DIM, :] = product(keys_t, scores_grad)
            from_keys = product_right(scores_grad, query)
            from_values = product_right(probs.astype(low), grad)
            key_grad = from_keys if key_grad is None else key_grad + from_keys
            value_grad = from_values if value_grad is None else value_grad + from_values
        for start, value in ((g * HEAD_DIM, key_grad), (KV + g * HEAD_DIM, value_grad)):
            turned = value.T.astype(low)
            for b in range(kv_ref.shape[0]):
                dkv_ref[b, start : start + HEAD_DIM, :] = turned[:, b * width : (b + 1) * width]


def attention_specs(blocks, block_len, length, seq):
    columns = pl.BlockSpec((ATTN, block_len), lambda i: (0, seq))
    pairs = pl.BlockSpec((blocks, 2 * KV, block_len), lambda i: (0, 0, seq))
    bias = pl.BlockSpec((1, length, block_len), lambda i: (seq, 0, 0))
    own = pl.BlockSpec((ATTN, block_len), lambda i: (0, 0))
    own_pairs = pl.BlockSpec((blocks, 2 * KV, block_len), lambda i: (0, 0, 0))
    logs = pl.BlockSpec((1, HEADS, block_len), lambda i: (0, 0, 0))
    return columns, pairs, bias, own, own_pairs, logs


def attend(query_t, pairs_t, bias, seq):
    _, length, block_len = bias.shape
    columns, pairs, bias_spec, own, _, logs = attention_specs(
        pairs_t.shape[0], block_len, length, seq
    )
    work = HEADS * length * block_len
    return pl.pallas_call(
        attend_kernel,
        grid=(1,),
        in_specs=[columns, pairs, bias_spec],
        out_specs=[own, logs],
        out_shape=[
            jax.ShapeDtypeStruct((ATTN, block_len), low),
            jax.ShapeDtypeStruct((1, HEADS, block_len), wide),
        ],
        compiler_params=pltpu.CompilerParams(vmem_limit_bytes=40 * 2**20),
        cost_estimate=pl.CostEstimate(
            flops=work, bytes_accessed=2**20, transcendentals=0
        ),
        name="attend",
    )(query_t, pairs_t, bias)


def attend_back(query_t, pairs_t, bias, mixed_t, logs_all, grad_t, seq):
    _, length, block_len = bias.shape
    columns, pairs, bias_spec, own, own_pairs, logs = attention_specs(
        pairs_t.shape[0], block_len, length, seq
    )
    work = HEADS * length * block_len
    return pl.pallas_call(
        attend_back_kernel,
        grid=(1,),
        in_specs=[columns, pairs, bias_spec, own, logs, columns],
        out_specs=[own, own_pairs],
        out_shape=[
            jax.ShapeDtypeStruct((ATTN, block_len), wide),
            jax.ShapeDtypeStruct((pairs_t.shape[0], 2 * KV, block_len), low),
        ],
        compiler_params=pltpu.CompilerParams(vmem_limit_bytes=48 * 2**20),
        cost_estimate=pl.CostEstimate(
            flops=work, bytes_accessed=2**20, transcendentals=0
        ),
        name="attend_back",
    )(query_t, pairs_t, bias, mixed_t, logs_all, grad_t)


def project_kernel(a_ref, q0_ref, q1_ref, p0_ref, p1_ref, cos_ref, sin_ref, q_ref, p_ref, *, scale):
    split = q0_ref.shape[0]
    half = HEAD_DIM // 2
    first, second = a_ref[:, :split], a_ref[:, split:]
    cosine, sine = cos_ref[...], sin_ref[...]

    def turned(value):
        upper, lower = value[half:], value[:half]
        return value * cosine + jnp.concatenate([-upper, lower], axis=0) * sine

    pairs = (product(first, p0_ref[...]) + product(second, p1_ref[...])).T
    for h in range(KV_HEADS):
        at = slice(h * HEAD_DIM, (h + 1) * HEAD_DIM)
        p_ref[at, :] = turned(pairs[at]).astype(low)
    p_ref[KV:, :] = pairs[KV:].astype(low)
    query = (product(first, q0_ref[...]) + product(second, q1_ref[...])).T
    for h in range(HEADS):
        at = slice(h * HEAD_DIM, (h + 1) * HEAD_DIM)
        q_ref[at, :] = (turned(query[at]) * scale).astype(low)


def project(normed, query_halves, pairs_halves, cosine, sine, scale):
    rows = normed.shape[0]
    halves = [h.reshape(-1, h.shape[-1]) for h in (*query_halves, *pairs_halves)]
    return pl.pallas_call(
        functools.partial(project_kernel, scale=scale),
        in_specs=[whole_spec()] * 7,
        out_specs=[whole_spec()] * 2,
        out_shape=[
            jax.ShapeDtypeStruct((ATTN, rows), low),
            jax.ShapeDtypeStruct((2 * KV, rows), low),
        ],
        compiler_params=pltpu.CompilerParams(vmem_limit_bytes=40 * 2**20),
        cost_estimate=pl.CostEstimate(flops=rows, bytes_accessed=2**20, transcendentals=0),
        name="project",
    )(normed, *halves, cosine, sine)


def key_bias(segment_all, segment_ids, ctx_here, masks):
    blocks, seqs, block_len = segment_all.shape
    place = jnp.arange(blocks, dtype=jnp.int32)
    owner = jnp.zeros_like(place)
    for bit, mask in enumerate(masks):
        owner = owner | (((place >> bit) & 1) * mask)
    inside = jnp.arange(block_len, dtype=jnp.int32)
    key_index = ((owner ^ ctx_here)[:, None] * block_len + inside[None, :]).reshape(-1)
    query_index = ctx_here * block_len + inside
    segments = segment_all.transpose(1, 0, 2).reshape(seqs, -1)
    allowed = (segments[:, :, None] == segment_ids[:, None, :]) & (
        key_index[None, :, None] <= query_index[None, None, :]
    )
    return jnp.where(allowed, 0.0, mask_fill)


def contract(left, right, left_dim, right_dim):
    return lax.dot_general(
        left, right, (((left_dim,), (right_dim,)), ((), ())), preferred_element_type=wide
    )


def silu_parts(gate, up):
    sigmoid = jax.nn.sigmoid(gate)
    return sigmoid, (gate * sigmoid * up).astype(low)


def silu_back(hidden_grad, gate, up, sigmoid):
    gate_grad = (hidden_grad * up * sigmoid * (1.0 + gate * (1.0 - sigmoid))).astype(low)
    return gate_grad, (hidden_grad * gate * sigmoid).astype(low)


def body_blocked(
    tokens, segment_ids, positions, norm_attn, w_query, w_key, w_value, w_out,
    norm_ffn, w_gate, w_up, w_down, cotangent,
):
    seqs, block_len, _ = tokens.shape
    n_dev = lax.axis_size(AXES)
    me, ctx_here = lax.axis_index(AXES), lax.axis_index("ctx")
    rows = seqs * block_len
    score_scale = HEAD_DIM ** (-0.5)
    cut, cut_ff = D // n_dev, FF // n_dev
    pad = -(-cut // 16) * 16
    top_ff = (cut_ff * 3 // 5) // 8 * 8
    low_ff = cut_ff - top_ff
    half = n_dev // 2
    split = half * pad
    slots = Slots()
    ahead = (seqs + 1) // 2

    def rows_of(shard, columns):
        return jnp.pad(shard.reshape(cut, columns), ((0, pad - cut), (0, 0)))

    def weight(move):
        return move.both.reshape(-1, move.both.shape[-1])

    attn_block = jnp.concatenate(
        [rows_of(w_key, KV), rows_of(w_value, KV), rows_of(w_query, ATTN)], axis=1
    )[None]
    attn = Spread(attn_block, 8)
    slots.run([attn])
    me, w_down, w_out = slots.after((me, w_down, w_out))
    mix_block = jnp.concatenate([w_down.reshape(cut_ff, D), rows_of(w_out, D)], axis=0)[None]
    mix = Spread(mix_block, 8)
    attn = Spread(attn.both, 16)
    seg_y = Move(slots.after(segment_ids), FIRST)
    inputs = slots.after(tokens).astype(wide).reshape(rows, D)
    slots.run([attn, mix], [seg_y])
    places = jnp.arange(n_dev, dtype=jnp.int32)
    order = block_owner(places) ^ me
    place = jnp.sum(jnp.where(order[:, None] == places[None, :], places[:, None], 0), axis=0)
    slot = jnp.arange(n_dev * pad, dtype=jnp.int32)
    source = jnp.where(slot % pad < cut, jnp.repeat(order, pad) * cut + slot % pad, -1)
    perm = (jnp.arange(D, dtype=jnp.int32)[:, None] == source[None, :]).astype(low)
    scale_attn = rms_scale(inputs)
    normed_attn = product((inputs * scale_attn * norm_attn).astype(low), perm).astype(low)
    segments = jnp.stack([segment_ids, seg_y.came])
    seg_c = Move(segments, CORE)
    pairs_w = SpreadFirst(attn.both[..., : 2 * KV], FIRST)
    query_w = Spread(attn.both[..., 2 * KV :], SECOND)
    angles = slots.after(positions).reshape(rows)
    mix = Spread(mix.both, 16)
    slots.run([pairs_w, query_w], [mix, seg_c])
    cosine, sine = rope_tables(angles)
    segments = jnp.concatenate([segments, seg_c.came], axis=0)
    bias = key_bias(slots.after(segments), segment_ids, ctx_here, (2, 1))
    slots.hold(normed_attn)
    pairs_w = SpreadBetween(pairs_w, SECOND)
    query_w = Spread(query_w.both, FIRST)
    w_gate, w_up = slots.after((w_gate, w_up))
    pair_block = jnp.concatenate([rows_of(w_gate, FF), rows_of(w_up, FF)], axis=1)[None]
    pair = Spread(pair_block, 8)
    slots.run([pairs_w, query_w])
    slots.hold(cosine, sine)
    pairs_w, query_w = Spread(pairs_w.both, CORE), Spread(query_w.both, CORE)
    top_w, low_w = Spread(mix.both[:, :top_ff], SECOND), SpreadFirst(mix.both[:, top_ff:], FIRST)
    slots.run([pairs_w, query_w], [top_w, low_w, pair])
    query_weight, kv_weight = weight(query_w), weight(pairs_w)
    query_t, pairs_t = project(
        normed_attn,
        (query_w.value, query_w.came),
        (pairs_w.value, pairs_w.came),
        cosine,
        sine,
        score_scale,
    )
    gate_w = Spread(pair.both[..., :FF], 16)
    pairs_all = Spread(pairs_t[None], FIRST)
    slots.hold(query_t)
    top_w, low_w = Spread(top_w.both, FIRST), SpreadBetween(low_w, SECOND)
    slots.run([pairs_all], [gate_w, low_w, top_w])
    pairs_all = Spread(pairs_all.both, CORE)
    up_w = Spread(pair.both[..., FF:], 16)
    gate_w = Spread(gate_w.both, SECOND)
    slots.run([pairs_all], [gate_w, up_w])
    pairs_all = pairs_all.both
    mixed, logs = [None] * seqs, [None] * seqs
    for seq in range(ahead):
        mixed[seq], logs[seq] = attend(query_t, pairs_all, bias, seq)
    up_w = SpreadFirst(up_w.both, FIRST)
    top_core = Move(top_w.both, CORE)
    low_core = Move(low_w.both, CORE)
    slots.run([], [up_w, top_core, low_core])
    gate_w, up_w = Spread(gate_w.both, FIRST), SpreadBetween(up_w, SECOND)
    slots.run([], [gate_w, up_w])
    for seq in range(ahead, seqs):
        mixed[seq], logs[seq] = attend(query_t, pairs_all, bias, seq)
    down_weight, out_weight = join_blocks(
        (top_w.both, top_core.came), (low_w.both, low_core.came), order, low_ff
    )
    down_weight, out_weight = down_weight.reshape(FF, D), out_weight.reshape(-1, D)
    down_grad = cotangent.reshape(rows, D)
    hidden_grad = product_right(down_grad, down_weight)
    gate_w, up_w = Spread(gate_w.both, CORE), Spread(up_w.both, CORE)
    slots.run([gate_w, up_w])
    attended = jnp.concatenate([contract(m, perm, 0, 0).astype(low) for m in mixed], axis=0)
    resid = inputs + product(attended, out_weight)
    scale_ffn = rms_scale(resid)
    normed_ffn = product((resid * scale_ffn * norm_ffn).astype(low), perm).astype(low)
    gate_weight, up_weight = weight(gate_w), weight(up_w)
    gate, up = product(normed_ffn, gate_weight), product(normed_ffn, up_weight)
    sigmoid, hidden = silu_parts(gate, up)
    gate_grad, up_grad = silu_back(hidden_grad, gate, up, sigmoid)

    def halves(left, right, right_dim):
        both = []
        for piece in (left[:, :split], left[:, split:]):
            grad = contract(piece, right, 0, right_dim).astype(low)
            both.append(grad.reshape(half, pad, -1))
        return FoldPair(*both, CORE)

    def flat(grad):
        return grad[:cut].reshape(-1)

    def collect_wide(value):
        high = lax.reduce_precision(value, 8, 7)
        return product_right(high.astype(low), perm) + product_right(
            (value - high).astype(low), perm
        )

    gate_s, up_s = halves(normed_ffn, gate_grad, 0), halves(normed_ffn, up_grad, 0)
    slots.run([gate_s, up_s])
    top_grad, low_grad = down_grad_blocks(slots.after(hidden), down_grad, place, top_ff)
    gate_low, up_low = slots.after((gate_grad, up_grad))
    top_s = FoldPair(top_grad[:half], top_grad[half:], CORE)
    low_s = FoldPair(low_grad[:half], low_grad[half:], CORE)
    gate_s, up_s = Fold(gate_s.sum, FIRST), FoldBetween(up_s.sum, SECOND)
    slots.run([gate_s, up_s], [top_s, low_s])
    normed_grad = product_right(gate_low, gate_weight) + product_right(up_low, up_weight)
    normed_grad = collect_wide(normed_grad)
    grad_out = cotangent.astype(wide).reshape(rows, D)
    resid_grad, ffn_gain_grad = norm_back(resid, scale_ffn, norm_ffn, normed_grad)
    resid_grad = resid_grad + grad_out
    branch_grad = resid_grad.astype(low)
    grad_t = product_right(perm, product_right(branch_grad, out_weight).astype(low)).astype(low)
    grad_t = slots.after(grad_t)
    back = [None] * seqs
    for seq in range(ahead):
        back[seq] = attend_back(query_t, pairs_all, bias, mixed[seq], logs[seq], grad_t, seq)
    gate_s, up_s = Fold(gate_s.sum, SECOND), Fold(up_s.sum, FIRST)
    top_s, low_s = Fold(top_s.sum, FIRST), FoldBetween(low_s.sum, SECOND)
    slots.run([gate_s, up_s], [top_s, low_s])
    grad_t = slots.after(grad_t)
    for seq in range(ahead, seqs):
        back[seq] = attend_back(query_t, pairs_all, bias, mixed[seq], logs[seq], grad_t, seq)
    gate_s, up_s = Fold(gate_s.sum, 16), Fold(up_s.sum, 16)
    out_s = halves(slots.after(attended), branch_grad, 0)
    slots.run([], [gate_s, up_s])
    pairs_part = jnp.concatenate([b[1] for b in back], axis=2)
    pairs_s = FoldPair(pairs_part[:2], pairs_part[2:], CORE)
    top_s, low_s = Fold(top_s.sum, SECOND), Fold(low_s.sum, FIRST)
    slots.run([pairs_s], [top_s, low_s, out_s])
    query_low = jnp.concatenate([b[0] for b in back], axis=1)
    query_low = rotate_back(query_low * score_scale, cosine, sine).astype(low)
    query_s = halves(normed_attn, query_low, 1)
    pairs_s = Fold(pairs_s.sum, FIRST, last=True)
    out_s = FoldBetween(out_s.sum, SECOND)
    down_s = Fold(jnp.concatenate([top_s.sum, low_s.sum], axis=1), 16)
    output = (resid + product(slots.after(hidden), down_weight)).astype(low)
    slots.run([pairs_s, query_s], [out_s, down_s])
    slots.hold(output)
    output = output.reshape(seqs, block_len, D)
    gate_s, up_s = Fold(gate_s.sum, 8, last=True), Fold(up_s.sum, 8, last=True)
    pairs_grad = slots.after(pairs_s.sum)
    query_s, out_s = Fold(query_s.sum, FIRST), Fold(out_s.sum, FIRST)
    slots.run([], [query_s, out_s, gate_s, up_s])
    pairs_low = jnp.concatenate(
        [rotate_back(pairs_grad[:KV], cosine, sine).astype(low), pairs_grad[KV:].astype(low)],
        axis=0,
    )
    pairs_s = halves(normed_attn, pairs_low, 1)
    slots.run([pairs_s])
    query_s = Fold(query_s.sum, SECOND)
    pairs_s = FoldBetween(pairs_s.sum, SECOND)
    down_s = Fold(down_s.sum, 8, last=True)
    slots.run([pairs_s], [query_s, down_s])
    query_low, pairs_low = slots.after((query_low, pairs_low))
    attn_normed_grad = collect_wide(
        contract(query_low, query_weight, 0, 1) + contract(pairs_low, kv_weight, 0, 1)
    )
    input_grad, attn_gain_grad = norm_back(inputs, scale_attn, norm_attn, attn_normed_grad)
    d_tokens = (input_grad + resid_grad).reshape(seqs, block_len, D)
    attn_s = Fold(jnp.concatenate([query_s.sum, out_s.sum], axis=2), 16)
    pairs_s = Fold(pairs_s.sum, FIRST)
    gains = Move(jnp.stack([attn_gain_grad, ffn_gain_grad]), CORE)
    slots.run([pairs_s, attn_s])
    attn_s = Fold(attn_s.sum, 8, last=True)
    pairs_s = Fold(pairs_s.sum, 16)
    slots.run([pairs_s], [gains])
    gains = gains.value + gains.came
    asked = [Move(gains, m) for m in (FIRST, SECOND, FIRST | SECOND)]
    slots.run([], [attn_s, *asked])
    gains = (gains + asked[0].came) + (asked[1].came + asked[2].came)
    pairs_s = Fold(pairs_s.sum, 8, last=True)
    asked = [Move(gains, m) for m in (8, 16, 24)]
    slots.run([], [pairs_s, *asked])
    gains = (gains + asked[0].came) + (asked[1].came + asked[2].came)
    return (
        output,
        d_tokens,
        gains[0],
        flat(attn_s.sum[:, :ATTN]),
        flat(pairs_s.sum[:, :KV]),
        flat(pairs_s.sum[:, KV:]),
        flat(attn_s.sum[:, ATTN:]),
        gains[1],
        flat(gate_s.sum),
        flat(up_s.sum),
        down_s.sum.reshape(-1),
    )


def body_whole(
    tokens, segment_ids, positions, norm_attn, w_query, w_key, w_value, w_out,
    norm_ffn, w_gate, w_up, w_down, cotangent,
):
    seqs, block_len, _ = tokens.shape
    n_dev = lax.axis_size(AXES)
    rows = seqs * block_len
    score_scale = HEAD_DIM ** (-0.5)

    def whole(shard, columns):
        return lax.all_gather(shard, AXES, axis=0, tiled=True).reshape(-1, columns)

    query_weight = whole(w_query, ATTN)
    kv_weight = jnp.concatenate([whole(w_key, KV), whole(w_value, KV)], axis=1)
    out_weight = whole(w_out, D)
    gate_weight, up_weight = whole(w_gate, FF), whole(w_up, FF)
    down_weight = whole(w_down, D)
    inputs = tokens.astype(wide).reshape(rows, D)
    grad_out = cotangent.astype(wide).reshape(rows, D)
    scale_attn = rms_scale(inputs)
    normed_attn = (inputs * scale_attn * norm_attn).astype(low)
    cosine, sine = rope_tables(positions.reshape(rows))
    bias = key_bias(ctx_gather(segment_ids), segment_ids, lax.axis_index("ctx"), ctx_masks())
    pairs_t = contract(kv_weight, normed_attn, 0, 1)
    pairs_t = jnp.concatenate(
        [rotate(pairs_t[:KV], cosine, sine).astype(low), pairs_t[KV:].astype(low)], axis=0
    )
    pairs_all = ctx_gather(pairs_t)
    query_t = contract(query_weight, normed_attn, 0, 1)
    query_t = (rotate(query_t, cosine, sine) * score_scale).astype(low)
    mixed, logs = zip(*[attend(query_t, pairs_all, bias, seq) for seq in range(seqs)])
    attended = jnp.concatenate([m.T for m in mixed], axis=0)
    resid = inputs + product(attended, out_weight)
    scale_ffn = rms_scale(resid)
    normed_ffn = (resid * scale_ffn * norm_ffn).astype(low)
    gate, up = product(normed_ffn, gate_weight), product(normed_ffn, up_weight)
    sigmoid, hidden = silu_parts(gate, up)
    output = (resid + product(hidden, down_weight)).astype(low).reshape(seqs, block_len, D)
    down_grad = cotangent.reshape(rows, D)
    gate_grad, up_grad = silu_back(product_right(down_grad, down_weight), gate, up, sigmoid)
    normed_grad = product_right(gate_grad, gate_weight) + product_right(up_grad, up_weight)
    resid_grad, ffn_gain_grad = norm_back(resid, scale_ffn, norm_ffn, normed_grad)
    resid_grad = resid_grad + grad_out
    branch_grad = resid_grad.astype(low)
    grad_t = product_right(branch_grad, out_weight).astype(low).T
    back = [
        attend_back(query_t, pairs_all, bias, mixed[seq], logs[seq], grad_t, seq)
        for seq in range(seqs)
    ]
    pairs_grad = ctx_scatter(jnp.concatenate([b[1] for b in back], axis=2))
    query_low = jnp.concatenate([b[0] for b in back], axis=1)
    query_low = rotate_back(query_low * score_scale, cosine, sine).astype(low)
    pairs_low = jnp.concatenate(
        [rotate_back(pairs_grad[:KV], cosine, sine).astype(low), pairs_grad[KV:].astype(low)],
        axis=0,
    )
    normed_grad = contract(query_low, query_weight, 0, 1) + contract(pairs_low, kv_weight, 0, 1)
    input_grad, attn_gain_grad = norm_back(inputs, scale_attn, norm_attn, normed_grad)
    d_tokens = (input_grad + resid_grad).reshape(seqs, block_len, D)

    def finish(left, right, right_dim):
        grad = contract(left, right, 0, right_dim).astype(low).reshape(n_dev, -1)
        grad = lax.psum_scatter(grad, AXES, scatter_dimension=0, tiled=True)
        return grad.astype(wide).reshape(-1)

    attn_gain_sum, ffn_gain_sum = lax.psum((attn_gain_grad, ffn_gain_grad), AXES)
    return (
        output,
        d_tokens,
        attn_gain_sum,
        finish(normed_attn, query_low, 1),
        finish(normed_attn, pairs_low[:KV], 1),
        finish(normed_attn, pairs_low[KV:], 1),
        finish(attended, branch_grad, 0),
        ffn_gain_sum,
        finish(normed_ffn, gate_grad, 0),
        finish(normed_ffn, up_grad, 0),
        finish(hidden, down_grad, 0),
    )


def solution(mesh):
    sizes = dict(mesh.shape)
    blocked = sizes["dp"] == 8 and sizes["ctx"] == 4
    body = body_blocked if blocked else body_whole
    one = P(AXES)
    tok = P("dp", "ctx", None)
    ids = P("dp", "ctx")
    in_specs = (tok, ids, ids, P(), one, one, one, one, P(), one, one, one, tok)
    out_specs = (tok, tok, P(), one, one, one, one, P(), one, one, one)
    return jax.shard_map(body, mesh=mesh, in_specs=in_specs, out_specs=out_specs, check_vma=False)
```
